256 devices in a mesh: row: 4 (over y_lo, core), col: 64 (over y_hi, z, x).
Axes of the slice: x: 4, y: 4 (y_hi: 2, y_lo: 2; y = y_hi * 2 + y_lo), z: 8, core: 2. Of those that a mesh axis runs over, the one named last changes fastest.
Arguments:
- matrix: float32 [8192, 32768], P('row', 'col')
- pivots: int32 [256], replicated, may hold values from 0 to 8191, as said below
- l_inverse: float32 [256, 256], replicated, as said below
Outputs:
- updated: float32 [8192, 32768], P('row', 'col')
- u_block: float32 [256, 32768], P(None, 'col')
- moved: float32 [1024, 32768], P('row', 'col')
The draws below stay inside these ranges and needn't reach their ends.
Inputs may be any that keep to these rules, and one draw needn't show every extreme that they name: Each pivots[i] is either i or a global row number of 256 or more; pivots[0] is 0; all entries are distinct. `l_inverse`: unit lower triangular.
All inputs are finite; a program needn't handle non-finite values.
Results may differ from the reference program's by a relative error of at most 0.00058.
Values may be sent and summed in bfloat16 or wider, within the bound.
A program may use at most 64 MiB of HBM per device.

```python
import jax
import jax.numpy as jnp
from jax import lax

NB = 256
ROWS_DEV = 2048
COLS_DEV = 512
M = 8192
N = 32768
N_ROW = 4
N_COL = 64


def draw_matrix(key, part):
    first = jax.random.fold_in(key, 0)
    values = jax.random.normal(first, (M, N), jnp.float32)
    column = jnp.arange(N)
    panel = (column < NB).astype(jnp.float32)
    factor = panel * (0.03 * NB ** (-0.5)) + (1.0 - panel)
    return (values * factor[None, :]).astype(jnp.float32)


def draw_l_inverse(key, part):
    values = jax.random.normal(key, (NB, NB), jnp.float32)
    row_ids = jnp.arange(NB)[:, None]
    col_ids = jnp.arange(NB)[None, :]
    lower = (row_ids > col_ids).astype(jnp.float32)
    unit = (row_ids == col_ids).astype(jnp.float32)
    return (values * lower * NB ** (-0.5) + unit).astype(jnp.float32)


def draw_pivots(key, part):
    first, second, third = jax.random.split(key, 3)
    chosen = jax.random.permutation(first, M - NB - 1)[:NB - 2] + NB
    chosen = jnp.concatenate([chosen, jnp.array([M - 1])]).astype(jnp.int32)
    order = jax.random.permutation(second, NB - 1)
    chosen = chosen[order]
    keep = jax.random.randint(third, (NB - 1,), 0, 4) > 0
    keep = keep | (chosen == M - 1)
    rest = jnp.where(keep, chosen, jnp.arange(1, NB)).astype(jnp.int32)
    return jnp.concatenate([jnp.zeros((1,), jnp.int32), rest]).astype(jnp.int32)


def setup_inputs(seed: int = 0) -> dict:
    splits = jax.random.split(jax.random.key(seed), 4)
    matrix = draw_matrix(jax.random.fold_in(splits[3], 71), 0)
    pivots = draw_pivots(jax.random.fold_in(splits[3], 71), 0)
    l_inverse = draw_l_inverse(jax.random.fold_in(splits[3], 71), 0)
    return {"matrix": matrix, "pivots": pivots, "l_inverse": l_inverse}


def stored_rows(glob):
    block = glob // NB
    owner = block % N_ROW
    local = (block // N_ROW) * NB + glob % NB
    return (owner * ROWS_DEV + local).astype(jnp.int32)


def reference(matrix, pivots, l_inverse):
    rows = stored_rows(pivots)
    l_panel = matrix[:, :NB].astype(jnp.bfloat16)
    slabs = jnp.transpose(matrix.reshape(M, N_COL, COLS_DEV), (1, 0, 2))

    def one_slab(args):
        slab, index = args
        top = slab[:NB]
        picked = slab[rows]
        swapped = slab.at[rows].set(top).at[:NB].set(picked)
        u_rows = jnp.dot(l_inverse, picked, precision=lax.Precision.HIGHEST, preferred_element_type=jnp.float32)
        update = jnp.dot(l_panel, u_rows.astype(jnp.bfloat16), preferred_element_type=jnp.float32)
        result = (swapped - update).at[:NB].set(u_rows)
        column = jnp.arange(COLS_DEV)
        is_panel = (index == 0) & (column < NB)
        return jnp.where(is_panel[None, :], slab, result), u_rows

    done, u_parts = lax.map(one_slab, (slabs, jnp.arange(N_COL).astype(jnp.int32)))
    updated = jnp.transpose(done, (1, 0, 2)).reshape(M, N)
    u_block = jnp.transpose(u_parts, (1, 0, 2)).reshape(NB, N)
    owners = (pivots // NB) % N_ROW
    high = pivots >= NB
    taken = updated[rows]
    blocks = []
    for grid_row in range(N_ROW):
        chosen = (owners == grid_row) & high
        blocks.append(jnp.where(chosen[:, None], taken, jnp.zeros_like(taken)))
    moved = jnp.concatenate(blocks, 0)
    return updated, u_block, moved
```

```python
import functools

import jax
import jax.numpy as jnp
from jax import lax
from jax.experimental import pallas as pl
from jax.experimental.pallas import tpu as pltpu
from jax.sharding import PartitionSpec as P

CHUNKS = 16
TILES = 8
SLOTS = 4
NZ = 8
NX = 4


def pick(cond, a, b):
    return jnp.where(cond, a, b)


def column(yh, z, x):
    return (yh * NZ + z) * NX + x


def tree(core, yh, z, x):
    first = core == 0
    root = (yh == 0) & (x == 0)
    flat = z == 0
    up = (z >= 1) & (z <= 3)
    down = (z == 6) | (z == 7)
    step = pick(up, z + 1, z - 1)
    a0 = pick(first, jnp.logical_not(root), root)
    v0 = (flat | up | down) & a0
    k0 = column(yh, pick(flat, 1, step), x)
    inplane = pick(first, flat, jnp.logical_not(flat))
    zlow = flat & a0
    s1x = inplane & (x <= 1)
    v1 = s1x
    k1 = column(yh, z, x + 1)
    wrap = inplane & (x == 0)
    back = first & (yh == 0) & (x == 1) & jnp.logical_not(flat)
    drop = jnp.logical_not(first) & (z == 1) & jnp.logical_not(root)
    v2 = wrap | back
    k2 = column(yh, z, pick(wrap, 3, 0))
    cross = inplane & root
    v3 = cross | zlow | drop
    k3 = pick(cross, column(1, z, x), column(yh, pick(drop, 0, 7), x))
    kids = ((v0, k0), (v1, k1), (v2, k2), (v3, k3))
    zback = pick(z <= 4, z - 1, (z + 1) % NZ)
    px = pick(x == 2, 1, 0)
    inparent = pick(x == 0, column(0, z, 0), column(yh, z, px))
    p_first = pick(
        flat, inparent, pick(root, column(0, z, 1), column(yh, zback, x))
    )
    p_second = pick(
        root, column(0, zback, 0), pick(flat, column(yh, 1, x), inparent)
    )
    return kids, pick(first, p_first, p_second)


def move_kernel(
    idx, mask, mat_hbm, panel, w_me, w_pair, m_far, mat, comb,
    in_sem, recv_sem, send_sem, x_send, x_recv,
):
    r = lax.axis_index("row")
    c = lax.axis_index("col")
    core = r % 2
    yl = r // 2
    x = c % NX
    z = (c // NX) % NZ
    yh = c // (NX * NZ)
    pair = yl * 2 + 1 - core
    far = (1 - yl) * 2 + core
    source = c == 0
    kids, parent = tree(core, yh, z, x)
    rows = mat_hbm.shape[0]
    tile = rows // TILES
    chunk = rows // CHUNKS
    per = CHUNKS // TILES
    width = panel.shape[1]
    nb = w_me.shape[0]

    def load(t):
        at = pl.ds(pl.multiple_of(t * tile, tile), tile)
        return pltpu.make_async_copy(mat_hbm.at[at], mat.at[at], in_sem.at[t])

    def forward(j, k):
        at = pl.ds(pl.multiple_of(j * chunk, chunk), chunk)
        return pltpu.make_async_remote_copy(
            src_ref=panel.at[at],
            dst_ref=panel.at[at],
            send_sem=send_sem.at[k],
            recv_sem=recv_sem.at[j],
            device_id={"row": r, "col": kids[k][1]},
            device_id_type=pl.DeviceIdType.MESH,
        )

    def send(j):
        for k in range(SLOTS):
            @pl.when(kids[k][0])
            def _():
                forward(j, k).start()

    for t in range(TILES):
        load(t).start()

    barrier = pltpu.get_barrier_semaphore()

    @pl.when(jnp.logical_not(source))
    def _():
        pl.semaphore_signal(
            barrier, inc=1, device_id={"row": r, "col": parent}, device_id_type=pl.DeviceIdType.MESH
        )

    for other in (pair, far):
        pl.semaphore_signal(
            barrier, inc=1, device_id={"row": other, "col": c}, device_id_type=pl.DeviceIdType.MESH
        )
    expect = 2
    for k in range(SLOTS):
        expect = expect + kids[k][0].astype(jnp.int32)
    pl.semaphore_wait(barrier, expect)

    @pl.when(source)
    def _():
        @pl.loop(0, TILES)
        def _(t):
            load(t).wait()
            at = pl.ds(pl.multiple_of(t * tile, tile), tile)
            panel[at] = mat[at, :width].astype(panel.dtype)
            for s in range(per):
                send(t * per + s)

    @pl.when(jnp.logical_not(source))
    def _():
        @pl.loop(0, TILES)
        def _(t):
            load(t).wait()

    @pl.loop(0, nb // 8)
    def _(g):
        for s in range(8):
            i = g * 8 + s
            w_me[pl.ds(i, 1)] = mat[pl.ds(idx[i], 1)]

    swap = pltpu.make_async_remote_copy(
        src_ref=w_me, dst_ref=w_pair, send_sem=x_send.at[0], recv_sem=x_recv.at[0],
        device_id={"row": pair, "col": c}, device_id_type=pl.DeviceIdType.MESH,
    )
    swap.start()
    swap.wait()
    comb[...] = jnp.where(mask[...] == 1, w_pair[...], w_me[...])
    across = pltpu.make_async_remote_copy(
        src_ref=comb, dst_ref=m_far, send_sem=x_send.at[1], recv_sem=x_recv.at[1],
        device_id={"row": far, "col": c}, device_id_type=pl.DeviceIdType.MESH,
    )
    across.start()

    @pl.when(jnp.logical_not(source))
    def _():
        @pl.loop(0, CHUNKS)
        def _(j):
            forward(j, 0).wait_recv()
            send(j)

    across.wait()
    whole = pltpu.make_async_remote_copy
    for k in range(SLOTS):
        @pl.when(kids[k][0])
        def _():
            whole(
                src_ref=panel, dst_ref=panel, send_sem=send_sem.at[k], recv_sem=recv_sem.at[0],
                device_id={"row": r, "col": kids[k][1]}, device_id_type=pl.DeviceIdType.MESH,
            ).wait_send()


def finish_kernel(
    dst, src, flags, mat_hbm, panel, w_me, w_pair, m_far, code, l_inverse,
    out_hbm, u_ref, moved, mat, u_half, top, in_sem, out_sem,
):
    rows = out_hbm.shape[0]
    tile = rows // TILES
    nb = u_ref.shape[0]
    width = panel.shape[1]
    me = flags[0]
    owns_panel = flags[1] == 1

    def piece(t):
        return pl.ds(pl.multiple_of(t * tile, tile), tile)

    def load(t):
        return pltpu.make_async_copy(mat_hbm.at[piece(t)], mat.at[piece(t)], in_sem.at[t])

    def store(t):
        return pltpu.make_async_copy(mat.at[piece(t)], out_hbm.at[piece(t)], out_sem.at[t])

    for t in range(TILES):
        load(t).start()
    who = code[...]
    picked = jnp.where(who == 0, w_me[...], jnp.where(who == 1, w_pair[...], m_far[...]))
    u = jnp.dot(
        l_inverse[...], picked, precision=lax.Precision.HIGHEST, preferred_element_type=jnp.float32
    )
    u_ref[...] = u
    u_half[...] = u.astype(u_half.dtype)

    for t in range(TILES):
        load(t).wait()

    @pl.when(me == 0)
    def _():
        top[...] = mat[pl.ds(0, nb)]

    @pl.when(me == 1)
    def _():
        top[...] = w_pair[...]

    @pl.when(me >= 2)
    def _():
        top[...] = m_far[...]

    @pl.when(owns_panel)
    def _():
        top[:, :width] = w_me[:, :width]

    mat[pl.ds(rows + 8, 8)] = jnp.zeros((8, mat.shape[1]), mat.dtype)

    @pl.loop(0, nb // 8)
    def _(g):
        for s in range(8):
            i = g * 8 + s
            mat[pl.ds(dst[i], 1)] = top[pl.ds(i, 1)]

    @pl.loop(0, TILES)
    def _(t):
        at = piece(t)
        old = mat[at]
        new = old - jnp.dot(panel[at], u_half[...], preferred_element_type=jnp.float32)
        new = jnp.where((t == 0) & (me == 0), u_ref[...], new)
        mat[at, :width] = jnp.where(owns_panel, old[:, :width], new[:, :width])
        mat[at, width:] = new[:, width:]
        store(t).start()

    @pl.loop(0, nb // 8)
    def _(g):
        for s in range(8):
            i = g * 8 + s
            moved[pl.ds(i, 1)] = mat[pl.ds(src[i], 1)]

    for t in range(TILES):
        store(t).wait()


def body(matrix, pivots, l_inverse):
    rows, cols = matrix.shape
    nb = l_inverse.shape[0]
    f32, bf16 = jnp.float32, jnp.bfloat16
    row_count = lax.axis_size("row")
    me = lax.axis_index("row")
    my_col = lax.axis_index("col")
    block = pivots // nb
    owner = block % row_count
    local = block // row_count * nb + pivots % nb
    mine = owner == me
    landed = mine & (pivots >= nb)
    pair = me + 1 - 2 * (me % 2)
    idx = jnp.where(mine, local, jnp.arange(nb)).astype(jnp.int32)
    from_pair = jnp.where(me % 2 == 1, owner != me, owner == pair)
    mask = from_pair.astype(jnp.int32)[:, None]
    code = jnp.where(mine, 0, jnp.where(owner == pair, 1, 2)).astype(jnp.int32)[:, None]
    dst = jnp.where(landed, local, rows).astype(jnp.int32)
    src = jnp.where(landed, local, rows + 8).astype(jnp.int32)
    flags = jnp.stack([me, my_col == 0]).astype(jnp.int32)
    vmem = pl.BlockSpec(memory_space=pltpu.VMEM)
    smem = pl.BlockSpec(memory_space=pltpu.SMEM)
    hbm = pl.BlockSpec(memory_space=pl.ANY)
    shape = jax.ShapeDtypeStruct
    panel, w_me, w_pair, m_far = pl.pallas_call(
        move_kernel,
        out_shape=(
            shape((rows, nb), bf16), shape((nb, cols), f32),
            shape((nb, cols), f32), shape((nb, cols), f32),
        ),
        in_specs=[smem, vmem, hbm],
        out_specs=[vmem] * 4,
        scratch_shapes=[
            pltpu.VMEM((rows, cols), f32),
            pltpu.VMEM((nb, cols), f32),
            pltpu.SemaphoreType.DMA((TILES,)),
            pltpu.SemaphoreType.DMA((CHUNKS,)),
            pltpu.SemaphoreType.DMA((SLOTS,)),
            pltpu.SemaphoreType.DMA((2,)),
            pltpu.SemaphoreType.DMA((2,)),
        ],
        compiler_params=pltpu.CompilerParams(collective_id=0, has_side_effects=True),
        name="move",
    )(idx, mask, matrix)
    return pl.pallas_call(
        finish_kernel,
        out_shape=(shape((rows, cols), f32), shape((nb, cols), f32), shape((nb, cols), f32)),
        in_specs=[smem, smem, smem, hbm] + [vmem] * 6,
        out_specs=[hbm, vmem, vmem],
        scratch_shapes=[
            pltpu.VMEM((rows + 16, cols), f32),
            pltpu.VMEM((nb, cols), bf16),
            pltpu.VMEM((nb, cols), f32),
            pltpu.SemaphoreType.DMA((TILES,)),
            pltpu.SemaphoreType.DMA((TILES,)),
        ],
        name="finish",
    )(dst, src, flags, matrix, panel, w_me, w_pair, m_far, code, l_inverse)


def solution(mesh):
    return jax.shard_map(
        body,
        mesh=mesh,
        in_specs=(P("row", "col"), P(), P()),
        out_specs=(P("row", "col"), P(None, "col"), P("row", "col")),
        check_vma=False,
    )
```

```python
import jax
import jax.numpy as jnp
from jax import lax
from jax.experimental import pallas as pl
from jax.experimental.pallas import tpu as pltpu
from jax.sharding import PartitionSpec as P

CHUNKS = 32
TILES = 8
SLOTS = 4
MOVE_VMEM = 20 * 2**20
FINISH_VMEM = 20 * 2**20
NZ = 8
NX = 4


def pick(cond, a, b):
    return jnp.where(cond, a, b)


def column(yh, z, x):
    return (yh * NZ + z) * NX + x


def tree(core, yh, z, x):
    first = core == 0
    root = (yh == 0) & (x == 0)
    flat = z == 0
    up = (z >= 1) & (z <= 3)
    down = (z == 6) | (z == 7)
    step = pick(up, z + 1, z - 1)
    a0 = pick(first, jnp.logical_not(root), root)
    v0 = (flat | up | down) & a0
    k0 = column(yh, pick(flat, 1, step), x)
    inplane = pick(first, flat, jnp.logical_not(flat))
    zlow = flat & a0
    s1x = inplane & (x <= 1)
    v1 = s1x
    k1 = column(yh, z, x + 1)
    wrap = inplane & (x == 0)
    back = first & (yh == 0) & (x == 1) & jnp.logical_not(flat)
    drop = jnp.logical_not(first) & (z == 1) & jnp.logical_not(root)
    v2 = wrap | back
    k2 = column(yh, z, pick(wrap, 3, 0))
    cross = inplane & root
    v3 = cross | zlow | drop
    k3 = pick(cross, column(1, z, x), column(yh, pick(drop, 0, 7), x))
    kids = ((v0, k0), (v1, k1), (v2, k2), (v3, k3))
    zback = pick(z <= 4, z - 1, (z + 1) % NZ)
    px = pick(x == 2, 1, 0)
    inparent = pick(x == 0, column(0, z, 0), column(yh, z, px))
    p_first = pick(
        flat, inparent, pick(root, column(0, z, 1), column(yh, zback, x))
    )
    p_second = pick(
        root, column(0, zback, 0), pick(flat, column(yh, 1, x), inparent)
    )
    return kids, pick(first, p_first, p_second)


def grid_place():
    r = lax.axis_index("row")
    c = lax.axis_index("col")
    return r, c, r % 2, r // 2, c // (NX * NZ), (c // NX) % NZ, c % NX


def hops(core, yh, z, x):
    dz = jnp.minimum(z, NZ - z)
    dx = jnp.minimum(x, NX - x)
    return dz + dx + yh


def local_row(p, nb, row_count):
    shift = nb.bit_length() - 1
    deal = row_count.bit_length() - 1
    block = jnp.right_shift(p, shift)
    owner = block & (row_count - 1)
    local = jnp.left_shift(jnp.right_shift(block, deal), shift) + (p & (nb - 1))
    return owner, local


def move_kernel(
    pivots, pivot_row, mat_hbm, l_hbm, panel, mat, u_ref, top,
    w_me, w_pair, m_far, comb, code, l_inverse,
    in_sem, recv_sem, send_sem, x_send, x_recv,
):
    r, c, core, yl, yh, z, x = grid_place()
    pair = yl * 2 + 1 - core
    far = (1 - yl) * 2 + core
    source = c == 0
    kids, parent = tree(core, yh, z, x)
    rows, cols = mat_hbm.shape
    tile = rows // TILES
    chunk = rows // CHUNKS
    per = CHUNKS // TILES
    width = panel.shape[1]
    nb = w_me.shape[0]
    half = nb // 2
    row_count = lax.axis_size("row")

    def load(t):
        at = pl.ds(pl.multiple_of(t * tile, tile), tile)
        return pltpu.make_async_copy(mat_hbm.at[at], mat.at[at], in_sem.at[t])

    def forward(j, k):
        at = pl.ds(pl.multiple_of(j * chunk, chunk), chunk)
        return pltpu.make_async_remote_copy(
            src_ref=panel.at[at],
            dst_ref=panel.at[at],
            send_sem=send_sem.at[k],
            recv_sem=recv_sem.at[j],
            device_id={"row": r, "col": kids[k][1]},
            device_id_type=pl.DeviceIdType.MESH,
        )

    def send(j):
        for k in range(SLOTS):
            @pl.when(kids[k][0])
            def _():
                forward(j, k).start()

    def swap(step, src, dst, other):
        return pltpu.make_async_remote_copy(
            src_ref=src, dst_ref=dst, send_sem=x_send.at[step], recv_sem=x_recv.at[step],
            device_id={"row": other, "col": c}, device_id_type=pl.DeviceIdType.MESH,
        )

    mine = pl.ds(pl.multiple_of(core * half, half), half)
    with_pair = swap(0, w_me, w_pair, pair)
    across = swap(1, comb, m_far.at[mine], far)
    pass_on = swap(2, m_far.at[mine], m_far.at[mine], pair)

    for t in range(TILES):
        load(t).start()
    load_l = pltpu.make_async_copy(l_hbm, l_inverse, in_sem.at[TILES])
    load_l.start()

    barrier = pltpu.get_barrier_semaphore()

    @pl.when(jnp.logical_not(source))
    def _():
        pl.semaphore_signal(
            barrier, inc=1, device_id={"row": r, "col": parent}, device_id_type=pl.DeviceIdType.MESH
        )

    for other in (pair, far):
        pl.semaphore_signal(
            barrier, inc=1, device_id={"row": other, "col": c}, device_id_type=pl.DeviceIdType.MESH
        )

    owner, _ = local_row(pivot_row[...], nb, row_count)
    kind = jnp.where(owner == r, 0.0, jnp.where(owner == pair, 1.0, 2.0))
    down = lax.broadcasted_iota(jnp.int32, (nb, nb), 0)
    along = lax.broadcasted_iota(jnp.int32, (nb, nb), 1)
    spread = jnp.where(down == along, jnp.broadcast_to(kind, (nb, nb)), 0.0)
    code[...] = jnp.sum(spread, axis=1, keepdims=True)

    expect = 2
    for k in range(SLOTS):
        expect = expect + kids[k][0].astype(jnp.int32)
    pl.semaphore_wait(barrier, expect)

    @pl.when(source)
    def _():
        @pl.loop(0, TILES)
        def _(t):
            load(t).wait()
            at = pl.ds(pl.multiple_of(t * tile, tile), tile)
            panel[at] = mat[at, :width].astype(panel.dtype)
            for s in range(per):
                send(t * per + s)

    @pl.when(jnp.logical_not(source))
    def _():
        @pl.loop(0, TILES)
        def _(t):
            load(t).wait()

    @pl.loop(0, nb // 8)
    def _(g):
        for s in range(8):
            i = g * 8 + s
            own, local = local_row(pivots[i], nb, row_count)
            w_me[pl.ds(i, 1)] = mat[pl.ds(jnp.where(own == r, local, i), 1)]

    with_pair.start()

    def step_across():
        with_pair.wait_recv()
        kind = code[mine]
        from_pair = (kind > 0.5) & (kind < jnp.where(core == 1, 9.0, 1.5))
        comb[...] = jnp.where(from_pair, w_pair[mine], w_me[mine])
        across.start()

    def step_pass():
        across.wait_recv()
        pass_on.start()

    def step_u():
        load_l.wait()
        pass_other = swap(2, m_far.at[mine], m_far.at[mine], pair)
        pass_other.wait_recv()
        kind = code[...]
        picked = jnp.where(kind < 0.5, w_me[...], jnp.where(kind < 1.5, w_pair[...], m_far[...]))
        u_ref[...] = jnp.dot(
            l_inverse[...], picked, precision=lax.Precision.HIGHEST, preferred_element_type=jnp.float32
        )

        @pl.when(r == 0)
        def _():
            top[...] = mat[pl.ds(0, nb)]

        @pl.when(r == 1)
        def _():
            top[...] = w_pair[...]

        @pl.when(r >= 2)
        def _():
            top[...] = m_far[...]

        @pl.when(source)
        def _():
            top[:, :width] = w_me[:, :width]

    depth = hops(core, yh, z, x)
    leaf = expect == 2
    scale = CHUNKS // 8
    late = (x == 0) & (z == 0)
    at_across = jnp.where(late, CHUNKS, jnp.where(depth <= 1, scale, 0))
    at_pass = jnp.where(
        late, CHUNKS, jnp.maximum(0, scale * 7 - (scale * 3) // 2 * (depth - 1))
    )
    at_u = jnp.where(leaf & (depth >= 5), CHUNKS // 2, CHUNKS)

    @pl.when(jnp.logical_not(source))
    def _():
        @pl.loop(0, CHUNKS)
        def _(j):
            pl.when(j == at_across)(step_across)
            pl.when(j == at_pass)(step_pass)
            pl.when(j == at_u)(step_u)
            forward(j, 0).wait_recv()
            send(j)

    pl.when(at_across == CHUNKS)(step_across)
    pl.when(at_pass == CHUNKS)(step_pass)
    pl.when(at_u == CHUNKS)(step_u)

    with_pair.wait_send()
    across.wait_send()
    pass_on.wait_send()
    for k in range(SLOTS):
        @pl.when(kids[k][0])
        def _():
            pltpu.make_async_remote_copy(
                src_ref=panel, dst_ref=panel, send_sem=send_sem.at[k], recv_sem=recv_sem.at[0],
                device_id={"row": r, "col": kids[k][1]}, device_id_type=pl.DeviceIdType.MESH,
            ).wait_send()


def finish_kernel(
    pivots, work_in, panel, u_ref, top,
    out_hbm, u_out, moved, mat, u_half, out_sem, u_sem,
):
    del work_in
    rows = out_hbm.shape[0]
    tile = rows // TILES
    nb, cols = u_ref.shape
    width = panel.shape[1]
    row_count = lax.axis_size("row")
    me = lax.axis_index("row")
    owns_panel = lax.axis_index("col") == 0

    def piece(t):
        return pl.ds(pl.multiple_of(t * tile, tile), tile)

    def store(t):
        return pltpu.make_async_copy(mat.at[piece(t)], out_hbm.at[piece(t)], out_sem.at[t])

    def target(i, other):
        p = pivots[i]
        own, local = local_row(p, nb, row_count)
        return jnp.where((own == me) & (p >= nb), local, other)

    give_u = pltpu.make_async_copy(u_ref, u_out, u_sem.at[0])
    give_u.start()
    u_half[...] = u_ref[...].astype(u_half.dtype)
    mat[pl.ds(rows + 8, 8)] = jnp.zeros((8, cols), mat.dtype)

    @pl.loop(0, nb // 8)
    def _(g):
        for s in range(8):
            i = g * 8 + s
            mat[pl.ds(target(i, rows), 1)] = top[pl.ds(i, 1)]

    @pl.loop(0, TILES)
    def _(t):
        at = piece(t)
        old = mat[at]
        new = old - jnp.dot(panel[at], u_half[...], preferred_element_type=jnp.float32)
        new = jnp.where((t == 0) & (me == 0), u_ref[...], new)
        mat[at, :width] = jnp.where(owns_panel, old[:, :width], new[:, :width])
        mat[at, width:] = new[:, width:]
        store(t).start()

    @pl.loop(0, nb // 8)
    def _(g):
        for s in range(8):
            i = g * 8 + s
            moved[pl.ds(i, 1)] = mat[pl.ds(target(i, rows + 8), 1)]

    for t in range(TILES):
        store(t).wait()
    give_u.wait()


def body(matrix, pivots, l_inverse):
    rows, cols = matrix.shape
    nb = l_inverse.shape[0]
    f32, bf16 = jnp.float32, jnp.bfloat16
    vmem = pl.BlockSpec(memory_space=pltpu.VMEM)
    smem = pl.BlockSpec(memory_space=pltpu.SMEM)
    hbm = pl.BlockSpec(memory_space=pltpu.HBM)
    shape = jax.ShapeDtypeStruct
    panel, work, u_rows, top = pl.pallas_call(
        move_kernel,
        out_shape=(
            shape((rows, nb), bf16), shape((rows + 16, cols), f32),
            shape((nb, cols), f32), shape((nb, cols), f32),
        ),
        in_specs=[smem, vmem, hbm, hbm],
        out_specs=[vmem] * 4,
        scratch_shapes=[
            pltpu.VMEM((nb, cols), f32),
            pltpu.VMEM((nb, cols), f32),
            pltpu.VMEM((nb, cols), f32),
            pltpu.VMEM((nb // 2, cols), f32),
            pltpu.VMEM((nb, 1), f32),
            pltpu.VMEM((nb, nb), f32),
            pltpu.SemaphoreType.DMA((TILES + 1,)),
            pltpu.SemaphoreType.DMA((CHUNKS,)),
            pltpu.SemaphoreType.DMA((SLOTS,)),
            pltpu.SemaphoreType.DMA((3,)),
            pltpu.SemaphoreType.DMA((3,)),
        ],
        compiler_params=pltpu.CompilerParams(
            collective_id=0, has_side_effects=True, vmem_limit_bytes=MOVE_VMEM
        ),
        name="move",
    )(pivots, pivots.reshape(1, nb), matrix, l_inverse)
    out, u_block, moved, _ = pl.pallas_call(
        finish_kernel,
        out_shape=(
            shape((rows, cols), f32), shape((nb, cols), f32), shape((nb, cols), f32),
            shape((rows + 16, cols), f32),
        ),
        in_specs=[smem] + [vmem] * 4,
        out_specs=[hbm, hbm, vmem, vmem],
        scratch_shapes=[
            pltpu.VMEM((nb, cols), bf16),
            pltpu.SemaphoreType.DMA((TILES,)),
            pltpu.SemaphoreType.DMA((1,)),
        ],
        input_output_aliases={1: 3},
        compiler_params=pltpu.CompilerParams(vmem_limit_bytes=FINISH_VMEM),
        name="finish",
    )(pivots, work, panel, u_rows, top)
    return out, u_block, moved


def solution(mesh):
    return jax.shard_map(
        body,
        mesh=mesh,
        in_specs=(P("row", "col"), P(), P()),
        out_specs=(P("row", "col"), P(None, "col"), P("row", "col")),
        check_vma=False,
    )
```

```python
import jax
import jax.numpy as jnp
from jax import lax
from jax.experimental import pallas as pl
from jax.experimental.pallas import tpu as pltpu
from jax.sharding import PartitionSpec as P

CHUNKS = 32
TILES = 8
SLOTS = 4
MOVE_VMEM = 24 * 2**20
FINISH_VMEM = 8 * 2**20
NZ = 8
NX = 4


def pick(cond, a, b):
    return jnp.where(cond, a, b)


def column(yh, z, x):
    return (yh * NZ + z) * NX + x


def tree(core, yh, z, x):
    first = core == 0
    root = (yh == 0) & (x == 0)
    flat = z == 0
    up = (z >= 1) & (z <= 3)
    down = (z == 6) | (z == 7)
    step = pick(up, z + 1, z - 1)
    a0 = pick(first, jnp.logical_not(root), root)
    v0 = (flat | up | down) & a0
    k0 = column(yh, pick(flat, 1, step), x)
    inplane = pick(first, flat, jnp.logical_not(flat))
    zlow = flat & a0
    s1x = inplane & (x <= 1)
    v1 = s1x
    k1 = column(yh, z, x + 1)
    wrap = inplane & (x == 0)
    back = first & (yh == 0) & (x == 1) & jnp.logical_not(flat)
    drop = jnp.logical_not(first) & (z == 1) & jnp.logical_not(root)
    v2 = wrap | back
    k2 = column(yh, z, pick(wrap, 3, 0))
    cross = inplane & root
    v3 = cross | zlow | drop
    k3 = pick(cross, column(1, z, x), column(yh, pick(drop, 0, 7), x))
    kids = ((v0, k0), (v1, k1), (v2, k2), (v3, k3))
    zback = pick(z <= 4, z - 1, (z + 1) % NZ)
    px = pick(x == 2, 1, 0)
    inparent = pick(x == 0, column(0, z, 0), column(yh, z, px))
    p_first = pick(
        flat, inparent, pick(root, column(0, z, 1), column(yh, zback, x))
    )
    p_second = pick(
        root, column(0, zback, 0), pick(flat, column(yh, 1, x), inparent)
    )
    return kids, pick(first, p_first, p_second)


def place():
    r = lax.axis_index("row")
    c = lax.axis_index("col")
    return r, c, r % 2, r // 2, c // (NX * NZ), (c // NX) % NZ, c % NX


def hops(core, yh, z, x):
    dz = jnp.minimum(z, NZ - z)
    dx = jnp.minimum(x, NX - x)
    root = (yh == 0) & (x == 0)
    flat = z == 0
    around = pick(core == 0, root & jnp.logical_not(flat), flat & jnp.logical_not(root))
    return dz + dx + yh + pick(around, 2, 0)


def local_row(p, nb, row_count):
    shift = nb.bit_length() - 1
    deal = row_count.bit_length() - 1
    block = jnp.right_shift(p, shift)
    owner = block & (row_count - 1)
    local = jnp.left_shift(jnp.right_shift(block, deal), shift) + (p & (nb - 1))
    return owner, local


def move_kernel(
    pivots_hbm, row_hbm, mat_hbm, l_hbm, mat, u_ref,
    panel, w_me, w_pair, m_far, comb, code, l_inverse, pivot_row, u_half, top, parts, pivots,
    in_sem, recv_sem, send_sem, x_send, x_recv,
):
    r, c, core, yl, yh, z, x = place()
    pair = yl * 2 + 1 - core
    far = (1 - yl) * 2 + core
    source = c == 0
    other = jnp.logical_not(source)
    kids, parent = tree(core, yh, z, x)
    rows, cols = mat_hbm.shape
    tile = rows // TILES
    chunk = rows // CHUNKS
    per = CHUNKS // TILES
    nb, width = l_hbm.shape
    half = nb // 2
    row_count = lax.axis_size("row")

    def load(t):
        at = pl.ds(pl.multiple_of(t * tile, tile), tile)
        return pltpu.make_async_copy(mat_hbm.at[at], mat.at[at], in_sem.at[t])

    def forward(j, k):
        at = pl.ds(pl.multiple_of(j * chunk, chunk), chunk)
        return pltpu.make_async_remote_copy(
            src_ref=panel.at[at],
            dst_ref=panel.at[at],
            send_sem=send_sem.at[k],
            recv_sem=recv_sem.at[j],
            device_id={"row": r, "col": kids[k][1]},
            device_id_type=pl.DeviceIdType.MESH,
        )

    def send(j):
        for k in range(SLOTS):
            @pl.when(kids[k][0])
            def _():
                forward(j, k).start()

    def swap(step, src, dst, to):
        return pltpu.make_async_remote_copy(
            src_ref=src, dst_ref=dst, send_sem=x_send.at[step], recv_sem=x_recv.at[step],
            device_id={"row": to, "col": c}, device_id_type=pl.DeviceIdType.MESH,
        )

    def signal(row, col):
        pl.semaphore_signal(
            barrier, inc=1, device_id={"row": row, "col": col}, device_id_type=pl.DeviceIdType.MESH
        )

    mine = pl.ds(pl.multiple_of(core * half, half), half)
    with_pair = swap(0, w_me, w_pair, pair)
    across = swap(1, comb, m_far.at[mine], far)
    pass_on = swap(2, m_far.at[mine], m_far.at[mine], pair)

    barrier = pltpu.get_barrier_semaphore()

    @pl.when(other)
    def _():
        signal(r, parent)

    signal(pair, c)
    signal(far, c)
    load_p = pltpu.make_async_copy(pivots_hbm, pivots, in_sem.at[TILES])
    load_q = pltpu.make_async_copy(row_hbm, pivot_row, in_sem.at[TILES + 1])
    load_l = pltpu.make_async_copy(l_hbm, l_inverse, in_sem.at[TILES + 2])
    load(0).start()
    load_p.start()
    load_q.start()
    for t in range(1, TILES):
        load(t).start()
    load_l.start()

    expect = 2
    for k in range(SLOTS):
        expect = expect + kids[k][0].astype(jnp.int32)
    pl.semaphore_wait(barrier, expect)

    @pl.when(source)
    def _():
        @pl.loop(0, TILES)
        def _(t):
            load(t).wait()
            at = pl.ds(pl.multiple_of(t * tile, tile), tile)
            panel[at] = mat[at, :width].astype(panel.dtype)
            for s in range(per):
                send(t * per + s)

    @pl.when(other)
    def _():
        @pl.loop(0, TILES)
        def _(t):
            load(t).wait()

    load_p.wait()

    @pl.loop(0, nb // 8)
    def _(g):
        for s in range(8):
            i = g * 8 + s
            own, local = local_row(pivots[i], nb, row_count)
            w_me[pl.ds(i, 1)] = mat[pl.ds(jnp.where(own == r, local, i), 1)]

    with_pair.start()

    load_q.wait()
    owner, local = local_row(pivot_row[...], nb, row_count)
    kind = jnp.where(owner == r, 0.0, jnp.where(owner == pair, 1.0, 2.0))
    down = lax.broadcasted_iota(jnp.int32, (nb, nb), 0)
    along = lax.broadcasted_iota(jnp.int32, (nb, nb), 1)
    spread = jnp.where(down == along, jnp.broadcast_to(kind, (nb, nb)), 0.0)
    code[...] = jnp.sum(spread, axis=1, keepdims=True)
    pivot_row[...] = jnp.where((owner == r) & (pivot_row[...] >= nb), local, rows)

    def step_across():
        with_pair.wait_recv()
        kind = code[mine]
        from_pair = (kind > 0.5) & (kind < jnp.where(core == 1, 9.0, 1.5))
        comb[...] = jnp.where(from_pair, w_pair[mine], w_me[mine])
        across.start()

    def step_pass():
        across.wait_recv()
        pass_on.start()

    def step_u():
        load_l.wait()
        pass_on.wait_recv()
        kind = code[...]
        picked = jnp.where(kind < 0.5, w_me[...], jnp.where(kind < 1.5, w_pair[...], m_far[...]))
        u = jnp.dot(
            l_inverse[...], picked, precision=lax.Precision.HIGHEST, preferred_element_type=jnp.float32
        )
        u_ref[...] = u
        u_half[...] = u.astype(u_half.dtype)

        @pl.when(r == 0)
        def _():
            top[...] = mat[pl.ds(0, nb)]

        @pl.when(r == 1)
        def _():
            top[...] = w_pair[...]

        @pl.when(r >= 2)
        def _():
            top[...] = m_far[...]

        @pl.when(source)
        def _():
            top[:, :width] = w_me[:, :width]

        whole = top[...]
        edge = float(jnp.finfo(jnp.bfloat16).max)
        for p in range(3):
            part = jnp.clip(whole, -edge, edge).astype(jnp.bfloat16)
            parts[p] = part
            whole = whole - part.astype(jnp.float32)

        @pl.loop(0, TILES)
        def _(t):
            at = pl.ds(pl.multiple_of(t * tile, tile), tile)
            place = lax.broadcasted_iota(jnp.int32, (tile, nb), 0) + t * tile
            onehot = jnp.where(place == pivot_row[...], 1.0, 0.0)
            hit = jnp.max(onehot, axis=1, keepdims=True) > 0.5
            onehot = onehot.astype(jnp.bfloat16)
            rows_in = jnp.zeros((tile, cols), jnp.float32)
            for p in (2, 1, 0):
                rows_in += jnp.dot(onehot, parts[p], preferred_element_type=jnp.float32)
            mat[at] = jnp.where(hit, rows_in, mat[at])

    def update(j, size):
        at = pl.ds(pl.multiple_of(j * size, size), size)
        is_top = (r == 0) & (j < nb // size)

        @pl.when(is_top & other)
        def _():
            mat[at] = u_ref[pl.ds(pl.multiple_of((j % (nb // size)) * size, size), size)]

        @pl.when(is_top & source)
        def _():
            mat[at, width:] = u_ref[pl.ds(pl.multiple_of((j % (nb // size)) * size, size), size), width:]

        @pl.when(jnp.logical_not(is_top) & other)
        def _():
            mat[at] = mat[at] - jnp.dot(panel[at], u_half[...], preferred_element_type=jnp.float32)

        @pl.when(jnp.logical_not(is_top) & source)
        def _():
            mat[at, width:] = mat[at, width:] - jnp.dot(
                panel[at], u_half[:, width:], preferred_element_type=jnp.float32
            )

    depth = hops(core, yh, z, x)
    leaf = expect == 2
    early = leaf & (depth >= 5)
    scale = CHUNKS // 8
    late = (yh == 1) & (x == 0) & (z == 0)
    first_go = pick(late, pick(core == 0, CHUNKS, scale * 5), pick(depth <= 1, scale, 0))
    pass_go = jnp.maximum(0, scale * 7 - (scale * 3) // 2 * (depth - 1))
    at_across = pick(source, CHUNKS, first_go)
    at_pass = pick(source | late, CHUNKS, pick(early, 0, pass_go))
    at_u = pick(early, 0, CHUNKS)

    @pl.loop(pick(source, CHUNKS, 0), CHUNKS + 1)
    def _(j):
        pl.when(j == at_across)(step_across)
        pl.when(j == at_pass)(step_pass)
        pl.when(j == at_u)(step_u)

        @pl.when(j < CHUNKS)
        def _():
            forward(j, 0).wait_recv()
            send(j)

            @pl.when(early)
            def _():
                update(j, chunk)

    @pl.when(jnp.logical_not(early))
    def _():
        @pl.loop(0, TILES)
        def _(t):
            update(t, tile)

    with_pair.wait_send()
    across.wait_send()
    pass_on.wait_send()
    for k in range(SLOTS):
        @pl.when(kids[k][0])
        def _():
            pltpu.make_async_remote_copy(
                src_ref=panel, dst_ref=panel, send_sem=send_sem.at[k], recv_sem=recv_sem.at[0],
                device_id={"row": r, "col": kids[k][1]}, device_id_type=pl.DeviceIdType.MESH,
            ).wait_send()


def finish_kernel(pivots_hbm, mat, u_ref, out, u_out, moved_out, moved, pivots, sem):
    rows = out.shape[0]
    tile = rows // TILES
    nb = u_ref.shape[0]
    row_count = lax.axis_size("row")
    me = lax.axis_index("row")
    load_p = pltpu.make_async_copy(pivots_hbm, pivots, sem.at[TILES])
    load_p.start()
    copies = [
        pltpu.make_async_copy(mat.at[pl.ds(t * tile, tile)], out.at[pl.ds(t * tile, tile)], sem.at[t])
        for t in range(TILES)
    ]
    copies.append(pltpu.make_async_copy(u_ref, u_out, sem.at[TILES + 1]))
    for copy in copies:
        copy.start()
    load_p.wait()

    @pl.loop(0, nb // 8)
    def _(g):
        for s in range(8):
            i = g * 8 + s
            p = pivots[i]
            own, local = local_row(p, nb, row_count)
            land = (own == me) & (p >= nb)
            row = mat[pl.ds(jnp.where(land, local, 0), 1)]
            moved[pl.ds(i, 1)] = jnp.where(land, row, jnp.zeros_like(row))

    last = pltpu.make_async_copy(moved, moved_out, sem.at[TILES + 2])
    last.start()
    copies.append(last)
    for copy in copies:
        copy.wait()


def body(matrix, pivots, l_inverse):
    rows, cols = matrix.shape
    nb = l_inverse.shape[0]
    f32, bf16, i32 = jnp.float32, jnp.bfloat16, jnp.int32
    vmem = pl.BlockSpec(memory_space=pltpu.VMEM)
    hbm = pl.BlockSpec(memory_space=pltpu.HBM)
    shape = jax.ShapeDtypeStruct
    stay = lambda array: pltpu.with_memory_space_constraint(array, pltpu.HBM)
    work, u_rows = pl.pallas_call(
        move_kernel,
        out_shape=(shape((rows, cols), f32), shape((nb, cols), f32)),
        in_specs=[hbm] * 4,
        out_specs=[vmem] * 2,
        scratch_shapes=[
            pltpu.VMEM((rows, nb), bf16),
            pltpu.VMEM((nb, cols), f32),
            pltpu.VMEM((nb, cols), f32),
            pltpu.VMEM((nb, cols), f32),
            pltpu.VMEM((nb // 2, cols), f32),
            pltpu.VMEM((nb, 1), f32),
            pltpu.VMEM((nb, nb), f32),
            pltpu.VMEM((1, nb), i32),
            pltpu.VMEM((nb, cols), bf16),
            pltpu.VMEM((nb, cols), f32),
            pltpu.VMEM((3, nb, cols), bf16),
            pltpu.SMEM((nb,), i32),
            pltpu.SemaphoreType.DMA((TILES + 3,)),
            pltpu.SemaphoreType.DMA((CHUNKS,)),
            pltpu.SemaphoreType.DMA((SLOTS,)),
            pltpu.SemaphoreType.DMA((3,)),
            pltpu.SemaphoreType.DMA((3,)),
        ],
        compiler_params=pltpu.CompilerParams(
            collective_id=0, has_side_effects=True, vmem_limit_bytes=MOVE_VMEM
        ),
        name="move",
    )(stay(pivots), stay(pivots.reshape(1, nb)), stay(matrix), stay(l_inverse))
    return pl.pallas_call(
        finish_kernel,
        out_shape=(shape((rows, cols), f32), shape((nb, cols), f32), shape((nb, cols), f32)),
        in_specs=[hbm, vmem, vmem],
        out_specs=[hbm] * 3,
        scratch_shapes=[
            pltpu.VMEM((nb, cols), f32),
            pltpu.SMEM((nb,), i32),
            pltpu.SemaphoreType.DMA((TILES + 3,)),
        ],
        compiler_params=pltpu.CompilerParams(vmem_limit_bytes=FINISH_VMEM),
        name="finish",
    )(stay(pivots), work, u_rows)


def solution(mesh):
    return jax.shard_map(
        body,
        mesh=mesh,
        in_specs=(P("row", "col"), P(), P()),
        out_specs=(P("row", "col"), P(None, "col"), P("row", "col")),
        check_vma=False,
    )
```

```python
import jax
import jax.numpy as jnp
from jax import lax
from jax.experimental import pallas as pl
from jax.experimental.pallas import tpu as pltpu
from jax.sharding import PartitionSpec as P

CHUNKS = 32
TILES = 8
SLOTS = 4
PARTS = 3
MOVE_VMEM = 24 * 2**20
FINISH_VMEM = 8 * 2**20
NZ = 8
NX = 4


def pick(cond, a, b):
    return jnp.where(cond, a, b)


def column(yh, z, x):
    return (yh * NZ + z) * NX + x


def tree(core, yh, z, x):
    first = core == 0
    root = (yh == 0) & (x == 0)
    flat = z == 0
    up = (z >= 1) & (z <= 3)
    down = (z == 6) | (z == 7)
    step = pick(up, z + 1, z - 1)
    a0 = pick(first, jnp.logical_not(root), root)
    v0 = (flat | up | down) & a0
    k0 = column(yh, pick(flat, 1, step), x)
    inplane = pick(first, flat, jnp.logical_not(flat))
    zlow = flat & a0
    s1x = inplane & (x <= 1)
    v1 = s1x
    k1 = column(yh, z, x + 1)
    wrap = inplane & (x == 0)
    back = first & (yh == 0) & (x == 1) & jnp.logical_not(flat)
    drop = jnp.logical_not(first) & (z == 1) & jnp.logical_not(root)
    v2 = wrap | back
    k2 = column(yh, z, pick(wrap, 3, 0))
    cross = inplane & root
    v3 = cross | zlow | drop
    k3 = pick(cross, column(1, z, x), column(yh, pick(drop, 0, 7), x))
    kids = ((v0, k0), (v1, k1), (v2, k2), (v3, k3))
    zback = pick(z <= 4, z - 1, (z + 1) % NZ)
    px = pick(x == 2, 1, 0)
    inparent = pick(x == 0, column(0, z, 0), column(yh, z, px))
    p_first = pick(
        flat, inparent, pick(root, column(0, z, 1), column(yh, zback, x))
    )
    p_second = pick(
        root, column(0, zback, 0), pick(flat, column(yh, 1, x), inparent)
    )
    return kids, pick(first, p_first, p_second)


def place():
    r = lax.axis_index("row")
    c = lax.axis_index("col")
    return r, c, r % 2, r // 2, c // (NX * NZ), (c // NX) % NZ, c % NX


def hops(core, yh, z, x):
    dz = jnp.minimum(z, NZ - z)
    dx = jnp.minimum(x, NX - x)
    root = (yh == 0) & (x == 0)
    flat = z == 0
    around = pick(core == 0, root & jnp.logical_not(flat), flat & jnp.logical_not(root))
    return dz + dx + yh + pick(around, 2, 0)


def local_row(p, nb, row_count):
    shift = nb.bit_length() - 1
    deal = row_count.bit_length() - 1
    block = jnp.right_shift(p, shift)
    owner = block & (row_count - 1)
    local = jnp.left_shift(jnp.right_shift(block, deal), shift) + (p & (nb - 1))
    return owner, local


def move_kernel(
    row_hbm, mat_hbm, l_hbm, mat, u_ref, takes,
    panel, w_me, w_pair, m_far, comb, code, l_inverse, pivot_row, u_half, parts, from_row, from_at,
    in_sem, recv_sem, send_sem, x_send, x_recv,
):
    r, c, core, yl, yh, z, x = place()
    pair = yl * 2 + 1 - core
    far = (1 - yl) * 2 + core
    source = c == 0
    other = jnp.logical_not(source)
    kids, parent = tree(core, yh, z, x)
    rows, cols = mat_hbm.shape
    tile = rows // TILES
    chunk = rows // CHUNKS
    per = CHUNKS // TILES
    nb, width = l_hbm.shape
    half = nb // 2
    row_count = lax.axis_size("row")

    def load(t):
        at = pl.ds(pl.multiple_of(t * tile, tile), tile)
        return pltpu.make_async_copy(mat_hbm.at[at], mat.at[at], in_sem.at[t])

    def forward(j, k):
        at = pl.ds(pl.multiple_of(j * chunk, chunk), chunk)
        return pltpu.make_async_remote_copy(
            src_ref=panel.at[at],
            dst_ref=panel.at[at],
            send_sem=send_sem.at[k],
            recv_sem=recv_sem.at[j],
            device_id={"row": r, "col": kids[k][1]},
            device_id_type=pl.DeviceIdType.MESH,
        )

    def send(j):
        for k in range(SLOTS):
            @pl.when(kids[k][0])
            def _():
                forward(j, k).start()

    def swap(step, src, dst, to):
        return pltpu.make_async_remote_copy(
            src_ref=src, dst_ref=dst, send_sem=x_send.at[step], recv_sem=x_recv.at[step],
            device_id={"row": to, "col": c}, device_id_type=pl.DeviceIdType.MESH,
        )

    def signal(row, col):
        pl.semaphore_signal(
            barrier, inc=1, device_id={"row": row, "col": col}, device_id_type=pl.DeviceIdType.MESH
        )

    mine = pl.ds(pl.multiple_of(core * half, half), half)
    with_pair = swap(0, w_me, w_pair, pair)
    across = swap(1, comb, m_far.at[mine], far)
    pass_on = swap(2, m_far.at[mine], m_far.at[mine], pair)

    barrier = pltpu.get_barrier_semaphore()

    @pl.when(other)
    def _():
        signal(r, parent)

    signal(pair, c)
    signal(far, c)
    load_p = pltpu.make_async_copy(row_hbm, pivot_row, in_sem.at[TILES])
    give_p = pltpu.make_async_copy(from_row, from_at, in_sem.at[TILES + 1])
    load_l = pltpu.make_async_copy(l_hbm, l_inverse, in_sem.at[TILES + 2])
    load_p.start()
    load(0).start()
    for t in range(1, TILES):
        load(t).start()
    load_l.start()

    load_p.wait()
    owner, local = local_row(pivot_row[...], nb, row_count)
    from_row[...] = jnp.where(owner == r, local, lax.broadcasted_iota(jnp.int32, (1, nb), 1))
    takes[...] = jnp.where((owner == r) & (pivot_row[...] >= nb), local, rows)
    mat[pl.ds(rows, 8)] = jnp.zeros((8, cols), mat.dtype)
    kind = jnp.where(owner == r, 0.0, jnp.where(owner == pair, 1.0, 2.0))
    down = lax.broadcasted_iota(jnp.int32, (nb, nb), 0)
    along = lax.broadcasted_iota(jnp.int32, (nb, nb), 1)
    spread = jnp.where(down == along, jnp.broadcast_to(kind, (nb, nb)), 0.0)
    code[...] = jnp.sum(spread, axis=1, keepdims=True)
    give_p.start()

    expect = 2
    for k in range(SLOTS):
        expect = expect + kids[k][0].astype(jnp.int32)
    pl.semaphore_wait(barrier, expect)

    @pl.when(source)
    def _():
        @pl.loop(0, TILES)
        def _(t):
            load(t).wait()
            at = pl.ds(pl.multiple_of(t * tile, tile), tile)
            panel[at] = mat[at, :width].astype(panel.dtype)
            for s in range(per):
                send(t * per + s)

    @pl.when(other)
    def _():
        @pl.loop(0, TILES)
        def _(t):
            load(t).wait()

    give_p.wait()

    @pl.loop(0, nb // 8)
    def _(g):
        out = w_me.at[pl.ds(pl.multiple_of(g * 8, 8), 8)]
        got = [mat[pl.ds(from_at[0, g * 8 + s], 1)] for s in range(8)]
        for s in range(8):
            out[pl.ds(s, 1)] = got[s]

    with_pair.start()

    def step_across():
        with_pair.wait_recv()
        kind = code[mine]
        from_pair = (kind > 0.5) & (kind < jnp.where(core == 1, 9.0, 1.5))
        comb[...] = jnp.where(from_pair, w_pair[mine], w_me[mine])
        across.start()

    def step_pass():
        across.wait_recv()
        pass_on.start()

    def step_u():
        load_l.wait()
        pass_on.wait_recv()
        kind = code[...]
        picked = jnp.where(kind < 0.5, w_me[...], jnp.where(kind < 1.5, w_pair[...], m_far[...]))
        u = jnp.dot(
            l_inverse[...], picked, precision=lax.Precision.HIGHEST, preferred_element_type=jnp.float32
        )
        u_ref[...] = u
        u_half[...] = u.astype(u_half.dtype)

        def split(at, whole):
            edge = float(jnp.finfo(jnp.bfloat16).max)
            for p in range(PARTS):
                part = jnp.clip(whole, -edge, edge).astype(jnp.bfloat16)
                parts[pl.ds(p * nb, nb), at] = part
                whole = whole - part.astype(jnp.float32)

        whole = jnp.where(r == 0, mat[pl.ds(0, nb)], jnp.where(r == 1, w_pair[...], m_far[...]))
        split(pl.ds(0, cols), whole)

        @pl.when(source)
        def _():
            split(pl.ds(0, width), w_me[:, :width])

    def step_swap(t):
        at = pl.ds(pl.multiple_of(t * tile, tile), tile)
        index = lax.broadcasted_iota(jnp.int32, (tile, nb), 0) + t * tile
        onehot = jnp.where(index == takes[...], 1.0, 0.0)
        hit = jnp.max(onehot, axis=1, keepdims=True) > 0.5
        onehot = onehot.astype(jnp.bfloat16)
        rows_in = jnp.dot(
            jnp.concatenate([onehot] * PARTS, axis=1), parts[...], preferred_element_type=jnp.float32
        )
        mat[at] = jnp.where(hit, rows_in, mat[at])

    def update(j, size):
        at = pl.ds(pl.multiple_of(j * size, size), size)
        is_top = (r == 0) & (j < nb // size)

        @pl.when(is_top & other)
        def _():
            mat[at] = u_ref[pl.ds(pl.multiple_of((j % (nb // size)) * size, size), size)]

        @pl.when(is_top & source)
        def _():
            mat[at, width:] = u_ref[pl.ds(pl.multiple_of((j % (nb // size)) * size, size), size), width:]

        @pl.when(jnp.logical_not(is_top) & other)
        def _():
            mat[at] = mat[at] - jnp.dot(panel[at], u_half[...], preferred_element_type=jnp.float32)

        @pl.when(jnp.logical_not(is_top) & source)
        def _():
            mat[at, width:] = mat[at, width:] - jnp.dot(
                panel[at], u_half[:, width:], preferred_element_type=jnp.float32
            )

    depth = hops(core, yh, z, x)
    leaf = expect == 2
    free = leaf | source | (depth >= 6)
    scale = CHUNKS // 8
    swapped = 1 + 2 * TILES
    late = (yh == 1) & (x == 0) & (z == 0)
    late_go = pick(core == 0, CHUNKS - scale // 2, scale * 5)
    at_across = pick(late, late_go, pick((depth <= 1) & other, scale, 0))
    pass_go = jnp.maximum(0, scale * 7 - (scale * 3) // 2 * (depth - 1))
    at_pass = pick(late, pick(core == 0, CHUNKS, scale * 5 + 1), pick(free, 0, pass_go))
    at_u = pick(late, at_pass + 1, pick(free, 0, CHUNKS))

    @pl.loop(0, jnp.maximum(CHUNKS, at_u + swapped + CHUNKS // 2))
    def _(j):
        pl.when(j == at_across)(step_across)
        pl.when(j == at_pass)(step_pass)

        q = j - at_u
        pl.when(q == 0)(step_u)

        @pl.when((j < CHUNKS) & other)
        def _():
            forward(j, 0).wait_recv()
            send(j)

        @pl.when((q > 0) & (q < swapped) & (q % 2 == 0))
        def _():
            step_swap(q // 2 - 1)

        @pl.when(q >= swapped)
        def _():
            k = (q - swapped) * 2

            @pl.loop(jnp.minimum(k, j), jnp.minimum(jnp.minimum(k + 2, j + 1), CHUNKS))
            def _(i):
                update(i, chunk)

    with_pair.wait_send()
    across.wait_send()
    pass_on.wait_send()
    for k in range(SLOTS):
        @pl.when(kids[k][0])
        def _():
            pltpu.make_async_remote_copy(
                src_ref=panel, dst_ref=panel, send_sem=send_sem.at[k], recv_sem=recv_sem.at[0],
                device_id={"row": r, "col": kids[k][1]}, device_id_type=pl.DeviceIdType.MESH,
            ).wait_send()


def finish_kernel(mat, u_ref, takes, out, u_out, moved_out, moved, takes_at, sem):
    rows = out.shape[0]
    tile = rows // TILES
    nb = u_ref.shape[0]
    give_t = pltpu.make_async_copy(takes, takes_at, sem.at[TILES])
    give_t.start()
    copies = [
        pltpu.make_async_copy(mat.at[pl.ds(t * tile, tile)], out.at[pl.ds(t * tile, tile)], sem.at[t])
        for t in range(TILES)
    ]
    copies.append(pltpu.make_async_copy(u_ref, u_out, sem.at[TILES + 1]))
    for copy in copies:
        copy.start()
    give_t.wait()

    @pl.loop(0, nb // 8)
    def _(g):
        eight = moved.at[pl.ds(pl.multiple_of(g * 8, 8), 8)]
        got = [mat[pl.ds(takes_at[0, g * 8 + s], 1)] for s in range(8)]
        for s in range(8):
            eight[pl.ds(s, 1)] = got[s]

    last = pltpu.make_async_copy(moved, moved_out, sem.at[TILES + 2])
    last.start()
    copies.append(last)
    for copy in copies:
        copy.wait()


def body(matrix, pivots, l_inverse):
    rows, cols = matrix.shape
    nb = l_inverse.shape[0]
    f32, bf16, i32 = jnp.float32, jnp.bfloat16, jnp.int32
    vmem = pl.BlockSpec(memory_space=pltpu.VMEM)
    hbm = pl.BlockSpec(memory_space=pltpu.HBM)
    shape = jax.ShapeDtypeStruct
    stay = lambda array: pltpu.with_memory_space_constraint(array, pltpu.HBM)
    work, u_rows, takes = pl.pallas_call(
        move_kernel,
        out_shape=(shape((rows + 8, cols), f32), shape((nb, cols), f32), shape((1, nb), i32)),
        in_specs=[hbm] * 3,
        out_specs=[vmem] * 3,
        scratch_shapes=[
            pltpu.VMEM((rows, nb), bf16),
            pltpu.VMEM((nb, cols), f32),
            pltpu.VMEM((nb, cols), f32),
            pltpu.VMEM((nb, cols), f32),
            pltpu.VMEM((nb // 2, cols), f32),
            pltpu.VMEM((nb, 1), f32),
            pltpu.VMEM((nb, nb), f32),
            pltpu.VMEM((1, nb), i32),
            pltpu.VMEM((nb, cols), bf16),
            pltpu.VMEM((PARTS * nb, cols), bf16),
            pltpu.VMEM((1, nb), i32),
            pltpu.SMEM((1, nb), i32),
            pltpu.SemaphoreType.DMA((TILES + 3,)),
            pltpu.SemaphoreType.DMA((CHUNKS,)),
            pltpu.SemaphoreType.DMA((SLOTS,)),
            pltpu.SemaphoreType.DMA((3,)),
            pltpu.SemaphoreType.DMA((3,)),
        ],
        compiler_params=pltpu.CompilerParams(
            collective_id=0, has_side_effects=True, vmem_limit_bytes=MOVE_VMEM
        ),
        name="move",
    )(stay(pivots.reshape(1, nb)), stay(matrix), stay(l_inverse))
    return pl.pallas_call(
        finish_kernel,
        out_shape=(shape((rows, cols), f32), shape((nb, cols), f32), shape((nb, cols), f32)),
        in_specs=[vmem] * 3,
        out_specs=[hbm] * 3,
        scratch_shapes=[
            pltpu.VMEM((nb, cols), f32),
            pltpu.SMEM((1, nb), i32),
            pltpu.SemaphoreType.DMA((TILES + 3,)),
        ],
        compiler_params=pltpu.CompilerParams(vmem_limit_bytes=FINISH_VMEM),
        name="finish",
    )(work, u_rows, takes)


def solution(mesh):
    return jax.shard_map(
        body,
        mesh=mesh,
        in_specs=(P("row", "col"), P(), P()),
        out_specs=(P("row", "col"), P(None, "col"), P("row", "col")),
        check_vma=False,
    )
```

```python
import jax
import jax.numpy as jnp
from jax import lax
from jax.experimental import pallas as pl
from jax.experimental.pallas import tpu as pltpu
from jax.sharding import PartitionSpec as P

CHUNKS = 32
TILES = 8
SLOTS = 4
PARTS = 3
SIDES = 2
MOVE_VMEM = 24 * 2**20
FINISH_VMEM = 8 * 2**20
NZ = 8
NX = 4


def pick(cond, a, b):
    return jnp.where(cond, a, b)


def column(yh, z, x):
    return (yh * NZ + z) * NX + x


def tree(core, yh, z, x):
    first = core == 0
    root = (yh == 0) & (x == 0)
    flat = z == 0
    up = (z >= 1) & (z <= 3)
    down = (z == 6) | (z == 7)
    step = pick(up, z + 1, z - 1)
    a0 = pick(first, jnp.logical_not(root), root)
    v0 = (flat | up | down) & a0
    k0 = column(yh, pick(flat, 1, step), x)
    inplane = pick(first, flat, jnp.logical_not(flat))
    zlow = flat & a0
    s1x = inplane & (x <= 1)
    v1 = s1x
    k1 = column(yh, z, x + 1)
    wrap = inplane & (x == 0)
    back = first & (yh == 0) & (x == 1) & jnp.logical_not(flat)
    drop = jnp.logical_not(first) & (z == 1) & jnp.logical_not(root)
    v2 = wrap | back
    k2 = column(yh, z, pick(wrap, 3, 0))
    cross = inplane & root
    v3 = cross | zlow | drop
    k3 = pick(cross, column(1, z, x), column(yh, pick(drop, 0, 7), x))
    kids = ((v0, k0), (v1, k1), (v2, k2), (v3, k3))
    zback = pick(z <= 4, z - 1, (z + 1) % NZ)
    px = pick(x == 2, 1, 0)
    inparent = pick(x == 0, column(0, z, 0), column(yh, z, px))
    p_first = pick(
        flat, inparent, pick(root, column(0, z, 1), column(yh, zback, x))
    )
    p_second = pick(
        root, column(0, zback, 0), pick(flat, column(yh, 1, x), inparent)
    )
    return kids, pick(first, p_first, p_second)


def place():
    r = lax.axis_index("row")
    c = lax.axis_index("col")
    return r, c, r % 2, r // 2, c // (NX * NZ), (c // NX) % NZ, c % NX


def hops(core, yh, z, x):
    dz = jnp.minimum(z, NZ - z)
    dx = jnp.minimum(x, NX - x)
    root = (yh == 0) & (x == 0)
    flat = z == 0
    around = pick(core == 0, root & jnp.logical_not(flat), flat & jnp.logical_not(root))
    return dz + dx + yh + pick(around, 2, 0)


def local_row(p, nb, row_count):
    shift = nb.bit_length() - 1
    deal = row_count.bit_length() - 1
    block = jnp.right_shift(p, shift)
    owner = block & (row_count - 1)
    local = jnp.left_shift(jnp.right_shift(block, deal), shift) + (p & (nb - 1))
    return owner, local


def move_kernel(
    row_hbm, mat_hbm, l_hbm, mat, u_ref, takes,
    panel, w_me, w_pair, m_far, comb, code, l_inverse, pivot_row, u_half, parts, from_row, from_at,
    in_sem, recv_sem, send_sem, x_send, x_recv,
):
    r, c, core, yl, yh, z, x = place()
    pair = yl * 2 + 1 - core
    far = (1 - yl) * 2 + core
    source = c == 0
    other = jnp.logical_not(source)
    kids, parent = tree(core, yh, z, x)
    rows, cols = mat_hbm.shape
    tile = rows // TILES
    chunk = rows // CHUNKS
    per = CHUNKS // TILES
    nb, width = l_hbm.shape
    half = nb // 2
    side = cols // SIDES
    row_count = lax.axis_size("row")

    def load(t):
        at = pl.ds(pl.multiple_of(t * tile, tile), tile)
        return pltpu.make_async_copy(mat_hbm.at[at], mat.at[at], in_sem.at[t])

    def forward(j, k):
        at = pl.ds(pl.multiple_of(j * chunk, chunk), chunk)
        return pltpu.make_async_remote_copy(
            src_ref=panel.at[at],
            dst_ref=panel.at[at],
            send_sem=send_sem.at[k],
            recv_sem=recv_sem.at[j],
            device_id={"row": r, "col": kids[k][1]},
            device_id_type=pl.DeviceIdType.MESH,
        )

    def send(j):
        for k in range(SLOTS):
            @pl.when(kids[k][0])
            def _():
                forward(j, k).start()

    def swap(step, src, dst, to):
        return pltpu.make_async_remote_copy(
            src_ref=src, dst_ref=dst, send_sem=x_send.at[step], recv_sem=x_recv.at[step],
            device_id={"row": to, "col": c}, device_id_type=pl.DeviceIdType.MESH,
        )

    def signal(row, col):
        pl.semaphore_signal(
            barrier, inc=1, device_id={"row": row, "col": col}, device_id_type=pl.DeviceIdType.MESH
        )

    mine = pl.ds(pl.multiple_of(core * half, half), half)
    with_pair = swap(0, w_me, w_pair, pair)
    across = swap(1, comb, m_far.at[mine], far)
    pass_on = swap(2, m_far.at[mine], m_far.at[mine], pair)

    barrier = pltpu.get_barrier_semaphore()

    @pl.when(other)
    def _():
        signal(r, parent)

    signal(pair, c)
    signal(far, c)
    load_p = pltpu.make_async_copy(row_hbm, pivot_row, in_sem.at[TILES])
    give_p = pltpu.make_async_copy(from_row, from_at, in_sem.at[TILES + 1])
    load_l = pltpu.make_async_copy(l_hbm, l_inverse, in_sem.at[TILES + 2])
    load_p.start()
    load(0).start()
    for t in range(1, TILES):
        load(t).start()
    load_l.start()

    load_p.wait()
    owner, local = local_row(pivot_row[...], nb, row_count)
    from_row[...] = jnp.where(owner == r, local, lax.broadcasted_iota(jnp.int32, (1, nb), 1))
    takes[...] = jnp.where((owner == r) & (pivot_row[...] >= nb), local, rows)
    mat[pl.ds(rows, 8)] = jnp.zeros((8, cols), mat.dtype)
    kind = jnp.where(owner == r, 0.0, jnp.where(owner == pair, 1.0, 2.0))
    down = lax.broadcasted_iota(jnp.int32, (nb, nb), 0)
    along = lax.broadcasted_iota(jnp.int32, (nb, nb), 1)
    spread = jnp.where(down == along, jnp.broadcast_to(kind, (nb, nb)), 0.0)
    code[...] = jnp.sum(spread, axis=1, keepdims=True)
    give_p.start()

    expect = 2
    for k in range(SLOTS):
        expect = expect + kids[k][0].astype(jnp.int32)
    pl.semaphore_wait(barrier, expect)

    @pl.when(source)
    def _():
        @pl.loop(0, TILES)
        def _(t):
            load(t).wait()
            at = pl.ds(pl.multiple_of(t * tile, tile), tile)
            panel[at] = mat[at, :width].astype(panel.dtype)
            for s in range(per):
                send(t * per + s)

    @pl.when(other)
    def _():
        @pl.loop(0, TILES)
        def _(t):
            load(t).wait()

    give_p.wait()

    @pl.loop(0, nb // 8)
    def _(g):
        out = w_me.at[pl.ds(pl.multiple_of(g * 8, 8), 8)]
        got = [mat[pl.ds(from_at[0, g * 8 + s], 1)] for s in range(8)]
        for s in range(8):
            out[pl.ds(s, 1)] = got[s]

    with_pair.start()

    def step_across():
        with_pair.wait_recv()
        kind = code[mine]
        from_pair = (kind > 0.5) & (kind < jnp.where(core == 1, 9.0, 1.5))
        comb[...] = jnp.where(from_pair, w_pair[mine], w_me[mine])
        across.start()

    def step_pass():
        across.wait_recv()
        pass_on.start()

    def step_wait():
        load_l.wait()
        pass_on.wait_recv()

    def step_u(h):
        at = pl.ds(pl.multiple_of(h * side, side), side)
        kind = code[...]
        picked = jnp.where(kind < 0.5, w_me[:, at], jnp.where(kind < 1.5, w_pair[:, at], m_far[:, at]))
        u = jnp.dot(
            l_inverse[...], picked, precision=lax.Precision.HIGHEST, preferred_element_type=jnp.float32
        )
        u_ref[:, at] = u
        u_half[:, at] = u.astype(u_half.dtype)

    def step_split(h):
        at = pl.ds(pl.multiple_of(h * side, side), side)
        whole = jnp.where(
            r == 0, mat[pl.ds(0, nb), at], jnp.where(r == 1, w_pair[:, at], m_far[:, at])
        )
        whole = jnp.where(source & (h * side < width), w_me[:, at], whole)
        edge = float(jnp.finfo(jnp.bfloat16).max)
        for p in range(PARTS):
            part = jnp.clip(whole, -edge, edge).astype(jnp.bfloat16)
            parts[pl.ds(p * nb, nb), at] = part
            whole = whole - part.astype(jnp.float32)

    def step_swap(t):
        at = pl.ds(pl.multiple_of(t * tile, tile), tile)
        index = lax.broadcasted_iota(jnp.int32, (tile, nb), 0) + t * tile
        onehot = jnp.where(index == takes[...], 1.0, 0.0)
        hit = jnp.max(onehot, axis=1, keepdims=True) > 0.5
        onehot = onehot.astype(jnp.bfloat16)
        rows_in = jnp.dot(
            jnp.concatenate([onehot] * PARTS, axis=1), parts[...], preferred_element_type=jnp.float32
        )
        mat[at] = jnp.where(hit, rows_in, mat[at])

    def update(j, size):
        at = pl.ds(pl.multiple_of(j * size, size), size)
        is_top = (r == 0) & (j < nb // size)

        @pl.when(is_top & other)
        def _():
            mat[at] = u_ref[pl.ds(pl.multiple_of((j % (nb // size)) * size, size), size)]

        @pl.when(is_top & source)
        def _():
            mat[at, width:] = u_ref[pl.ds(pl.multiple_of((j % (nb // size)) * size, size), size), width:]

        @pl.when(jnp.logical_not(is_top) & other)
        def _():
            mat[at] = mat[at] - jnp.dot(panel[at], u_half[...], preferred_element_type=jnp.float32)

        @pl.when(jnp.logical_not(is_top) & source)
        def _():
            mat[at, width:] = mat[at, width:] - jnp.dot(
                panel[at], u_half[:, width:], preferred_element_type=jnp.float32
            )

    depth = hops(core, yh, z, x)
    scale = CHUNKS // 8
    gap = (scale * 3) // 2
    late = (yh == 1) & (x == 0) & (z == 0)
    compact = (expect == 2) & jnp.logical_not(late)
    spread_out = jnp.logical_not(compact)
    late_go = pick(core == 0, CHUNKS - scale // 2, scale * 5)
    at_across = pick(late, late_go, pick((depth <= 1) & other, scale, 0))
    at_pass = pick(late, pick(core == 0, CHUNKS, late_go + 1), jnp.maximum(0, gap * (5 - depth) + 1))
    at_u = pick(late, at_pass + 1, pick(depth >= 6, 0, gap * (6 - depth) + 1))
    at_across = pick(source, 0, at_across)
    at_pass = pick(source, 1, at_pass)
    at_u = pick(source, 2, at_u)
    split_at = 4 * SIDES
    swap_at = split_at + 2 * SIDES
    steps = swap_at + 2 * TILES

    @pl.when(compact)
    def _():
        step_across()
        step_pass()
        step_wait()

        @pl.loop(0, SIDES)
        def _(h):
            step_u(h)
            step_split(h)

        @pl.loop(0, TILES)
        def _(t):
            step_swap(t)

    @pl.loop(0, pick(compact, CHUNKS, jnp.maximum(CHUNKS, at_u + steps)))
    def _(j):
        pl.when(spread_out & (j == at_across))(step_across)
        pl.when(spread_out & (j == at_pass))(step_pass)

        @pl.when((j < CHUNKS) & other)
        def _():
            forward(j, 0).wait_recv()
            send(j)

        @pl.when(compact)
        def _():
            update(j, chunk)

        q = j - at_u
        pl.when(spread_out & (q == 0))(step_wait)

        @pl.when(spread_out & (q >= 0) & (q < split_at) & (q % 4 == 0))
        def _():
            step_u(q // 4)

        @pl.when(spread_out & (q >= split_at) & (q < swap_at) & (q % 2 == 0))
        def _():
            step_split((q - split_at) // 2)

        @pl.when(spread_out & (q >= swap_at) & (q < steps) & (q % 2 == 0))
        def _():
            step_swap((q - swap_at) // 2)

    @pl.when(spread_out)
    def _():
        @pl.loop(0, TILES)
        def _(t):
            update(t, tile)

    with_pair.wait_send()
    across.wait_send()
    pass_on.wait_send()
    for k in range(SLOTS):
        @pl.when(kids[k][0])
        def _():
            pltpu.make_async_remote_copy(
                src_ref=panel, dst_ref=panel, send_sem=send_sem.at[k], recv_sem=recv_sem.at[0],
                device_id={"row": r, "col": kids[k][1]}, device_id_type=pl.DeviceIdType.MESH,
            ).wait_send()


def finish_kernel(mat, u_ref, takes, out, u_out, moved_out, moved, takes_at, sem):
    rows = out.shape[0]
    tile = rows // TILES
    nb = u_ref.shape[0]
    give_t = pltpu.make_async_copy(takes, takes_at, sem.at[TILES])
    give_t.start()
    copies = [
        pltpu.make_async_copy(mat.at[pl.ds(t * tile, tile)], out.at[pl.ds(t * tile, tile)], sem.at[t])
        for t in range(TILES)
    ]
    copies.append(pltpu.make_async_copy(u_ref, u_out, sem.at[TILES + 1]))
    for copy in copies:
        copy.start()
    give_t.wait()

    @pl.loop(0, nb // 8)
    def _(g):
        eight = moved.at[pl.ds(pl.multiple_of(g * 8, 8), 8)]
        got = [mat[pl.ds(takes_at[0, g * 8 + s], 1)] for s in range(8)]
        for s in range(8):
            eight[pl.ds(s, 1)] = got[s]

    last = pltpu.make_async_copy(moved, moved_out, sem.at[TILES + 2])
    last.start()
    copies.append(last)
    for copy in copies:
        copy.wait()


def body(matrix, pivots, l_inverse):
    rows, cols = matrix.shape
    nb = l_inverse.shape[0]
    f32, bf16, i32 = jnp.float32, jnp.bfloat16, jnp.int32
    vmem = pl.BlockSpec(memory_space=pltpu.VMEM)
    hbm = pl.BlockSpec(memory_space=pltpu.HBM)
    shape = jax.ShapeDtypeStruct
    stay = lambda array: pltpu.with_memory_space_constraint(array, pltpu.HBM)
    work, u_rows, takes = pl.pallas_call(
        move_kernel,
        out_shape=(shape((rows + 8, cols), f32), shape((nb, cols), f32), shape((1, nb), i32)),
        in_specs=[hbm] * 3,
        out_specs=[vmem] * 3,
        scratch_shapes=[
            pltpu.VMEM((rows, nb), bf16),
            pltpu.VMEM((nb, cols), f32),
            pltpu.VMEM((nb, cols), f32),
            pltpu.VMEM((nb, cols), f32),
            pltpu.VMEM((nb // 2, cols), f32),
            pltpu.VMEM((nb, 1), f32),
            pltpu.VMEM((nb, nb), f32),
            pltpu.VMEM((1, nb), i32),
            pltpu.VMEM((nb, cols), bf16),
            pltpu.VMEM((PARTS * nb, cols), bf16),
            pltpu.VMEM((1, nb), i32),
            pltpu.SMEM((1, nb), i32),
            pltpu.SemaphoreType.DMA((TILES + 3,)),
            pltpu.SemaphoreType.DMA((CHUNKS,)),
            pltpu.SemaphoreType.DMA((SLOTS,)),
            pltpu.SemaphoreType.DMA((3,)),
            pltpu.SemaphoreType.DMA((3,)),
        ],
        compiler_params=pltpu.CompilerParams(
            collective_id=0, has_side_effects=True, vmem_limit_bytes=MOVE_VMEM
        ),
        name="move",
    )(stay(pivots.reshape(1, nb)), stay(matrix), stay(l_inverse))
    return pl.pallas_call(
        finish_kernel,
        out_shape=(shape((rows, cols), f32), shape((nb, cols), f32), shape((nb, cols), f32)),
        in_specs=[vmem] * 3,
        out_specs=[hbm] * 3,
        scratch_shapes=[
            pltpu.VMEM((nb, cols), f32),
            pltpu.SMEM((1, nb), i32),
            pltpu.SemaphoreType.DMA((TILES + 3,)),
        ],
        compiler_params=pltpu.CompilerParams(vmem_limit_bytes=FINISH_VMEM),
        name="finish",
    )(work, u_rows, takes)


def solution(mesh):
    return jax.shard_map(
        body,
        mesh=mesh,
        in_specs=(P("row", "col"), P(), P()),
        out_specs=(P("row", "col"), P(None, "col"), P("row", "col")),
        check_vma=False,
    )
```

```python
import jax
import jax.numpy as jnp
from jax import lax
from jax.experimental import pallas as pl
from jax.experimental.pallas import tpu as pltpu
from jax.sharding import PartitionSpec as P

CHUNKS = 32
TILES = 8
SLOTS = 4
PARTS = 3
SIDES = 2
MOVE_VMEM = 24 * 2**20
FINISH_VMEM = 8 * 2**20
NZ = 8
NX = 4


def pick(cond, a, b):
    return jnp.where(cond, a, b)


def column(yh, z, x):
    return (yh * NZ + z) * NX + x


def tree(core, yh, z, x):
    first = core == 0
    root = (yh == 0) & (x == 0)
    flat = z == 0
    up = (z >= 1) & (z <= 3)
    down = (z == 6) | (z == 7)
    step = pick(up, z + 1, z - 1)
    a0 = pick(first, jnp.logical_not(root), root)
    v0 = (flat | up | down) & a0
    k0 = column(yh, pick(flat, 1, step), x)
    inplane = pick(first, flat, jnp.logical_not(flat))
    zlow = flat & a0
    s1x = inplane & (x <= 1)
    v1 = s1x
    k1 = column(yh, z, x + 1)
    wrap = inplane & (x == 0)
    back = first & (yh == 0) & (x == 1) & jnp.logical_not(flat)
    drop = jnp.logical_not(first) & (z == 1) & jnp.logical_not(root)
    v2 = wrap | back
    k2 = column(yh, z, pick(wrap, 3, 0))
    cross = inplane & root
    v3 = cross | zlow | drop
    k3 = pick(cross, column(1, z, x), column(yh, pick(drop, 0, 7), x))
    kids = ((v0, k0), (v1, k1), (v2, k2), (v3, k3))
    zback = pick(z <= 4, z - 1, (z + 1) % NZ)
    px = pick(x == 2, 1, 0)
    inparent = pick(x == 0, column(0, z, 0), column(yh, z, px))
    p_first = pick(
        flat, inparent, pick(root, column(0, z, 1), column(yh, zback, x))
    )
    p_second = pick(
        root, column(0, zback, 0), pick(flat, column(yh, 1, x), inparent)
    )
    return kids, pick(first, p_first, p_second)


def place():
    r = lax.axis_index("row")
    c = lax.axis_index("col")
    return r, c, r % 2, r // 2, c // (NX * NZ), (c // NX) % NZ, c % NX


def hops(core, yh, z, x):
    dz = jnp.minimum(z, NZ - z)
    dx = jnp.minimum(x, NX - x)
    root = (yh == 0) & (x == 0)
    flat = z == 0
    around = pick(core == 0, root & jnp.logical_not(flat), flat & jnp.logical_not(root))
    return dz + dx + yh + pick(around, 2, 0)


def local_row(p, nb, row_count):
    shift = nb.bit_length() - 1
    deal = row_count.bit_length() - 1
    block = jnp.right_shift(p, shift)
    owner = block & (row_count - 1)
    local = jnp.left_shift(jnp.right_shift(block, deal), shift) + (p & (nb - 1))
    return owner, local


def move_kernel(
    row_hbm, mat_hbm, l_hbm, mat, u_ref, takes,
    panel, w_me, w_pair, m_far, comb, code, l_inverse, pivot_row, u_half, parts, from_row, from_at,
    in_sem, recv_sem, send_sem, x_send, x_recv,
):
    r, c, core, yl, yh, z, x = place()
    pair = yl * 2 + 1 - core
    far = (1 - yl) * 2 + core
    source = c == 0
    other = jnp.logical_not(source)
    kids, parent = tree(core, yh, z, x)
    rows, cols = mat_hbm.shape
    tile = rows // TILES
    chunk = rows // CHUNKS
    per = CHUNKS // TILES
    nb, width = l_hbm.shape
    half = nb // 2
    side = cols // SIDES
    row_count = lax.axis_size("row")

    def load(t):
        at = pl.ds(pl.multiple_of(t * tile, tile), tile)
        return pltpu.make_async_copy(mat_hbm.at[at], mat.at[at], in_sem.at[t])

    def forward(j, k):
        at = pl.ds(pl.multiple_of(j * chunk, chunk), chunk)
        return pltpu.make_async_remote_copy(
            src_ref=panel.at[at],
            dst_ref=panel.at[at],
            send_sem=send_sem.at[k],
            recv_sem=recv_sem.at[j],
            device_id={"row": r, "col": kids[k][1]},
            device_id_type=pl.DeviceIdType.MESH,
        )

    def send(j):
        for k in range(SLOTS):
            @pl.when(kids[k][0])
            def _():
                forward(j, k).start()

    def swap(step, src, dst, to):
        return pltpu.make_async_remote_copy(
            src_ref=src, dst_ref=dst, send_sem=x_send.at[step], recv_sem=x_recv.at[step],
            device_id={"row": to, "col": c}, device_id_type=pl.DeviceIdType.MESH,
        )

    def signal(row, col):
        pl.semaphore_signal(
            barrier, inc=1, device_id={"row": row, "col": col}, device_id_type=pl.DeviceIdType.MESH
        )

    mine = pl.ds(pl.multiple_of(core * half, half), half)
    with_pair = swap(0, w_me, w_pair, pair)
    across = swap(1, comb, m_far.at[mine], far)
    pass_on = swap(2, m_far.at[mine], m_far.at[mine], pair)

    barrier = pltpu.get_barrier_semaphore()

    @pl.when(other)
    def _():
        signal(r, parent)

    signal(pair, c)
    signal(far, c)
    load_p = pltpu.make_async_copy(row_hbm, pivot_row, in_sem.at[TILES])
    give_p = pltpu.make_async_copy(from_row, from_at, in_sem.at[TILES + 1])
    load_l = pltpu.make_async_copy(l_hbm, l_inverse, in_sem.at[TILES + 2])
    load_p.start()
    load(0).start()
    for t in range(1, TILES):
        load(t).start()
    load_l.start()

    load_p.wait()
    owner, local = local_row(pivot_row[...], nb, row_count)
    from_row[...] = jnp.where(owner == r, local, lax.broadcasted_iota(jnp.int32, (1, nb), 1))
    takes[...] = jnp.where((owner == r) & (pivot_row[...] >= nb), local, rows)
    mat[pl.ds(rows, 8)] = jnp.zeros((8, cols), mat.dtype)
    kind = jnp.where(owner == r, 0.0, jnp.where(owner == pair, 1.0, 2.0))
    down = lax.broadcasted_iota(jnp.int32, (nb, nb), 0)
    along = lax.broadcasted_iota(jnp.int32, (nb, nb), 1)
    spread = jnp.where(down == along, jnp.broadcast_to(kind, (nb, nb)), 0.0)
    code[...] = jnp.sum(spread, axis=1, keepdims=True)
    give_p.start()

    expect = 2
    for k in range(SLOTS):
        expect = expect + kids[k][0].astype(jnp.int32)
    pl.semaphore_wait(barrier, expect)

    @pl.when(source)
    def _():
        @pl.loop(0, TILES)
        def _(t):
            load(t).wait()
            at = pl.ds(pl.multiple_of(t * tile, tile), tile)
            panel[at] = mat[at, :width].astype(panel.dtype)
            for s in range(per):
                send(t * per + s)

    @pl.when(other)
    def _():
        @pl.loop(0, TILES)
        def _(t):
            load(t).wait()

    give_p.wait()

    @pl.loop(0, nb // 8)
    def _(g):
        out = w_me.at[pl.ds(pl.multiple_of(g * 8, 8), 8)]
        got = [mat[pl.ds(from_at[0, g * 8 + s], 1)] for s in range(8)]
        for s in range(8):
            out[pl.ds(s, 1)] = got[s]

    with_pair.start()

    def sent():
        for k in range(SLOTS):
            @pl.when(kids[k][0])
            def _():
                pltpu.make_async_remote_copy(
                    src_ref=panel, dst_ref=panel, send_sem=send_sem.at[k], recv_sem=recv_sem.at[0],
                    device_id={"row": r, "col": kids[k][1]}, device_id_type=pl.DeviceIdType.MESH,
                ).wait_send()

    def step_across():
        with_pair.wait_recv()
        kind = code[mine]
        from_pair = (kind > 0.5) & (kind < jnp.where(core == 1, 9.0, 1.5))
        comb[...] = jnp.where(from_pair, w_pair[mine], w_me[mine])
        across.start()

    def step_pass():
        across.wait_recv()
        pass_on.start()

    def step_wait():
        load_l.wait()
        pass_on.wait_recv()

    def step_u(h):
        at = pl.ds(pl.multiple_of(h * side, side), side)
        kind = code[...]
        picked = jnp.where(kind < 0.5, w_me[:, at], jnp.where(kind < 1.5, w_pair[:, at], m_far[:, at]))
        u = jnp.dot(
            l_inverse[...], picked, precision=lax.Precision.HIGHEST, preferred_element_type=jnp.float32
        )
        u_ref[:, at] = u
        u_half[:, at] = u.astype(u_half.dtype)

    def step_split(h):
        at = pl.ds(pl.multiple_of(h * side, side), side)
        whole = jnp.where(
            r == 0, mat[pl.ds(0, nb), at], jnp.where(r == 1, w_pair[:, at], m_far[:, at])
        )
        whole = jnp.where(source & (h * side < width), w_me[:, at], whole)
        edge = float(jnp.finfo(jnp.bfloat16).max)
        for p in range(PARTS):
            part = jnp.clip(whole, -edge, edge).astype(jnp.bfloat16)
            parts[pl.ds(p * nb, nb), at] = part
            whole = whole - part.astype(jnp.float32)

    def step_swap(t):
        at = pl.ds(pl.multiple_of(t * tile, tile), tile)
        index = lax.broadcasted_iota(jnp.int32, (tile, nb), 0) + t * tile
        onehot = jnp.where(index == takes[...], 1.0, 0.0)
        hit = jnp.max(onehot, axis=1, keepdims=True) > 0.5
        onehot = onehot.astype(jnp.bfloat16)
        rows_in = jnp.dot(
            jnp.concatenate([onehot] * PARTS, axis=1), parts[...], preferred_element_type=jnp.float32
        )
        mat[at] = jnp.where(hit, rows_in, mat[at])

    def update(j, size):
        at = pl.ds(pl.multiple_of(j * size, size), size)
        is_top = (r == 0) & (j < nb // size)

        @pl.when(is_top & other)
        def _():
            mat[at] = u_ref[pl.ds(pl.multiple_of((j % (nb // size)) * size, size), size)]

        @pl.when(is_top & source)
        def _():
            mat[at, width:] = u_ref[pl.ds(pl.multiple_of((j % (nb // size)) * size, size), size), width:]

        @pl.when(jnp.logical_not(is_top) & other)
        def _():
            mat[at] = mat[at] - jnp.dot(panel[at], u_half[...], preferred_element_type=jnp.float32)

        @pl.when(jnp.logical_not(is_top) & source)
        def _():
            mat[at, width:] = mat[at, width:] - jnp.dot(
                panel[at], u_half[:, width:], preferred_element_type=jnp.float32
            )

    depth = hops(core, yh, z, x)
    scale = CHUNKS // 8
    gap = (scale * 3) // 2
    compact = expect == 2
    arrive = compact & (depth >= 6)
    spread_out = jnp.logical_not(compact)
    at_across = pick(depth <= 1, scale, 0)
    at_pass = jnp.maximum(0, gap * (5 - depth) + 1)
    at_u = pick(depth >= 6, 0, gap * (6 - depth) + 1)
    at_across = pick(source, 0, at_across)
    at_pass = pick(source, 1, at_pass)
    at_u = pick(source, 2, at_u)
    split_at = 4 * SIDES
    swap_at = split_at + 2 * SIDES
    steps = swap_at + 2 * TILES

    pl.when(source)(sent)

    @pl.when(compact)
    def _():
        step_across()
        step_pass()
        step_wait()

        @pl.loop(0, SIDES)
        def _(h):
            step_u(h)
            step_split(h)

        @pl.loop(0, TILES)
        def _(t):
            step_swap(t)

    @pl.loop(0, pick(compact, CHUNKS, jnp.maximum(CHUNKS, at_u + steps)))
    def _(j):
        pl.when(spread_out & (j == at_across))(step_across)
        pl.when(spread_out & (j == at_pass))(step_pass)

        @pl.when((j < CHUNKS) & other)
        def _():
            forward(j, 0).wait_recv()
            send(j)

        @pl.when(arrive)
        def _():
            update(j, chunk)

        q = j - at_u
        pl.when(spread_out & (q == 0))(step_wait)

        @pl.when(spread_out & (q >= 0) & (q < split_at) & (q % 4 == 0))
        def _():
            step_u(q // 4)

        @pl.when(spread_out & (q >= split_at) & (q < swap_at) & (q % 2 == 0))
        def _():
            step_split((q - split_at) // 2)

        @pl.when(spread_out & (q >= swap_at) & (q < steps) & (q % 2 == 0))
        def _():
            step_swap((q - swap_at) // 2)

    @pl.when(jnp.logical_not(arrive))
    def _():
        @pl.loop(0, TILES)
        def _(t):
            update(t, tile)

    with_pair.wait_send()
    across.wait_send()
    pass_on.wait_send()
    pl.when(other)(sent)


def finish_kernel(mat, u_ref, takes, out, u_out, moved_out, moved, takes_at, sem):
    rows = out.shape[0]
    tile = rows // TILES
    nb = u_ref.shape[0]
    give_t = pltpu.make_async_copy(takes, takes_at, sem.at[TILES])
    give_t.start()
    copies = [
        pltpu.make_async_copy(mat.at[pl.ds(t * tile, tile)], out.at[pl.ds(t * tile, tile)], sem.at[t])
        for t in range(TILES)
    ]
    copies.append(pltpu.make_async_copy(u_ref, u_out, sem.at[TILES + 1]))
    for copy in copies:
        copy.start()
    give_t.wait()

    @pl.loop(0, nb // 8)
    def _(g):
        eight = moved.at[pl.ds(pl.multiple_of(g * 8, 8), 8)]
        got = [mat[pl.ds(takes_at[0, g * 8 + s], 1)] for s in range(8)]
        for s in range(8):
            eight[pl.ds(s, 1)] = got[s]

    last = pltpu.make_async_copy(moved, moved_out, sem.at[TILES + 2])
    last.start()
    copies.append(last)
    for copy in copies:
        copy.wait()


def body(matrix, pivots, l_inverse):
    rows, cols = matrix.shape
    nb = l_inverse.shape[0]
    f32, bf16, i32 = jnp.float32, jnp.bfloat16, jnp.int32
    vmem = pl.BlockSpec(memory_space=pltpu.VMEM)
    hbm = pl.BlockSpec(memory_space=pltpu.HBM)
    shape = jax.ShapeDtypeStruct
    stay = lambda array: pltpu.with_memory_space_constraint(array, pltpu.HBM)
    work, u_rows, takes = pl.pallas_call(
        move_kernel,
        out_shape=(shape((rows + 8, cols), f32), shape((nb, cols), f32), shape((1, nb), i32)),
        in_specs=[hbm] * 3,
        out_specs=[vmem] * 3,
        scratch_shapes=[
            pltpu.VMEM((rows, nb), bf16),
            pltpu.VMEM((nb, cols), f32),
            pltpu.VMEM((nb, cols), f32),
            pltpu.VMEM((nb, cols), f32),
            pltpu.VMEM((nb // 2, cols), f32),
            pltpu.VMEM((nb, 1), f32),
            pltpu.VMEM((nb, nb), f32),
            pltpu.VMEM((1, nb), i32),
            pltpu.VMEM((nb, cols), bf16),
            pltpu.VMEM((PARTS * nb, cols), bf16),
            pltpu.VMEM((1, nb), i32),
            pltpu.SMEM((1, nb), i32),
            pltpu.SemaphoreType.DMA((TILES + 3,)),
            pltpu.SemaphoreType.DMA((CHUNKS,)),
            pltpu.SemaphoreType.DMA((SLOTS,)),
            pltpu.SemaphoreType.DMA((3,)),
            pltpu.SemaphoreType.DMA((3,)),
        ],
        compiler_params=pltpu.CompilerParams(
            collective_id=0, has_side_effects=True, vmem_limit_bytes=MOVE_VMEM
        ),
        name="move",
    )(stay(pivots.reshape(1, nb)), stay(matrix), stay(l_inverse))
    return pl.pallas_call(
        finish_kernel,
        out_shape=(shape((rows, cols), f32), shape((nb, cols), f32), shape((nb, cols), f32)),
        in_specs=[vmem] * 3,
        out_specs=[hbm] * 3,
        scratch_shapes=[
            pltpu.VMEM((nb, cols), f32),
            pltpu.SMEM((1, nb), i32),
            pltpu.SemaphoreType.DMA((TILES + 3,)),
        ],
        compiler_params=pltpu.CompilerParams(vmem_limit_bytes=FINISH_VMEM),
        name="finish",
    )(work, u_rows, takes)


def solution(mesh):
    return jax.shard_map(
        body,
        mesh=mesh,
        in_specs=(P("row", "col"), P(), P()),
        out_specs=(P("row", "col"), P(None, "col"), P("row", "col")),
        check_vma=False,
    )
```

```python
import jax
import jax.numpy as jnp
from jax import lax
from jax.experimental import pallas as pl
from jax.experimental.pallas import tpu as pltpu
from jax.sharding import PartitionSpec as P

CHUNKS = 32
TILES = 8
SLOTS = 4
PARTS = 2
SIDES = 2
MOVE_VMEM = 24 * 2**20
FINISH_VMEM = 8 * 2**20
NZ = 8
NX = 4


def pick(cond, a, b):
    return jnp.where(cond, a, b)


def column(yh, z, x):
    return (yh * NZ + z) * NX + x


def tree(core, yh, z, x):
    first = core == 0
    second = jnp.logical_not(first)
    root = (yh == 0) & (x == 0)
    off = jnp.logical_not(root)
    flat = z == 0
    up = (z >= 1) & (z <= 3)
    down = (z == 6) | (z == 7)
    odd = (x % 2) == 1
    inplane = pick(first, flat, jnp.logical_not(flat))
    twin = first & ((x == 2) | ((yh == 1) & (x == 0)))
    only = pick(x == 1, 2, 3)
    along = pick(first, off, root)
    v0 = along & (flat | up | down | (twin & (z == 5)))
    k0 = column(yh, pick(flat, 1, pick(up, z + 1, z - 1)), x)
    c0 = pick(twin & (z == 3), 2, pick(twin & (z == 5), 3, 0))
    drop = second & (z == 1) & off
    v2 = (along & flat) | drop
    k2 = column(yh, pick(drop, 0, 7), x)
    c2 = pick(twin, 1, 0)
    back = first & jnp.logical_not(flat) & (yh == 0) & (x == 1)
    v1 = (inplane & jnp.logical_not((yh == 0) & (x == 2))) | back
    x1 = pick(odd, 2, pick(x == 2, 1, pick(yh == 0, 1, 3)))
    k1 = column(yh, z, pick(back, 0, x1))
    c1 = pick(back | root, 0, pick(odd, only, pick(x == 2, 3, 2)))
    v3 = inplane & (root | odd)
    k3 = pick(root, column(0, z, 3), pick(yh == 0, column(1, z, x), column(1, z, 0)))
    c3 = pick(root, pick(first, 1, 0), only)
    kids = ((v0, c0, k0), (v1, c1, k1), (v2, c2, k2), (v3, c3, k3))
    near = pick(z <= 4, z - 1, (z + 1) % NZ)
    in_a = pick(
        yh == 0,
        pick(odd, column(0, z, 0), column(0, z, 1)),
        pick(x == 1, column(0, z, 1), pick(x == 3, column(1, z, 0), column(1, z, 1))),
    )
    in_b = pick(
        yh == 0,
        pick(odd, column(0, z, 0), column(0, z, 3)),
        pick(x == 1, column(1, z, 2), pick(x == 3, column(0, z, 3), column(1, z, 3))),
    )
    chain_a = pick(root, column(0, z, 1), column(yh, near, x))
    chain_b = pick(twin & (z == 4), column(yh, 5, x), chain_a)
    stem = pick(root, column(0, near, 0), column(yh, 1, x))
    other_plane = pick(first, jnp.logical_not(flat), flat | root)
    parent_a = pick(other_plane, pick(first, chain_a, stem), in_a)
    parent_b = pick(other_plane, pick(first, chain_b, stem), in_b)
    beyond = z >= 5
    turn = pick(flat | (z == 4), 2, pick(beyond, 1, 0))
    side = (yh == 1) & (x == 3) & jnp.logical_not(flat)
    order = pick(first, pick(twin, turn, pick(x == 3, 1, 0)), pick(side, 2, 0))
    passes = (flat & root) | (twin & flat)
    return kids, parent_a, parent_b, order, passes


def start_time(core, yh, z, x):
    first = core == 0
    dz = jnp.minimum(z, NZ - z)
    flat = z == 0
    root = (yh == 0) & (x == 0)
    dx = pick(x % 2 == 1, 1, pick(root & (jnp.logical_not(first) | flat), 0, 2))
    dz = dz + pick(flat & jnp.logical_not(first) & jnp.logical_not(root), 2, 0)
    return (pick(first, 7, 5) * dx + pick(first, 6, 4) * dz + pick(first, 8, 6) * yh) * (CHUNKS // 32)


def place():
    r = lax.axis_index("row")
    c = lax.axis_index("col")
    return r, c, r % 2, r // 2, c // (NX * NZ), (c // NX) % NZ, c % NX


def local_row(p, nb, row_count):
    shift = nb.bit_length() - 1
    deal = row_count.bit_length() - 1
    block = jnp.right_shift(p, shift)
    owner = block & (row_count - 1)
    local = jnp.left_shift(jnp.right_shift(block, deal), shift) + (p & (nb - 1))
    return owner, local


def move_kernel(
    row_hbm, mat_hbm, l_hbm, mat, u_ref, takes,
    panel, w_me, w_pair, m_far, comb, code, l_inverse, pivot_row, u_half, parts, from_row, from_at,
    in_sem, recv_sem, send_sem, x_send, x_recv,
):
    r, c, core, yl, yh, z, x = place()
    pair = yl * 2 + 1 - core
    far = (1 - yl) * 2 + core
    source = c == 0
    other = jnp.logical_not(source)
    kids, parent_a, parent_b, order, passes = tree(core, yh, z, x)
    rows, cols = mat_hbm.shape
    tile = rows // TILES
    chunk = rows // CHUNKS
    per = CHUNKS // TILES
    nb, width = l_hbm.shape
    half = nb // 2
    side = cols // SIDES
    row_count = lax.axis_size("row")

    def load(t):
        at = pl.ds(pl.multiple_of(t * tile, tile), tile)
        return pltpu.make_async_copy(mat_hbm.at[at], mat.at[at], in_sem.at[t])

    split_point = CHUNKS // 2

    def turn(mode, j):
        late_first = pick(j < split_point, j + split_point, j - split_point)
        return pick(mode == 0, j, pick(mode == 1, late_first, j // 2 + (j % 2) * split_point))

    def forward(i, k):
        at = pl.ds(pl.multiple_of(i * chunk, chunk), chunk)
        return pltpu.make_async_remote_copy(
            src_ref=panel.at[at],
            dst_ref=panel.at[at],
            send_sem=send_sem.at[k],
            recv_sem=recv_sem.at[i],
            device_id={"row": r, "col": kids[k][2]},
            device_id_type=pl.DeviceIdType.MESH,
        )

    def send(i, second=False):
        head = i < split_point
        for k, (valid, kind, _) in enumerate(kids):
            match = jnp.logical_xor((kind % 2) == 1, head)
            both = kind < 2
            if second:
                go = both & jnp.logical_not(match)
            else:
                go = match | (both & jnp.logical_not(passes))

            @pl.when(valid & go)
            def _():
                forward(i, k).start()

    def swap(step, src, dst, to):
        return pltpu.make_async_remote_copy(
            src_ref=src, dst_ref=dst, send_sem=x_send.at[step], recv_sem=x_recv.at[step],
            device_id={"row": to, "col": c}, device_id_type=pl.DeviceIdType.MESH,
        )

    def signal(row, col):
        pl.semaphore_signal(
            barrier, inc=1, device_id={"row": row, "col": col}, device_id_type=pl.DeviceIdType.MESH
        )

    mine = pl.ds(pl.multiple_of(core * half, half), half)
    with_pair = swap(0, w_me, w_pair, pair)
    across = swap(1, comb, m_far.at[mine], far)
    pass_on = swap(2, m_far.at[mine], m_far.at[mine], pair)

    barrier = pltpu.get_barrier_semaphore()

    @pl.when(other)
    def _():
        signal(r, parent_a)

        @pl.when(parent_b != parent_a)
        def _():
            signal(r, parent_b)

    signal(pair, c)
    signal(far, c)
    load_p = pltpu.make_async_copy(row_hbm, pivot_row, in_sem.at[TILES])
    give_p = pltpu.make_async_copy(from_row, from_at, in_sem.at[TILES + 1])
    load_l = pltpu.make_async_copy(l_hbm, l_inverse, in_sem.at[TILES + 2])
    load_p.start()
    load(0).start()
    for t in range(1, TILES):
        load(t).start()
    load_l.start()

    load_p.wait()
    owner, local = local_row(pivot_row[...], nb, row_count)
    from_row[...] = jnp.where(owner == r, local, lax.broadcasted_iota(jnp.int32, (1, nb), 1))
    takes[...] = jnp.where((owner == r) & (pivot_row[...] >= nb), local, rows)
    mat[pl.ds(rows, 8)] = jnp.zeros((8, cols), mat.dtype)
    kind = jnp.where(owner == r, 0.0, jnp.where(owner == pair, 1.0, 2.0))
    down = lax.broadcasted_iota(jnp.int32, (nb, nb), 0)
    along = lax.broadcasted_iota(jnp.int32, (nb, nb), 1)
    spread = jnp.where(down == along, jnp.broadcast_to(kind, (nb, nb)), 0.0)
    code[...] = jnp.sum(spread, axis=1, keepdims=True)
    give_p.start()

    expect = 2
    for k in range(SLOTS):
        expect = expect + kids[k][0].astype(jnp.int32)
    pl.semaphore_wait(barrier, expect)

    @pl.when(source)
    def _():
        @pl.loop(0, TILES // 2)
        def _(t):
            for half_t in (t, t + TILES // 2):
                load(half_t).wait()
                at = pl.ds(pl.multiple_of(half_t * tile, tile), tile)
                panel[at] = mat[at, :width].astype(panel.dtype)

            @pl.loop(t * 2 * per, (t + 1) * 2 * per)
            def _(j):
                send(turn(2, j))

        @pl.loop(0, CHUNKS)
        def _(j):
            send(turn(2, j), second=True)

    @pl.when(other)
    def _():
        @pl.loop(0, TILES)
        def _(t):
            load(t).wait()

    give_p.wait()

    @pl.loop(0, nb // 8)
    def _(g):
        out = w_me.at[pl.ds(pl.multiple_of(g * 8, 8), 8)]
        got = [mat[pl.ds(from_at[0, g * 8 + s], 1)] for s in range(8)]
        for s in range(8):
            out[pl.ds(s, 1)] = got[s]

    with_pair.start()

    def sent():
        for k, (valid, kind, col) in enumerate(kids):
            for whole in (True, False):
                part = panel if whole else panel.at[pl.ds(0, rows // 2)]

                @pl.when(valid & ((kind < 2) == whole))
                def _():
                    pltpu.make_async_remote_copy(
                        src_ref=part, dst_ref=part, send_sem=send_sem.at[k], recv_sem=recv_sem.at[0],
                        device_id={"row": r, "col": col}, device_id_type=pl.DeviceIdType.MESH,
                    ).wait_send()

    def step_across():
        with_pair.wait_recv()
        kind = code[mine]
        from_pair = (kind > 0.5) & (kind < jnp.where(core == 1, 9.0, 1.5))
        comb[...] = jnp.where(from_pair, w_pair[mine], w_me[mine])
        across.start()

    def step_pass():
        across.wait_recv()
        pass_on.start()

    def step_wait():
        load_l.wait()
        pass_on.wait_recv()

    def step_u(h):
        at = pl.ds(pl.multiple_of(h * side, side), side)
        kind = code[...]
        picked = jnp.where(kind < 0.5, w_me[:, at], jnp.where(kind < 1.5, w_pair[:, at], m_far[:, at]))
        u = jnp.dot(
            l_inverse[...], picked, precision=lax.Precision.HIGHEST, preferred_element_type=jnp.float32
        )
        u_ref[:, at] = u
        u_half[:, at] = u.astype(u_half.dtype)

    def step_split(h):
        at = pl.ds(pl.multiple_of(h * side, side), side)
        whole = jnp.where(
            r == 0, mat[pl.ds(0, nb), at], jnp.where(r == 1, w_pair[:, at], m_far[:, at])
        )
        whole = jnp.where(source & (h * side < width), w_me[:, at], whole)
        edge = float(jnp.finfo(jnp.bfloat16).max)
        for p in range(PARTS):
            part = jnp.clip(whole, -edge, edge).astype(jnp.bfloat16)
            parts[pl.ds(p * nb, nb), at] = part
            whole = whole - part.astype(jnp.float32)

    def step_swap(t):
        at = pl.ds(pl.multiple_of(t * tile, tile), tile)
        index = lax.broadcasted_iota(jnp.int32, (tile, nb), 0) + t * tile
        onehot = jnp.where(index == takes[...], 1.0, 0.0)
        hit = jnp.max(onehot, axis=1, keepdims=True) > 0.5
        onehot = onehot.astype(jnp.bfloat16)
        rows_in = jnp.dot(
            jnp.concatenate([onehot] * PARTS, axis=1), parts[...], preferred_element_type=jnp.float32
        )
        mat[at] = jnp.where(hit, rows_in, mat[at])

    def update(j, size):
        at = pl.ds(pl.multiple_of(j * size, size), size)
        is_top = (r == 0) & (j < nb // size)

        @pl.when(is_top & other)
        def _():
            mat[at] = u_ref[pl.ds(pl.multiple_of((j % (nb // size)) * size, size), size)]

        @pl.when(is_top & source)
        def _():
            mat[at, width:] = u_ref[pl.ds(pl.multiple_of((j % (nb // size)) * size, size), size), width:]

        @pl.when(jnp.logical_not(is_top) & other)
        def _():
            mat[at] = mat[at] - jnp.dot(panel[at], u_half[...], preferred_element_type=jnp.float32)

        @pl.when(jnp.logical_not(is_top) & source)
        def _():
            mat[at, width:] = mat[at, width:] - jnp.dot(
                panel[at], u_half[:, width:], preferred_element_type=jnp.float32
            )

    came = start_time(core, yh, z, x)
    late = (yh == 0) & (z == 0) & (x % 2 == 1)
    compact = (expect == 2) & jnp.logical_not(late)
    spread_out = jnp.logical_not(compact)
    unit = CHUNKS // 32
    free_link = unit * 23
    swap_time = pick(late, free_link, unit * 11)
    at_across = jnp.maximum(0, swap_time - came)
    at_pass = jnp.maximum(0, pick(late, free_link + unit * 23, unit * 33) - came)
    last = pick(passes, 2 * CHUNKS, CHUNKS)
    settle = passes & other
    at_across = pick(source, 0, pick(settle, jnp.minimum(2 * at_across, last), at_across))
    at_pass = pick(source, 1, pick(settle, last, at_pass))
    at_u = pick(source, 2, pick(settle, last + 1, at_pass + unit * 6))
    split_at = 4 * SIDES
    swap_at = split_at + 2 * SIDES
    steps = swap_at + 2 * TILES

    @pl.when(compact)
    def _():
        step_across()
        step_pass()
        step_wait()

        @pl.loop(0, SIDES)
        def _(h):
            step_u(h)
            step_split(h)

        @pl.loop(0, TILES)
        def _(t):
            step_swap(t)

        group = CHUNKS // 4

        @pl.loop(0, 4)
        def _(g):
            @pl.loop(g * group, (g + 1) * group)
            def _(j):
                forward(turn(order, j), 0).wait_recv()

            one = pick(order == 0, 2 * g, pick(order == 1, (2 * g + TILES // 2) % TILES, g))
            update(one, tile)
            update(one + pick(order == 2, TILES // 2, 1), tile)

    @pl.when(spread_out)
    def _():
        @pl.loop(0, jnp.maximum(last, at_u + steps))
        def _(j):
            pl.when(j == at_across)(step_across)
            pl.when(j == at_pass)(step_pass)

            @pl.when((j < CHUNKS) & other)
            def _():
                i = turn(order, j)
                forward(i, 0).wait_recv()
                send(i)

            @pl.when(settle & (j >= CHUNKS) & (j < last))
            def _():
                send(turn(2, jnp.minimum(j - CHUNKS, CHUNKS - 1)), second=True)

            q = j - at_u
            pl.when(q == 0)(step_wait)

            @pl.when((q >= 0) & (q < split_at) & (q % 4 == 0))
            def _():
                step_u(q // 4)

            @pl.when((q >= split_at) & (q < swap_at) & (q % 2 == 0))
            def _():
                step_split((q - split_at) // 2)

            @pl.when((q >= swap_at) & (q < steps) & (q % 2 == 0))
            def _():
                step_swap((q - swap_at) // 2)

        @pl.loop(0, TILES)
        def _(t):
            update(t, tile)

    with_pair.wait_send()
    across.wait_send()
    pass_on.wait_send()
    sent()


def finish_kernel(mat, u_ref, takes, out, u_out, moved_out, moved, takes_at, sem):
    rows = out.shape[0]
    tile = rows // TILES
    nb = u_ref.shape[0]
    give_t = pltpu.make_async_copy(takes, takes_at, sem.at[TILES])
    give_t.start()
    copies = [
        pltpu.make_async_copy(mat.at[pl.ds(t * tile, tile)], out.at[pl.ds(t * tile, tile)], sem.at[t])
        for t in range(TILES)
    ]
    copies.append(pltpu.make_async_copy(u_ref, u_out, sem.at[TILES + 1]))
    for copy in copies:
        copy.start()
    give_t.wait()

    @pl.loop(0, nb // 8)
    def _(g):
        eight = moved.at[pl.ds(pl.multiple_of(g * 8, 8), 8)]
        got = [mat[pl.ds(takes_at[0, g * 8 + s], 1)] for s in range(8)]
        for s in range(8):
            eight[pl.ds(s, 1)] = got[s]

    last = pltpu.make_async_copy(moved, moved_out, sem.at[TILES + 2])
    last.start()
    copies.append(last)
    for copy in copies:
        copy.wait()


def body(matrix, pivots, l_inverse):
    rows, cols = matrix.shape
    nb = l_inverse.shape[0]
    f32, bf16, i32 = jnp.float32, jnp.bfloat16, jnp.int32
    vmem = pl.BlockSpec(memory_space=pltpu.VMEM)
    hbm = pl.BlockSpec(memory_space=pltpu.HBM)
    shape = jax.ShapeDtypeStruct
    stay = lambda array: pltpu.with_memory_space_constraint(array, pltpu.HBM)
    work, u_rows, takes = pl.pallas_call(
        move_kernel,
        out_shape=(shape((rows + 8, cols), f32), shape((nb, cols), f32), shape((1, nb), i32)),
        in_specs=[hbm] * 3,
        out_specs=[vmem] * 3,
        scratch_shapes=[
            pltpu.VMEM((rows, nb), bf16),
            pltpu.VMEM((nb, cols), f32),
            pltpu.VMEM((nb, cols), f32),
            pltpu.VMEM((nb, cols), f32),
            pltpu.VMEM((nb // 2, cols), f32),
            pltpu.VMEM((nb, 1), f32),
            pltpu.VMEM((nb, nb), f32),
            pltpu.VMEM((1, nb), i32),
            pltpu.VMEM((nb, cols), bf16),
            pltpu.VMEM((PARTS * nb, cols), bf16),
            pltpu.VMEM((1, nb), i32),
            pltpu.SMEM((1, nb), i32),
            pltpu.SemaphoreType.DMA((TILES + 3,)),
            pltpu.SemaphoreType.DMA((CHUNKS,)),
            pltpu.SemaphoreType.DMA((SLOTS,)),
            pltpu.SemaphoreType.DMA((3,)),
            pltpu.SemaphoreType.DMA((3,)),
        ],
        compiler_params=pltpu.CompilerParams(
            collective_id=0, has_side_effects=True, vmem_limit_bytes=MOVE_VMEM
        ),
        name="move",
    )(stay(pivots.reshape(1, nb)), stay(matrix), stay(l_inverse))
    return pl.pallas_call(
        finish_kernel,
        out_shape=(shape((rows, cols), f32), shape((nb, cols), f32), shape((nb, cols), f32)),
        in_specs=[vmem] * 3,
        out_specs=[hbm] * 3,
        scratch_shapes=[
            pltpu.VMEM((nb, cols), f32),
            pltpu.SMEM((1, nb), i32),
            pltpu.SemaphoreType.DMA((TILES + 3,)),
        ],
        compiler_params=pltpu.CompilerParams(vmem_limit_bytes=FINISH_VMEM),
        name="finish",
    )(work, u_rows, takes)


def solution(mesh):
    return jax.shard_map(
        body,
        mesh=mesh,
        in_specs=(P("row", "col"), P(), P()),
        out_specs=(P("row", "col"), P(None, "col"), P("row", "col")),
        check_vma=False,
    )
```

```python
import jax
import jax.numpy as jnp
from jax import lax
from jax.experimental import pallas as pl
from jax.experimental.pallas import tpu as pltpu
from jax.sharding import PartitionSpec as P

CHUNKS = 32
TILES = 8
SLOTS = 4
PARTS = 2
SIDES = 2
MOVE_VMEM = 24 * 2**20
FINISH_VMEM = 8 * 2**20
NZ = 8
NX = 4


def pick(cond, a, b):
    return jnp.where(cond, a, b)


def column(yh, z, x):
    return (yh * NZ + z) * NX + x


def tree(core, yh, z, x):
    first = core == 0
    second = jnp.logical_not(first)
    root = (yh == 0) & (x == 0)
    off = jnp.logical_not(root)
    flat = z == 0
    up = (z >= 1) & (z <= 3)
    down = (z == 6) | (z == 7)
    odd = (x % 2) == 1
    inplane = pick(first, flat, jnp.logical_not(flat))
    folded = inplane & (first | (z == 1) | (z == 7))
    plain = inplane & jnp.logical_not(folded)
    twin = first & ((x == 2) | ((yh == 1) & (x == 0)))
    only = pick(x == 1, 2, 3)
    along = pick(first, off, root)
    v0 = along & (flat | up | down | (twin & (z == 5)))
    k0 = column(yh, pick(flat, 1, pick(up, z + 1, z - 1)), x)
    c0 = pick(twin & (z == 3), 2, pick(twin & (z == 5), 3, 0))
    drop = second & (z == 1) & off
    over = plain & root
    v2 = (along & flat) | drop | over
    k2 = pick(over, column(1, z, 0), column(yh, pick(drop, 0, 7), x))
    c2 = pick(twin, 1, 0)
    back = first & jnp.logical_not(flat) & (yh == 0) & (x == 1)
    v1 = (folded & jnp.logical_not((yh == 0) & (x == 2))) | back | (plain & (x <= 1))
    x1 = pick(odd, 2, pick(x == 2, 1, pick(yh == 0, 1, 3)))
    k1 = column(yh, z, pick(back, 0, pick(plain, x + 1, x1)))
    c1 = pick(back | root | plain, 0, pick(odd, only, pick(x == 2, 3, 2)))
    v3 = (folded & (root | odd)) | (plain & (x == 0))
    k3 = pick(root | plain, column(yh, z, 3), pick(yh == 0, column(1, z, x), column(1, z, 0)))
    c3 = pick(root | plain, pick(first, 1, 0), only)
    kids = ((v0, c0, k0), (v1, c1, k1), (v2, c2, k2), (v3, c3, k3))
    near = pick(z <= 4, z - 1, (z + 1) % NZ)
    in_a = pick(
        yh == 0,
        pick(odd, column(0, z, 0), column(0, z, 1)),
        pick(x == 1, column(0, z, 1), pick(x == 3, column(1, z, 0), column(1, z, 1))),
    )
    in_b = pick(
        yh == 0,
        pick(odd, column(0, z, 0), column(0, z, 3)),
        pick(x == 1, column(1, z, 2), pick(x == 3, column(0, z, 3), column(1, z, 3))),
    )
    chain_a = pick(root, column(0, z, 1), column(yh, near, x))
    chain_b = pick(twin & (z == 4), column(yh, 5, x), chain_a)
    stem = pick(root, column(0, near, 0), column(yh, 1, x))
    other_plane = pick(first, jnp.logical_not(flat), flat | root)
    in_plain = pick(x == 2, column(yh, z, 1), pick(x == 0, column(0, z, 0), column(yh, z, 0)))
    parent_a = pick(other_plane, pick(first, chain_a, stem), pick(plain, in_plain, in_a))
    parent_b = pick(other_plane, pick(first, chain_b, stem), pick(plain, in_plain, in_b))
    beyond = z >= 5
    turn = pick(flat | (z == 4), 2, pick(beyond, 1, 0))
    side = (yh == 1) & (x == 3) & folded
    order = pick(first, pick(twin, turn, pick(x == 3, 1, 0)), pick(side, 2, 0))
    passes = (flat & root) | (twin & flat)
    return kids, parent_a, parent_b, order, passes


def start_time(core, yh, z, x):
    first = core == 0
    dz = jnp.minimum(z, NZ - z)
    flat = z == 0
    root = (yh == 0) & (x == 0)
    straight = (z != 0) & (z != 1) & (z != 7) & (x == 0)
    none = (root & (jnp.logical_not(first) | flat)) | (jnp.logical_not(first) & straight)
    dx = pick(x % 2 == 1, 1, pick(none, 0, 2))
    dz = dz + pick(flat & jnp.logical_not(first) & jnp.logical_not(root), 2, 0)
    return (pick(first, 7, 5) * dx + pick(first, 6, 4) * dz + pick(first, 8, 6) * yh) * (CHUNKS // 32)


def place():
    r = lax.axis_index("row")
    c = lax.axis_index("col")
    return r, c, r % 2, r // 2, c // (NX * NZ), (c // NX) % NZ, c % NX


def local_row(p, nb, row_count):
    shift = nb.bit_length() - 1
    deal = row_count.bit_length() - 1
    block = jnp.right_shift(p, shift)
    owner = block & (row_count - 1)
    local = jnp.left_shift(jnp.right_shift(block, deal), shift) + (p & (nb - 1))
    return owner, local


def move_kernel(
    row_hbm, mat_hbm, l_hbm, mat, u_ref, takes,
    panel, w_me, w_pair, m_far, comb, code, l_inverse, pivot_row, u_half, parts, from_row, from_at,
    in_sem, recv_sem, send_sem, x_send, x_recv,
):
    r, c, core, yl, yh, z, x = place()
    pair = yl * 2 + 1 - core
    far = (1 - yl) * 2 + core
    source = c == 0
    other = jnp.logical_not(source)
    kids, parent_a, parent_b, order, passes = tree(core, yh, z, x)
    rows, cols = mat_hbm.shape
    tile = rows // TILES
    chunk = rows // CHUNKS
    per = CHUNKS // TILES
    nb, width = l_hbm.shape
    half = nb // 2
    side = cols // SIDES
    row_count = lax.axis_size("row")

    def load(t):
        at = pl.ds(pl.multiple_of(t * tile, tile), tile)
        return pltpu.make_async_copy(mat_hbm.at[at], mat.at[at], in_sem.at[t])

    split_point = CHUNKS // 2

    def turn(mode, j):
        late_first = pick(j < split_point, j + split_point, j - split_point)
        return pick(mode == 0, j, pick(mode == 1, late_first, j // 2 + (j % 2) * split_point))

    def forward(i, k):
        at = pl.ds(pl.multiple_of(i * chunk, chunk), chunk)
        return pltpu.make_async_remote_copy(
            src_ref=panel.at[at],
            dst_ref=panel.at[at],
            send_sem=send_sem.at[k],
            recv_sem=recv_sem.at[i],
            device_id={"row": r, "col": kids[k][2]},
            device_id_type=pl.DeviceIdType.MESH,
        )

    def send(i, second=False):
        head = i < split_point
        for k, (valid, kind, _) in enumerate(kids):
            match = jnp.logical_xor((kind % 2) == 1, head)
            both = kind < 2
            if second:
                go = both & jnp.logical_not(match)
            else:
                go = match | (both & jnp.logical_not(passes))

            @pl.when(valid & go)
            def _():
                forward(i, k).start()

    def swap(step, src, dst, to):
        return pltpu.make_async_remote_copy(
            src_ref=src, dst_ref=dst, send_sem=x_send.at[step], recv_sem=x_recv.at[step],
            device_id={"row": to, "col": c}, device_id_type=pl.DeviceIdType.MESH,
        )

    def signal(row, col):
        pl.semaphore_signal(
            barrier, inc=1, device_id={"row": row, "col": col}, device_id_type=pl.DeviceIdType.MESH
        )

    mine = pl.ds(pl.multiple_of(core * half, half), half)
    with_pair = swap(0, w_me, w_pair, pair)
    across = swap(1, comb, m_far.at[mine], far)
    pass_on = swap(2, m_far.at[mine], m_far.at[mine], pair)

    barrier = pltpu.get_barrier_semaphore()

    @pl.when(other)
    def _():
        signal(r, parent_a)

        @pl.when(parent_b != parent_a)
        def _():
            signal(r, parent_b)

    signal(pair, c)
    signal(far, c)
    load_p = pltpu.make_async_copy(row_hbm, pivot_row, in_sem.at[TILES])
    give_p = pltpu.make_async_copy(from_row, from_at, in_sem.at[TILES + 1])
    load_l = pltpu.make_async_copy(l_hbm, l_inverse, in_sem.at[TILES + 2])
    load_p.start()
    load(0).start()
    for t in range(1, TILES):
        load(t).start()
    load_l.start()

    load_p.wait()
    owner, local = local_row(pivot_row[...], nb, row_count)
    from_row[...] = jnp.where(owner == r, local, lax.broadcasted_iota(jnp.int32, (1, nb), 1))
    takes[...] = jnp.where((owner == r) & (pivot_row[...] >= nb), local, rows)
    mat[pl.ds(rows, 8)] = jnp.zeros((8, cols), mat.dtype)
    kind = jnp.where(owner == r, 0.0, jnp.where(owner == pair, 1.0, 2.0))
    down = lax.broadcasted_iota(jnp.int32, (nb, nb), 0)
    along = lax.broadcasted_iota(jnp.int32, (nb, nb), 1)
    spread = jnp.where(down == along, jnp.broadcast_to(kind, (nb, nb)), 0.0)
    code[...] = jnp.sum(spread, axis=1, keepdims=True)
    give_p.start()

    expect = 2
    for k in range(SLOTS):
        expect = expect + kids[k][0].astype(jnp.int32)
    pl.semaphore_wait(barrier, expect)

    @pl.when(source)
    def _():
        @pl.loop(0, TILES // 2)
        def _(t):
            for half_t in (t, t + TILES // 2):
                load(half_t).wait()
                at = pl.ds(pl.multiple_of(half_t * tile, tile), tile)
                panel[at] = mat[at, :width].astype(panel.dtype)

            @pl.loop(t * 2 * per, (t + 1) * 2 * per)
            def _(j):
                send(turn(2, j))

        @pl.loop(0, CHUNKS)
        def _(j):
            send(turn(2, j), second=True)

    @pl.when(other)
    def _():
        @pl.loop(0, TILES)
        def _(t):
            load(t).wait()

    give_p.wait()

    @pl.loop(0, nb // 8)
    def _(g):
        out = w_me.at[pl.ds(pl.multiple_of(g * 8, 8), 8)]
        got = [mat[pl.ds(from_at[0, g * 8 + s], 1)] for s in range(8)]
        for s in range(8):
            out[pl.ds(s, 1)] = got[s]

    with_pair.start()

    def sent():
        for k, (valid, kind, col) in enumerate(kids):
            for whole in (True, False):
                part = panel if whole else panel.at[pl.ds(0, rows // 2)]

                @pl.when(valid & ((kind < 2) == whole))
                def _():
                    pltpu.make_async_remote_copy(
                        src_ref=part, dst_ref=part, send_sem=send_sem.at[k], recv_sem=recv_sem.at[0],
                        device_id={"row": r, "col": col}, device_id_type=pl.DeviceIdType.MESH,
                    ).wait_send()

    def step_across():
        with_pair.wait_recv()
        kind = code[mine]
        from_pair = (kind > 0.5) & (kind < jnp.where(core == 1, 9.0, 1.5))
        comb[...] = jnp.where(from_pair, w_pair[mine], w_me[mine])
        across.start()

    def step_pass():
        across.wait_recv()
        pass_on.start()

    def step_wait():
        load_l.wait()
        pass_on.wait_recv()

    def step_u(h):
        at = pl.ds(pl.multiple_of(h * side, side), side)
        kind = code[...]
        picked = jnp.where(kind < 0.5, w_me[:, at], jnp.where(kind < 1.5, w_pair[:, at], m_far[:, at]))
        u = jnp.dot(
            l_inverse[...], picked, precision=lax.Precision.HIGHEST, preferred_element_type=jnp.float32
        )
        u_ref[:, at] = u
        u_half[:, at] = u.astype(u_half.dtype)

    def step_split(h):
        at = pl.ds(pl.multiple_of(h * side, side), side)
        whole = jnp.where(
            r == 0, mat[pl.ds(0, nb), at], jnp.where(r == 1, w_pair[:, at], m_far[:, at])
        )
        whole = jnp.where(source & (h * side < width), w_me[:, at], whole)
        edge = float(jnp.finfo(jnp.bfloat16).max)
        for p in range(PARTS):
            part = jnp.clip(whole, -edge, edge).astype(jnp.bfloat16)
            parts[pl.ds(p * nb, nb), at] = part
            whole = whole - part.astype(jnp.float32)

    def step_swap(t):
        at = pl.ds(pl.multiple_of(t * tile, tile), tile)
        index = lax.broadcasted_iota(jnp.int32, (tile, nb), 0) + t * tile
        onehot = jnp.where(index == takes[...], 1.0, 0.0)
        hit = jnp.max(onehot, axis=1, keepdims=True) > 0.5
        onehot = onehot.astype(jnp.bfloat16)
        rows_in = jnp.dot(
            jnp.concatenate([onehot] * PARTS, axis=1), parts[...], preferred_element_type=jnp.float32
        )
        mat[at] = jnp.where(hit, rows_in, mat[at])

    def update(j, size):
        at = pl.ds(pl.multiple_of(j * size, size), size)
        is_top = (r == 0) & (j < nb // size)

        @pl.when(is_top & other)
        def _():
            mat[at] = u_ref[pl.ds(pl.multiple_of((j % (nb // size)) * size, size), size)]

        @pl.when(is_top & source)
        def _():
            mat[at, width:] = u_ref[pl.ds(pl.multiple_of((j % (nb // size)) * size, size), size), width:]

        @pl.when(jnp.logical_not(is_top) & other)
        def _():
            mat[at] = mat[at] - jnp.dot(panel[at], u_half[...], preferred_element_type=jnp.float32)

        @pl.when(jnp.logical_not(is_top) & source)
        def _():
            mat[at, width:] = mat[at, width:] - jnp.dot(
                panel[at], u_half[:, width:], preferred_element_type=jnp.float32
            )

    came = start_time(core, yh, z, x)
    edge = (z == 1) | (z == 7)
    late = (yh == 0) & (((z == 0) & (x % 2 == 1)) | (edge & (x == 1)))
    compact = (expect == 2) & jnp.logical_not(late)
    spread_out = jnp.logical_not(compact)
    unit = CHUNKS // 32
    free_link = unit * 25
    swap_time = pick(late, free_link, unit * 11)
    at_across = jnp.maximum(0, swap_time - came)
    at_pass = jnp.maximum(0, pick(late, free_link + unit * 23, unit * 33) - came)
    slow = (core == 1) & (yh == 1) & (z != 0) & jnp.logical_not(edge)
    at_pass = pick(slow, at_pass // 2, at_pass)
    lags = (core == 1) & (yh == 1) & edge & (x % 2 == 1)
    at_pass = pick(lags, pick(x == 1, CHUNKS // 2 - 1, CHUNKS // 8), at_pass)
    after_pass = jnp.maximum(0, unit * 41 - came)
    after_pass = pick(slow, after_pass * 2 // 3, after_pass)
    after_pass = pick(lags & (x == 1), CHUNKS // 2, jnp.maximum(after_pass, at_pass + 1))
    last = pick(passes, 2 * CHUNKS, CHUNKS)
    settle = passes & other
    at_across = pick(source, 0, pick(settle, jnp.minimum(2 * at_across, last), at_across))
    at_pass = pick(source, 1, pick(settle, last, at_pass))
    at_u = pick(source, 2, pick(settle, last + 1, pick(late, at_pass + unit * 8, after_pass)))
    split_at = 4 * SIDES
    swap_at = split_at + 2 * SIDES
    steps = swap_at + 2 * TILES

    def tile_turn(p):
        upper = TILES // 2
        return pick(order == 0, p, pick(order == 1, (p + upper) % TILES, p // 2 + (p % 2) * upper))

    def early(p):
        done = pick(order == 2, (p // 2 + 1) * 2 * per - 1, (p + 1) * per - 1)
        return at_u + swap_at + 2 * p + 1 >= jnp.minimum(done, CHUNKS - 1)

    @pl.when(compact)
    def _():
        step_across()
        step_pass()
        step_wait()

        @pl.loop(0, SIDES)
        def _(h):
            step_u(h)
            step_split(h)

        @pl.loop(0, TILES)
        def _(t):
            step_swap(t)

        group = CHUNKS // 4

        @pl.loop(0, 4)
        def _(g):
            @pl.loop(g * group, (g + 1) * group)
            def _(j):
                forward(turn(order, j), 0).wait_recv()

            one = pick(order == 0, 2 * g, pick(order == 1, (2 * g + TILES // 2) % TILES, g))
            update(one, tile)
            update(one + pick(order == 2, TILES // 2, 1), tile)

    @pl.when(spread_out)
    def _():
        @pl.loop(0, jnp.maximum(last, at_u + steps))
        def _(j):
            pl.when(j == at_across)(step_across)
            pl.when(j == at_pass)(step_pass)

            @pl.when((j < CHUNKS) & other)
            def _():
                i = turn(order, j)
                forward(i, 0).wait_recv()
                send(i)

            @pl.when(settle & (j >= CHUNKS) & (j < last))
            def _():
                send(turn(2, jnp.minimum(j - CHUNKS, CHUNKS - 1)), second=True)

            q = j - at_u
            pl.when(q == 0)(step_wait)

            @pl.when((q >= 0) & (q < split_at) & (q % 4 == 0))
            def _():
                step_u(q // 4)

            @pl.when((q >= split_at) & (q < swap_at) & (q % 2 == 0))
            def _():
                step_split((q - split_at) // 2)

            @pl.when((q >= swap_at) & (q < steps) & (q % 2 == 0))
            def _():
                step_swap(tile_turn((q - swap_at) // 2))

            p = (q - swap_at) // 2

            @pl.when((q >= swap_at) & (q < steps) & (q % 2 == 1) & early(p))
            def _():
                update(tile_turn(p), tile)

        @pl.loop(0, TILES)
        def _(p):
            @pl.when(jnp.logical_not(early(p)))
            def _():
                update(tile_turn(p), tile)

    with_pair.wait_send()
    across.wait_send()
    pass_on.wait_send()
    sent()


def finish_kernel(mat, u_ref, takes, out, u_out, moved_out, moved, takes_at, sem):
    rows = out.shape[0]
    tile = rows // TILES
    nb = u_ref.shape[0]
    give_t = pltpu.make_async_copy(takes, takes_at, sem.at[TILES])
    give_t.start()
    copies = [
        pltpu.make_async_copy(mat.at[pl.ds(t * tile, tile)], out.at[pl.ds(t * tile, tile)], sem.at[t])
        for t in range(TILES)
    ]
    copies.append(pltpu.make_async_copy(u_ref, u_out, sem.at[TILES + 1]))
    for copy in copies:
        copy.start()
    give_t.wait()

    @pl.loop(0, nb // 8)
    def _(g):
        eight = moved.at[pl.ds(pl.multiple_of(g * 8, 8), 8)]
        got = [mat[pl.ds(takes_at[0, g * 8 + s], 1)] for s in range(8)]
        for s in range(8):
            eight[pl.ds(s, 1)] = got[s]

    last = pltpu.make_async_copy(moved, moved_out, sem.at[TILES + 2])
    last.start()
    copies.append(last)
    for copy in copies:
        copy.wait()


def body(matrix, pivots, l_inverse):
    rows, cols = matrix.shape
    nb = l_inverse.shape[0]
    f32, bf16, i32 = jnp.float32, jnp.bfloat16, jnp.int32
    vmem = pl.BlockSpec(memory_space=pltpu.VMEM)
    hbm = pl.BlockSpec(memory_space=pltpu.HBM)
    shape = jax.ShapeDtypeStruct
    stay = lambda array: pltpu.with_memory_space_constraint(array, pltpu.HBM)
    work, u_rows, takes = pl.pallas_call(
        move_kernel,
        out_shape=(shape((rows + 8, cols), f32), shape((nb, cols), f32), shape((1, nb), i32)),
        in_specs=[hbm] * 3,
        out_specs=[vmem] * 3,
        scratch_shapes=[
            pltpu.VMEM((rows, nb), bf16),
            pltpu.VMEM((nb, cols), f32),
            pltpu.VMEM((nb, cols), f32),
            pltpu.VMEM((nb, cols), f32),
            pltpu.VMEM((nb // 2, cols), f32),
            pltpu.VMEM((nb, 1), f32),
            pltpu.VMEM((nb, nb), f32),
            pltpu.VMEM((1, nb), i32),
            pltpu.VMEM((nb, cols), bf16),
            pltpu.VMEM((PARTS * nb, cols), bf16),
            pltpu.VMEM((1, nb), i32),
            pltpu.SMEM((1, nb), i32),
            pltpu.SemaphoreType.DMA((TILES + 3,)),
            pltpu.SemaphoreType.DMA((CHUNKS,)),
            pltpu.SemaphoreType.DMA((SLOTS,)),
            pltpu.SemaphoreType.DMA((3,)),
            pltpu.SemaphoreType.DMA((3,)),
        ],
        compiler_params=pltpu.CompilerParams(
            collective_id=0, has_side_effects=True, vmem_limit_bytes=MOVE_VMEM
        ),
        name="move",
    )(stay(pivots.reshape(1, nb)), stay(matrix), stay(l_inverse))
    return pl.pallas_call(
        finish_kernel,
        out_shape=(shape((rows, cols), f32), shape((nb, cols), f32), shape((nb, cols), f32)),
        in_specs=[vmem] * 3,
        out_specs=[hbm] * 3,
        scratch_shapes=[
            pltpu.VMEM((nb, cols), f32),
            pltpu.SMEM((1, nb), i32),
            pltpu.SemaphoreType.DMA((TILES + 3,)),
        ],
        compiler_params=pltpu.CompilerParams(vmem_limit_bytes=FINISH_VMEM),
        name="finish",
    )(work, u_rows, takes)


def solution(mesh):
    return jax.shard_map(
        body,
        mesh=mesh,
        in_specs=(P("row", "col"), P(), P()),
        out_specs=(P("row", "col"), P(None, "col"), P("row", "col")),
        check_vma=False,
    )
```

```python
import jax
import jax.numpy as jnp
from jax import lax
from jax.experimental import pallas as pl
from jax.experimental.pallas import tpu as pltpu
from jax.sharding import PartitionSpec as P

CHUNKS = 32
TILES = 8
SLOTS = 4
PARTS = 2
SIDES = 2
MOVE_VMEM = 24 * 2**20
FINISH_VMEM = 8 * 2**20
NZ = 8
NX = 4


def pick(cond, a, b):
    return jnp.where(cond, a, b)


def column(yh, z, x):
    return (yh * NZ + z) * NX + x


def tree(core, yh, z, x):
    first = core == 0
    second = jnp.logical_not(first)
    root = (yh == 0) & (x == 0)
    off = jnp.logical_not(root)
    flat = z == 0
    up = (z >= 1) & (z <= 3)
    down = (z == 6) | (z == 7)
    odd = (x % 2) == 1
    inplane = pick(first, flat, jnp.logical_not(flat))
    folded = inplane & (first | (z == 1) | (z == 7))
    plain = inplane & jnp.logical_not(folded)
    twin = first & ((x == 2) | ((yh == 1) & (x == 0)))
    only = pick(x == 1, 2, 3)
    along = pick(first, off, root)
    v0 = along & (flat | up | down | (twin & (z == 5)))
    k0 = column(yh, pick(flat, 1, pick(up, z + 1, z - 1)), x)
    c0 = pick(twin & (z == 3), 2, pick(twin & (z == 5), 3, 0))
    drop = second & (z == 1) & off
    over = plain & root
    v2 = (along & flat) | drop | over
    k2 = pick(over, column(1, z, 0), column(yh, pick(drop, 0, 7), x))
    c2 = pick(twin, 1, 0)
    back = first & jnp.logical_not(flat) & (yh == 0) & (x == 1)
    v1 = (folded & jnp.logical_not((yh == 0) & (x == 2))) | back | (plain & (x <= 1))
    x1 = pick(odd, 2, pick(x == 2, 1, pick(yh == 0, 1, 3)))
    k1 = column(yh, z, pick(back, 0, pick(plain, x + 1, x1)))
    c1 = pick(back | root | plain, 0, pick(odd, only, pick(x == 2, 3, 2)))
    v3 = (folded & (root | odd)) | (plain & (x == 0))
    k3 = pick(root | plain, column(yh, z, 3), pick(yh == 0, column(1, z, x), column(1, z, 0)))
    c3 = pick(root | plain, pick(first, 1, 0), only)
    kids = ((v0, c0, k0), (v1, c1, k1), (v2, c2, k2), (v3, c3, k3))
    near = pick(z <= 4, z - 1, (z + 1) % NZ)
    in_a = pick(
        yh == 0,
        pick(odd, column(0, z, 0), column(0, z, 1)),
        pick(x == 1, column(0, z, 1), pick(x == 3, column(1, z, 0), column(1, z, 1))),
    )
    in_b = pick(
        yh == 0,
        pick(odd, column(0, z, 0), column(0, z, 3)),
        pick(x == 1, column(1, z, 2), pick(x == 3, column(0, z, 3), column(1, z, 3))),
    )
    chain_a = pick(root, column(0, z, 1), column(yh, near, x))
    chain_b = pick(twin & (z == 4), column(yh, 5, x), chain_a)
    stem = pick(root, column(0, near, 0), column(yh, 1, x))
    other_plane = pick(first, jnp.logical_not(flat), flat | root)
    in_plain = pick(x == 2, column(yh, z, 1), pick(x == 0, column(0, z, 0), column(yh, z, 0)))
    parent_a = pick(other_plane, pick(first, chain_a, stem), pick(plain, in_plain, in_a))
    parent_b = pick(other_plane, pick(first, chain_b, stem), pick(plain, in_plain, in_b))
    beyond = z >= 5
    turn = pick(flat | (z == 4), pick(flat & (x == 0), 3, 2), pick(beyond, 1, 0))
    side = (yh == 1) & (x == 3) & folded
    order = pick(first, pick(twin, turn, pick(x == 3, 1, 0)), pick(side, 2, 0))
    passes = (flat & root) | (twin & flat)
    return kids, parent_a, parent_b, order, passes


def start_time(core, yh, z, x):
    first = core == 0
    dz = jnp.minimum(z, NZ - z)
    flat = z == 0
    root = (yh == 0) & (x == 0)
    straight = (z != 0) & (z != 1) & (z != 7) & (x == 0)
    none = (root & (jnp.logical_not(first) | flat)) | (jnp.logical_not(first) & straight)
    dx = pick(x % 2 == 1, 1, pick(none, 0, 2))
    dz = dz + pick(flat & jnp.logical_not(first) & jnp.logical_not(root), 2, 0)
    return (pick(first, 7, 5) * dx + pick(first, 6, 4) * dz + pick(first, 8, 6) * yh) * (CHUNKS // 32)


def place():
    r = lax.axis_index("row")
    c = lax.axis_index("col")
    return r, c, r % 2, r // 2, c // (NX * NZ), (c // NX) % NZ, c % NX


def local_row(p, nb, row_count):
    shift = nb.bit_length() - 1
    deal = row_count.bit_length() - 1
    block = jnp.right_shift(p, shift)
    owner = block & (row_count - 1)
    local = jnp.left_shift(jnp.right_shift(block, deal), shift) + (p & (nb - 1))
    return owner, local


def move_kernel(
    row_hbm, mat_hbm, l_hbm, mat, u_ref, takes,
    panel, w_me, w_pair, m_far, comb, code, l_inverse, pivot_row, u_half, parts, from_row, from_at,
    in_sem, recv_sem, send_sem, x_send, x_recv,
):
    r, c, core, yl, yh, z, x = place()
    pair = yl * 2 + 1 - core
    far = (1 - yl) * 2 + core
    source = c == 0
    other = jnp.logical_not(source)
    kids, parent_a, parent_b, order, passes = tree(core, yh, z, x)
    rows, cols = mat_hbm.shape
    tile = rows // TILES
    chunk = rows // CHUNKS
    per = CHUNKS // TILES
    nb, width = l_hbm.shape
    half = nb // 2
    side = cols // SIDES
    row_count = lax.axis_size("row")

    def load(t):
        at = pl.ds(pl.multiple_of(t * tile, tile), tile)
        return pltpu.make_async_copy(mat_hbm.at[at], mat.at[at], in_sem.at[t])

    split_point = CHUNKS // 2

    def turn(mode, j):
        late_first = pick(j < split_point, j + split_point, j - split_point)
        even = j // 2 + (j % 2) * split_point
        lead = CHUNKS // 8
        m = jnp.maximum(j - lead, 0)
        led = pick(m % 2 == 0, m // 2 + split_point, m // 2 + lead)
        led = pick(j < lead, j, pick(j < CHUNKS - lead, led, j))
        return pick(mode == 0, j, pick(mode == 1, late_first, pick(mode == 2, even, led)))

    def forward(i, k):
        at = pl.ds(pl.multiple_of(i * chunk, chunk), chunk)
        return pltpu.make_async_remote_copy(
            src_ref=panel.at[at],
            dst_ref=panel.at[at],
            send_sem=send_sem.at[k],
            recv_sem=recv_sem.at[i],
            device_id={"row": r, "col": kids[k][2]},
            device_id_type=pl.DeviceIdType.MESH,
        )

    def send(i, second=False):
        head = i < split_point
        for k, (valid, kind, _) in enumerate(kids):
            match = jnp.logical_xor((kind % 2) == 1, head)
            both = kind < 2
            if second:
                go = both & jnp.logical_not(match)
            else:
                go = match | (both & jnp.logical_not(passes))

            @pl.when(valid & go)
            def _():
                forward(i, k).start()

    def swap(step, src, dst, to):
        return pltpu.make_async_remote_copy(
            src_ref=src, dst_ref=dst, send_sem=x_send.at[step], recv_sem=x_recv.at[step],
            device_id={"row": to, "col": c}, device_id_type=pl.DeviceIdType.MESH,
        )

    def signal(row, col):
        pl.semaphore_signal(
            barrier, inc=1, device_id={"row": row, "col": col}, device_id_type=pl.DeviceIdType.MESH
        )

    mine = pl.ds(pl.multiple_of(core * half, half), half)
    with_pair = swap(0, w_me, w_pair, pair)
    across = swap(1, comb, m_far.at[mine], far)
    pass_on = swap(2, m_far.at[mine], m_far.at[mine], pair)

    load_p = pltpu.make_async_copy(row_hbm, pivot_row, in_sem.at[TILES])
    give_p = pltpu.make_async_copy(from_row, from_at, in_sem.at[TILES + 1])
    load_l = pltpu.make_async_copy(l_hbm, l_inverse, in_sem.at[TILES + 2])
    load(0).start()
    load(TILES // 2).start()
    load_p.start()
    for t in range(1, TILES):
        if t != TILES // 2:
            load(t).start()
    load_l.start()

    barrier = pltpu.get_barrier_semaphore()

    @pl.when(other)
    def _():
        signal(r, parent_a)

        @pl.when(parent_b != parent_a)
        def _():
            signal(r, parent_b)

    signal(pair, c)
    signal(far, c)
    def prepare():
        load_p.wait()
        owner, local = local_row(pivot_row[...], nb, row_count)
        from_row[...] = jnp.where(owner == r, local, lax.broadcasted_iota(jnp.int32, (1, nb), 1))
        takes[...] = jnp.where((owner == r) & (pivot_row[...] >= nb), local, rows)
        mat[pl.ds(rows, 8)] = jnp.zeros((8, cols), mat.dtype)
        kind = jnp.where(owner == r, 0.0, jnp.where(owner == pair, 1.0, 2.0))
        down = lax.broadcasted_iota(jnp.int32, (nb, nb), 0)
        along = lax.broadcasted_iota(jnp.int32, (nb, nb), 1)
        spread = jnp.where(down == along, jnp.broadcast_to(kind, (nb, nb)), 0.0)
        code[...] = jnp.sum(spread, axis=1, keepdims=True)
        give_p.start()

    pl.when(other)(prepare)

    expect = 2
    for k in range(SLOTS):
        expect = expect + kids[k][0].astype(jnp.int32)
    pl.semaphore_wait(barrier, expect)

    @pl.when(source)
    def _():
        @pl.loop(0, TILES // 2)
        def _(t):
            for half_t in (t, t + TILES // 2):
                load(half_t).wait()
                at = pl.ds(pl.multiple_of(half_t * tile, tile), tile)
                panel[at] = mat[at, :width].astype(panel.dtype)

            @pl.loop(t * 2 * per, (t + 1) * 2 * per)
            def _(j):
                send(turn(2, j))

        @pl.loop(0, CHUNKS)
        def _(j):
            send(turn(2, j), second=True)

        prepare()

    @pl.when(other)
    def _():
        @pl.loop(0, TILES)
        def _(t):
            load(t).wait()

    give_p.wait()

    @pl.loop(0, nb // 8)
    def _(g):
        out = w_me.at[pl.ds(pl.multiple_of(g * 8, 8), 8)]
        got = [mat[pl.ds(from_at[0, g * 8 + s], 1)] for s in range(8)]
        for s in range(8):
            out[pl.ds(s, 1)] = got[s]

    with_pair.start()

    def sent():
        for k, (valid, kind, col) in enumerate(kids):
            for whole in (True, False):
                part = panel if whole else panel.at[pl.ds(0, rows // 2)]

                @pl.when(valid & ((kind < 2) == whole))
                def _():
                    pltpu.make_async_remote_copy(
                        src_ref=part, dst_ref=part, send_sem=send_sem.at[k], recv_sem=recv_sem.at[0],
                        device_id={"row": r, "col": col}, device_id_type=pl.DeviceIdType.MESH,
                    ).wait_send()

    def step_across():
        with_pair.wait_recv()
        kind = code[mine]
        from_pair = (kind > 0.5) & (kind < jnp.where(core == 1, 9.0, 1.5))
        comb[...] = jnp.where(from_pair, w_pair[mine], w_me[mine])
        across.start()

    def step_pass():
        across.wait_recv()
        pass_on.start()

    def step_wait():
        load_l.wait()
        pass_on.wait_recv()

    def step_u(h):
        at = pl.ds(pl.multiple_of(h * side, side), side)
        kind = code[...]
        picked = jnp.where(kind < 0.5, w_me[:, at], jnp.where(kind < 1.5, w_pair[:, at], m_far[:, at]))
        u = jnp.dot(
            l_inverse[...], picked, precision=lax.Precision.HIGHEST, preferred_element_type=jnp.float32
        )
        u_ref[:, at] = u
        u_half[:, at] = u.astype(u_half.dtype)

    def step_split(h):
        at = pl.ds(pl.multiple_of(h * side, side), side)
        whole = jnp.where(
            r == 0, mat[pl.ds(0, nb), at], jnp.where(r == 1, w_pair[:, at], m_far[:, at])
        )
        whole = jnp.where(source & (h * side < width), w_me[:, at], whole)
        edge = float(jnp.finfo(jnp.bfloat16).max)
        for p in range(PARTS):
            part = jnp.clip(whole, -edge, edge).astype(jnp.bfloat16)
            parts[pl.ds(p * nb, nb), at] = part
            whole = whole - part.astype(jnp.float32)

    def step_swap(t):
        at = pl.ds(pl.multiple_of(t * tile, tile), tile)
        index = lax.broadcasted_iota(jnp.int32, (tile, nb), 0) + t * tile
        onehot = jnp.where(index == takes[...], 1.0, 0.0)
        hit = jnp.max(onehot, axis=1, keepdims=True) > 0.5
        onehot = onehot.astype(jnp.bfloat16)
        rows_in = jnp.dot(
            jnp.concatenate([onehot] * PARTS, axis=1), parts[...], preferred_element_type=jnp.float32
        )
        mat[at] = jnp.where(hit, rows_in, mat[at])

    def update(j, size):
        at = pl.ds(pl.multiple_of(j * size, size), size)
        is_top = (r == 0) & (j < nb // size)

        @pl.when(is_top & other)
        def _():
            mat[at] = u_ref[pl.ds(pl.multiple_of((j % (nb // size)) * size, size), size)]

        @pl.when(is_top & source)
        def _():
            mat[at, width:] = u_ref[pl.ds(pl.multiple_of((j % (nb // size)) * size, size), size), width:]

        @pl.when(jnp.logical_not(is_top) & other)
        def _():
            mat[at] = mat[at] - jnp.dot(panel[at], u_half[...], preferred_element_type=jnp.float32)

        @pl.when(jnp.logical_not(is_top) & source)
        def _():
            mat[at, width:] = mat[at, width:] - jnp.dot(
                panel[at], u_half[:, width:], preferred_element_type=jnp.float32
            )

    came = start_time(core, yh, z, x)
    edge = (z == 1) | (z == 7)
    late = (yh == 0) & (((z == 0) & (x % 2 == 1)) | (edge & (x == 1)))
    compact = (expect == 2) & jnp.logical_not(late)
    spread_out = jnp.logical_not(compact)
    unit = CHUNKS // 32
    free_link = unit * 25
    swap_time = pick(late, free_link, unit * 11)
    at_across = jnp.maximum(0, swap_time - came)
    at_pass = jnp.maximum(0, pick(late, free_link + unit * 23, unit * 33) - came)
    slow = (core == 1) & (yh == 1) & (z != 0) & jnp.logical_not(edge)
    at_pass = pick(slow, at_pass // 2, at_pass)
    lags = (core == 1) & (yh == 1) & edge & (x % 2 == 1)
    fast = lags & (z == 7)
    at_pass = pick(lags, pick(x == 1, CHUNKS // 2 - 1, CHUNKS // 8), at_pass)
    after_pass = jnp.maximum(0, unit * 41 - came)
    after_pass = pick(slow, after_pass * 2 // 3, after_pass)
    after_pass = pick(lags & (x == 1), CHUNKS // 2, jnp.maximum(after_pass, at_pass + 1))
    last = pick(passes, 2 * CHUNKS, CHUNKS)
    settle = passes & other
    at_across = pick(source, 0, pick(settle, jnp.minimum(2 * at_across, last), at_across))
    at_pass = pick(source, 1, pick(settle, last, at_pass))
    at_u = pick(source, 2, pick(settle, last + 1, pick(late, at_pass + unit * 8, after_pass)))
    split_at = 4 * SIDES
    swap_at = split_at + 2 * SIDES
    steps = swap_at + 2 * TILES

    def tile_turn(p):
        upper = TILES // 2
        return pick(order == 0, p, pick(order == 1, (p + upper) % TILES, p // 2 + (p % 2) * upper))

    def early(p):
        done = pick(order == 2, (p // 2 + 1) * 2 * per - 1, (p + 1) * per - 1)
        step = swap_at + 2 * p
        return at_u + pick(fast, step // 2, step) >= jnp.minimum(done, CHUNKS - 1)

    @pl.when(compact)
    def _():
        step_across()
        step_pass()
        step_wait()

        @pl.loop(0, SIDES)
        def _(h):
            step_u(h)
            step_split(h)

        @pl.loop(0, TILES)
        def _(t):
            step_swap(t)

        group = CHUNKS // 4

        @pl.loop(0, 4)
        def _(g):
            @pl.loop(g * group, (g + 1) * group)
            def _(j):
                forward(turn(order, j), 0).wait_recv()

            one = pick(order == 0, 2 * g, pick(order == 1, (2 * g + TILES // 2) % TILES, g))
            update(one, tile)
            update(one + pick(order == 2, TILES // 2, 1), tile)

    @pl.when(spread_out)
    def _():
        @pl.loop(0, jnp.maximum(last, at_u + pick(fast, steps // 2, steps)))
        def _(j):
            pl.when(j == at_across)(step_across)
            pl.when(j == at_pass)(step_pass)

            @pl.when((j < CHUNKS) & other)
            def _():
                i = turn(order, j)
                forward(i, 0).wait_recv()
                send(i)

            @pl.when(settle & (j >= CHUNKS) & (j < last))
            def _():
                send(turn(2, jnp.minimum(j - CHUNKS, CHUNKS - 1)), second=True)

            q = (j - at_u) * pick(fast, 2, 1)
            pl.when(q == 0)(step_wait)

            @pl.when((q >= 0) & (q < split_at) & (q % 4 == 0))
            def _():
                step_u(q // 4)

            @pl.when((q >= split_at) & (q < swap_at) & (q % 2 == 0))
            def _():
                step_split((q - split_at) // 2)

            @pl.when((q >= swap_at) & (q < steps) & (q % 2 == 0))
            def _():
                p = (q - swap_at) // 2
                step_swap(tile_turn(p))

                @pl.when(early(p))
                def _():
                    update(tile_turn(p), tile)

        @pl.loop(0, TILES)
        def _(p):
            @pl.when(jnp.logical_not(early(p)))
            def _():
                update(tile_turn(p), tile)

    with_pair.wait_send()
    across.wait_send()
    pass_on.wait_send()
    sent()


def finish_kernel(mat, u_ref, takes, out, u_out, moved_out, moved, takes_at, sem):
    rows = out.shape[0]
    tile = rows // TILES
    nb = u_ref.shape[0]
    give_t = pltpu.make_async_copy(takes, takes_at, sem.at[TILES])
    give_t.start()
    copies = [
        pltpu.make_async_copy(mat.at[pl.ds(t * tile, tile)], out.at[pl.ds(t * tile, tile)], sem.at[t])
        for t in range(TILES)
    ]
    copies.append(pltpu.make_async_copy(u_ref, u_out, sem.at[TILES + 1]))
    for copy in copies:
        copy.start()
    give_t.wait()

    def gather(g):
        eight = moved.at[pl.ds(pl.multiple_of(g * 8, 8), 8)]
        got = [mat[pl.ds(takes_at[0, g * 8 + s], 1)] for s in range(8)]
        for s in range(8):
            eight[pl.ds(s, 1)] = got[s]

    part = nb // 4
    for p in range(4):
        pl.loop(p * part // 8, (p + 1) * part // 8)(gather)
        at = pl.ds(p * part, part)
        last = pltpu.make_async_copy(moved.at[at], moved_out.at[at], sem.at[TILES + 2 + p])
        last.start()
        copies.append(last)
    for copy in copies:
        copy.wait()


def body(matrix, pivots, l_inverse):
    rows, cols = matrix.shape
    nb = l_inverse.shape[0]
    f32, bf16, i32 = jnp.float32, jnp.bfloat16, jnp.int32
    vmem = pl.BlockSpec(memory_space=pltpu.VMEM)
    hbm = pl.BlockSpec(memory_space=pltpu.HBM)
    shape = jax.ShapeDtypeStruct
    stay = lambda array: pltpu.with_memory_space_constraint(array, pltpu.HBM)
    work, u_rows, takes = pl.pallas_call(
        move_kernel,
        out_shape=(shape((rows + 8, cols), f32), shape((nb, cols), f32), shape((1, nb), i32)),
        in_specs=[hbm] * 3,
        out_specs=[vmem] * 3,
        scratch_shapes=[
            pltpu.VMEM((rows, nb), bf16),
            pltpu.VMEM((nb, cols), f32),
            pltpu.VMEM((nb, cols), f32),
            pltpu.VMEM((nb, cols), f32),
            pltpu.VMEM((nb // 2, cols), f32),
            pltpu.VMEM((nb, 1), f32),
            pltpu.VMEM((nb, nb), f32),
            pltpu.VMEM((1, nb), i32),
            pltpu.VMEM((nb, cols), bf16),
            pltpu.VMEM((PARTS * nb, cols), bf16),
            pltpu.VMEM((1, nb), i32),
            pltpu.SMEM((1, nb), i32),
            pltpu.SemaphoreType.DMA((TILES + 3,)),
            pltpu.SemaphoreType.DMA((CHUNKS,)),
            pltpu.SemaphoreType.DMA((SLOTS,)),
            pltpu.SemaphoreType.DMA((3,)),
            pltpu.SemaphoreType.DMA((3,)),
        ],
        compiler_params=pltpu.CompilerParams(
            collective_id=0, has_side_effects=True, vmem_limit_bytes=MOVE_VMEM
        ),
        name="move",
    )(stay(pivots.reshape(1, nb)), stay(matrix), stay(l_inverse))
    return pl.pallas_call(
        finish_kernel,
        out_shape=(shape((rows, cols), f32), shape((nb, cols), f32), shape((nb, cols), f32)),
        in_specs=[vmem] * 3,
        out_specs=[hbm] * 3,
        scratch_shapes=[
            pltpu.VMEM((nb, cols), f32),
            pltpu.SMEM((1, nb), i32),
            pltpu.SemaphoreType.DMA((TILES + 6,)),
        ],
        compiler_params=pltpu.CompilerParams(vmem_limit_bytes=FINISH_VMEM),
        name="finish",
    )(work, u_rows, takes)


def solution(mesh):
    return jax.shard_map(
        body,
        mesh=mesh,
        in_specs=(P("row", "col"), P(), P()),
        out_specs=(P("row", "col"), P(None, "col"), P("row", "col")),
        check_vma=False,
    )
```

```python
import jax
import jax.numpy as jnp
from jax import lax
from jax.experimental import pallas as pl
from jax.experimental.pallas import tpu as pltpu
from jax.sharding import PartitionSpec as P

CHUNKS = 32
TILES = 8
SLOTS = 4
PARTS = 2
SIDES = 2
MOVE_VMEM = 24 * 2**20
FINISH_VMEM = 8 * 2**20
NZ = 8
NX = 4


def pick(cond, a, b):
    return jnp.where(cond, a, b)


def column(yh, z, x):
    return (yh * NZ + z) * NX + x


def tree(core, yh, z, x):
    first = core == 0
    second = jnp.logical_not(first)
    root = (yh == 0) & (x == 0)
    off = jnp.logical_not(root)
    flat = z == 0
    up = (z >= 1) & (z <= 3)
    down = (z == 6) | (z == 7)
    odd = (x % 2) == 1
    inplane = pick(first, flat, jnp.logical_not(flat))
    folded = inplane & (first | (z == 1) | (z == 7))
    plain = inplane & jnp.logical_not(folded)
    twin = first & ((x == 2) | ((yh == 1) & (x == 0)))
    only = pick(x == 1, 2, 3)
    along = pick(first, off, root)
    v0 = along & (flat | up | down | (twin & (z == 5)))
    k0 = column(yh, pick(flat, 1, pick(up, z + 1, z - 1)), x)
    c0 = pick(twin & (z == 3), 2, pick(twin & (z == 5), 3, 0))
    drop = second & (z == 1) & off
    over = plain & root
    v2 = (along & flat) | drop | over
    k2 = pick(over, column(1, z, 0), column(yh, pick(drop, 0, 7), x))
    c2 = pick(twin, 1, 0)
    back = first & jnp.logical_not(flat) & (yh == 0) & (x == 1)
    v1 = (folded & jnp.logical_not((yh == 0) & (x == 2))) | back | (plain & (x <= 1))
    x1 = pick(odd, 2, pick(x == 2, 1, pick(yh == 0, 1, 3)))
    k1 = column(yh, z, pick(back, 0, pick(plain, x + 1, x1)))
    c1 = pick(back | root | plain, 0, pick(odd, only, pick(x == 2, 3, 2)))
    v3 = (folded & (root | odd)) | (plain & (x == 0))
    k3 = pick(root | plain, column(yh, z, 3), pick(yh == 0, column(1, z, x), column(1, z, 0)))
    c3 = pick(root | plain, pick(first, 1, 0), only)
    kids = ((v0, c0, k0), (v1, c1, k1), (v2, c2, k2), (v3, c3, k3))
    near = pick(z <= 4, z - 1, (z + 1) % NZ)
    in_a = pick(
        yh == 0,
        pick(odd, column(0, z, 0), column(0, z, 1)),
        pick(x == 1, column(0, z, 1), pick(x == 3, column(1, z, 0), column(1, z, 1))),
    )
    in_b = pick(
        yh == 0,
        pick(odd, column(0, z, 0), column(0, z, 3)),
        pick(x == 1, column(1, z, 2), pick(x == 3, column(0, z, 3), column(1, z, 3))),
    )
    chain_a = pick(root, column(0, z, 1), column(yh, near, x))
    chain_b = pick(twin & (z == 4), column(yh, 5, x), chain_a)
    stem = pick(root, column(0, near, 0), column(yh, 1, x))
    other_plane = pick(first, jnp.logical_not(flat), flat | root)
    in_plain = pick(x == 2, column(yh, z, 1), pick(x == 0, column(0, z, 0), column(yh, z, 0)))
    parent_a = pick(other_plane, pick(first, chain_a, stem), pick(plain, in_plain, in_a))
    parent_b = pick(other_plane, pick(first, chain_b, stem), pick(plain, in_plain, in_b))
    beyond = z >= 5
    turn = pick(flat | (z == 4), pick(flat & (x == 0), 3, 2), pick(beyond, 1, 0))
    side = (yh == 1) & (x == 3) & folded
    order = pick(first, pick(twin, turn, pick(x == 3, 1, 0)), pick(side, 2, 0))
    passes = (flat & root) | (twin & flat)
    return kids, parent_a, parent_b, order, passes


def start_time(core, yh, z, x):
    first = core == 0
    dz = jnp.minimum(z, NZ - z)
    flat = z == 0
    root = (yh == 0) & (x == 0)
    straight = (z != 0) & (z != 1) & (z != 7) & (x == 0)
    none = (root & (jnp.logical_not(first) | flat)) | (jnp.logical_not(first) & straight)
    dx = pick(x % 2 == 1, 1, pick(none, 0, 2))
    dz = dz + pick(flat & jnp.logical_not(first) & jnp.logical_not(root), 2, 0)
    return (pick(first, 7, 5) * dx + pick(first, 6, 4) * dz + pick(first, 8, 6) * yh) * (CHUNKS // 32)


def place():
    r = lax.axis_index("row")
    c = lax.axis_index("col")
    return r, c, r % 2, r // 2, c // (NX * NZ), (c // NX) % NZ, c % NX


def local_row(p, nb, row_count):
    shift = nb.bit_length() - 1
    deal = row_count.bit_length() - 1
    block = jnp.right_shift(p, shift)
    owner = block & (row_count - 1)
    local = jnp.left_shift(jnp.right_shift(block, deal), shift) + (p & (nb - 1))
    return owner, local


def move_kernel(
    row_hbm, mat_hbm, l_hbm, mat, u_ref, takes,
    panel, w_me, w_pair, m_far, comb, code, l_inverse, pivot_row, u_half, parts, from_row, from_at,
    in_sem, recv_sem, send_sem, x_send, x_recv,
):
    r, c, core, yl, yh, z, x = place()
    pair = yl * 2 + 1 - core
    far = (1 - yl) * 2 + core
    source = c == 0
    other = jnp.logical_not(source)
    kids, parent_a, parent_b, order, passes = tree(core, yh, z, x)
    rows, cols = mat_hbm.shape
    tile = rows // TILES
    chunk = rows // CHUNKS
    per = CHUNKS // TILES
    nb, width = l_hbm.shape
    half = nb // 2
    side = cols // SIDES
    row_count = lax.axis_size("row")

    def load(t):
        at = pl.ds(pl.multiple_of(t * tile, tile), tile)
        return pltpu.make_async_copy(mat_hbm.at[at], mat.at[at], in_sem.at[t])

    split_point = CHUNKS // 2

    def turn(mode, j):
        late_first = pick(j < split_point, j + split_point, j - split_point)
        even = j // 2 + (j % 2) * split_point
        lead = CHUNKS // 8
        m = jnp.maximum(j - lead, 0)
        led = pick(m % 2 == 0, m // 2 + split_point, m // 2 + lead)
        led = pick(j < lead, j, pick(j < CHUNKS - lead, led, j))
        return pick(mode == 0, j, pick(mode == 1, late_first, pick(mode == 2, even, led)))

    def forward(i, k):
        at = pl.ds(pl.multiple_of(i * chunk, chunk), chunk)
        return pltpu.make_async_remote_copy(
            src_ref=panel.at[at],
            dst_ref=panel.at[at],
            send_sem=send_sem.at[k],
            recv_sem=recv_sem.at[i],
            device_id={"row": r, "col": kids[k][2]},
            device_id_type=pl.DeviceIdType.MESH,
        )

    def send(i, second=False):
        head = i < split_point
        for k, (valid, kind, _) in enumerate(kids):
            match = jnp.logical_xor((kind % 2) == 1, head)
            both = kind < 2
            if second:
                go = both & jnp.logical_not(match)
            else:
                go = match | (both & jnp.logical_not(passes))

            @pl.when(valid & go)
            def _():
                forward(i, k).start()

    def swap(step, src, dst, to):
        return pltpu.make_async_remote_copy(
            src_ref=src, dst_ref=dst, send_sem=x_send.at[step], recv_sem=x_recv.at[step],
            device_id={"row": to, "col": c}, device_id_type=pl.DeviceIdType.MESH,
        )

    def signal(row, col):
        pl.semaphore_signal(
            barrier, inc=1, device_id={"row": row, "col": col}, device_id_type=pl.DeviceIdType.MESH
        )

    mine = pl.ds(pl.multiple_of(core * half, half), half)
    with_pair = swap(0, w_me, w_pair, pair)
    across = swap(1, comb, m_far.at[mine], far)
    pass_on = swap(2, m_far.at[mine], m_far.at[mine], pair)

    load_p = pltpu.make_async_copy(row_hbm, pivot_row, in_sem.at[TILES])
    give_p = pltpu.make_async_copy(from_row, from_at, in_sem.at[TILES + 1])
    load_l = pltpu.make_async_copy(l_hbm, l_inverse, in_sem.at[TILES + 2])
    load(0).start()
    load(TILES // 2).start()
    load_p.start()
    for t in range(1, TILES):
        if t != TILES // 2:
            load(t).start()
    load_l.start()

    barrier = pltpu.get_barrier_semaphore()

    @pl.when(other)
    def _():
        signal(r, parent_a)

        @pl.when(parent_b != parent_a)
        def _():
            signal(r, parent_b)

    signal(pair, c)
    signal(far, c)
    def prepare():
        load_p.wait()
        owner, local = local_row(pivot_row[...], nb, row_count)
        from_row[...] = jnp.where(owner == r, local, lax.broadcasted_iota(jnp.int32, (1, nb), 1))
        takes[...] = jnp.where((owner == r) & (pivot_row[...] >= nb), local, rows)
        mat[pl.ds(rows, 8)] = jnp.zeros((8, cols), mat.dtype)
        kind = jnp.where(owner == r, 0.0, jnp.where(owner == pair, 1.0, 2.0))
        down = lax.broadcasted_iota(jnp.int32, (nb, nb), 0)
        along = lax.broadcasted_iota(jnp.int32, (nb, nb), 1)
        spread = jnp.where(down == along, jnp.broadcast_to(kind, (nb, nb)), 0.0)
        code[...] = jnp.sum(spread, axis=1, keepdims=True)
        give_p.start()

    pl.when(other)(prepare)

    expect = 2
    for k in range(SLOTS):
        expect = expect + kids[k][0].astype(jnp.int32)
    pl.semaphore_wait(barrier, expect)

    @pl.when(source)
    def _():
        @pl.loop(0, TILES // 2)
        def _(t):
            for half_t in (t, t + TILES // 2):
                load(half_t).wait()
                at = pl.ds(pl.multiple_of(half_t * tile, tile), tile)
                panel[at] = mat[at, :width].astype(panel.dtype)

            @pl.loop(t * 2 * per, (t + 1) * 2 * per)
            def _(j):
                send(turn(2, j))

        @pl.loop(0, CHUNKS)
        def _(j):
            send(turn(2, j), second=True)

        prepare()

    @pl.when(other)
    def _():
        @pl.loop(0, TILES)
        def _(t):
            load(t).wait()

    give_p.wait()

    @pl.loop(0, nb // 8)
    def _(g):
        out = w_me.at[pl.ds(pl.multiple_of(g * 8, 8), 8)]
        got = [mat[pl.ds(from_at[0, g * 8 + s], 1)] for s in range(8)]
        for s in range(8):
            out[pl.ds(s, 1)] = got[s]

    with_pair.start()

    def sent():
        for k, (valid, kind, col) in enumerate(kids):
            for whole in (True, False):
                part = panel if whole else panel.at[pl.ds(0, rows // 2)]

                @pl.when(valid & ((kind < 2) == whole))
                def _():
                    pltpu.make_async_remote_copy(
                        src_ref=part, dst_ref=part, send_sem=send_sem.at[k], recv_sem=recv_sem.at[0],
                        device_id={"row": r, "col": col}, device_id_type=pl.DeviceIdType.MESH,
                    ).wait_send()

    def step_across():
        with_pair.wait_recv()
        kind = code[mine]
        from_pair = (kind > 0.5) & (kind < jnp.where(core == 1, 9.0, 1.5))
        comb[...] = jnp.where(from_pair, w_pair[mine], w_me[mine])
        across.start()

    def step_pass():
        across.wait_recv()
        pass_on.start()

    def step_wait():
        load_l.wait()
        pass_on.wait_recv()

    def step_u(h):
        at = pl.ds(pl.multiple_of(h * side, side), side)
        kind = code[...]
        picked = jnp.where(kind < 0.5, w_me[:, at], jnp.where(kind < 1.5, w_pair[:, at], m_far[:, at]))
        u = jnp.dot(
            l_inverse[...], picked, precision=lax.Precision.HIGHEST, preferred_element_type=jnp.float32
        )
        u_ref[:, at] = u
        u_half[:, at] = u.astype(u_half.dtype)

    def step_split(h):
        at = pl.ds(pl.multiple_of(h * side, side), side)
        whole = jnp.where(
            r == 0, mat[pl.ds(0, nb), at], jnp.where(r == 1, w_pair[:, at], m_far[:, at])
        )
        whole = jnp.where(source & (h * side < width), w_me[:, at], whole)
        edge = float(jnp.finfo(jnp.bfloat16).max)
        for p in range(PARTS):
            part = jnp.clip(whole, -edge, edge).astype(jnp.bfloat16)
            parts[pl.ds(p * nb, nb), at] = part
            whole = whole - part.astype(jnp.float32)

    def step_swap(t):
        at = pl.ds(pl.multiple_of(t * tile, tile), tile)
        index = lax.broadcasted_iota(jnp.int32, (tile, nb), 0) + t * tile
        onehot = jnp.where(index == takes[...], 1.0, 0.0)
        hit = jnp.max(onehot, axis=1, keepdims=True) > 0.5
        onehot = onehot.astype(jnp.bfloat16)
        rows_in = jnp.dot(
            jnp.concatenate([onehot] * PARTS, axis=1), parts[...], preferred_element_type=jnp.float32
        )
        mat[at] = jnp.where(hit, rows_in, mat[at])

    def update(j, size):
        at = pl.ds(pl.multiple_of(j * size, size), size)
        is_top = (r == 0) & (j < nb // size)

        @pl.when(is_top & other)
        def _():
            mat[at] = u_ref[pl.ds(pl.multiple_of((j % (nb // size)) * size, size), size)]

        @pl.when(is_top & source)
        def _():
            mat[at, width:] = u_ref[pl.ds(pl.multiple_of((j % (nb // size)) * size, size), size), width:]

        @pl.when(jnp.logical_not(is_top) & other)
        def _():
            mat[at] = mat[at] - jnp.dot(panel[at], u_half[...], preferred_element_type=jnp.float32)

        @pl.when(jnp.logical_not(is_top) & source)
        def _():
            mat[at, width:] = mat[at, width:] - jnp.dot(
                panel[at], u_half[:, width:], preferred_element_type=jnp.float32
            )

    came = start_time(core, yh, z, x)
    edge = (z == 1) | (z == 7)
    late = (yh == 0) & (((z == 0) & (x % 2 == 1)) | (edge & (x == 1)))
    compact = (expect == 2) & jnp.logical_not(late)
    spread_out = jnp.logical_not(compact)
    unit = CHUNKS // 32
    free_link = unit * 25
    swap_time = pick(late, free_link, unit * 11)
    at_across = jnp.maximum(0, swap_time - came)
    at_pass = jnp.maximum(0, pick(late, free_link + unit * 23, unit * 33) - came)
    slow = (core == 1) & (yh == 1) & (z != 0) & jnp.logical_not(edge)
    at_pass = pick(slow, at_pass // 2, at_pass)
    lags = (core == 1) & (yh == 1) & edge & (x % 2 == 1)
    fast = (lags & (z == 7)) | ((core == 1) & (yh == 1) & (z == 1) & (x == 0))
    at_pass = pick(lags, pick(x == 1, CHUNKS // 2 - 1, CHUNKS // 8), at_pass)
    after_pass = jnp.maximum(unit * 3, unit * 41 - came)
    after_pass = pick(slow, after_pass * 2 // 3, after_pass)
    after_pass = pick(lags & (x == 1), CHUNKS // 2, jnp.maximum(after_pass, at_pass + 1))
    last = pick(passes, 2 * CHUNKS, CHUNKS)
    settle = passes & other
    at_across = pick(source, 0, pick(settle, jnp.minimum(2 * at_across, last), at_across))
    at_pass = pick(source, 1, pick(settle, last, at_pass))
    at_u = pick(source, 2, pick(settle, last + 1, pick(late, at_pass + unit * 8, after_pass)))
    split_at = 4 * SIDES
    swap_at = split_at + 2 * SIDES
    steps = swap_at + 2 * TILES

    def tile_turn(p):
        upper = TILES // 2
        return pick(order == 0, p, pick(order == 1, (p + upper) % TILES, p // 2 + (p % 2) * upper))

    def early(p):
        done = pick(order == 2, (p // 2 + 1) * 2 * per - 1, (p + 1) * per - 1)
        step = swap_at + 2 * p
        return at_u + pick(fast, step // 2, step) >= jnp.minimum(done, CHUNKS - 1)

    @pl.when(compact)
    def _():
        step_across()
        step_pass()
        step_wait()

        @pl.loop(0, SIDES)
        def _(h):
            step_u(h)
            step_split(h)

        @pl.loop(0, TILES)
        def _(t):
            step_swap(t)

        group = CHUNKS // 4

        @pl.loop(0, 4)
        def _(g):
            @pl.loop(g * group, (g + 1) * group)
            def _(j):
                forward(turn(order, j), 0).wait_recv()

            one = pick(order == 0, 2 * g, pick(order == 1, (2 * g + TILES // 2) % TILES, g))
            update(one, tile)
            update(one + pick(order == 2, TILES // 2, 1), tile)

    @pl.when(spread_out)
    def _():
        @pl.loop(0, jnp.maximum(last, at_u + pick(fast, steps // 2, steps)))
        def _(j):
            pl.when(j == at_across)(step_across)
            pl.when(j == at_pass)(step_pass)

            @pl.when((j < CHUNKS) & other)
            def _():
                i = turn(order, j)
                forward(i, 0).wait_recv()
                send(i)

            @pl.when(settle & (j >= CHUNKS) & (j < last))
            def _():
                send(turn(2, jnp.minimum(j - CHUNKS, CHUNKS - 1)), second=True)

            q = (j - at_u) * pick(fast, 2, 1)
            pl.when(q == 0)(step_wait)

            @pl.when((q >= 0) & (q < split_at) & (q % 4 == 0))
            def _():
                step_u(q // 4)

            @pl.when((q >= split_at) & (q < swap_at) & (q % 2 == 0))
            def _():
                step_split((q - split_at) // 2)

            @pl.when((q >= swap_at) & (q < steps) & (q % 2 == 0))
            def _():
                p = (q - swap_at) // 2
                step_swap(tile_turn(p))

                @pl.when(early(p))
                def _():
                    update(tile_turn(p), tile)

        @pl.loop(0, TILES)
        def _(p):
            @pl.when(jnp.logical_not(early(p)))
            def _():
                update(tile_turn(p), tile)

    with_pair.wait_send()
    across.wait_send()
    pass_on.wait_send()
    sent()


def finish_kernel(mat, u_ref, takes, out, u_out, moved_out, moved, takes_at, sem):
    rows = out.shape[0]
    tile = rows // TILES
    nb = u_ref.shape[0]
    give_t = pltpu.make_async_copy(takes, takes_at, sem.at[TILES])
    give_t.start()
    copies = [
        pltpu.make_async_copy(mat.at[pl.ds(t * tile, tile)], out.at[pl.ds(t * tile, tile)], sem.at[t])
        for t in range(TILES)
    ]
    copies.append(pltpu.make_async_copy(u_ref, u_out, sem.at[TILES + 1]))
    for copy in copies:
        copy.start()
    give_t.wait()

    def gather(g):
        eight = moved.at[pl.ds(pl.multiple_of(g * 8, 8), 8)]
        got = [mat[pl.ds(takes_at[0, g * 8 + s], 1)] for s in range(8)]
        for s in range(8):
            eight[pl.ds(s, 1)] = got[s]

    part = nb // 4
    for p in range(4):
        pl.loop(p * part // 8, (p + 1) * part // 8)(gather)
        at = pl.ds(p * part, part)
        last = pltpu.make_async_copy(moved.at[at], moved_out.at[at], sem.at[TILES + 2 + p])
        last.start()
        copies.append(last)
    for copy in copies:
        copy.wait()


def body(matrix, pivots, l_inverse):
    rows, cols = matrix.shape
    nb = l_inverse.shape[0]
    f32, bf16, i32 = jnp.float32, jnp.bfloat16, jnp.int32
    vmem = pl.BlockSpec(memory_space=pltpu.VMEM)
    hbm = pl.BlockSpec(memory_space=pltpu.HBM)
    shape = jax.ShapeDtypeStruct
    stay = lambda array: pltpu.with_memory_space_constraint(array, pltpu.HBM)
    work, u_rows, takes = pl.pallas_call(
        move_kernel,
        out_shape=(shape((rows + 8, cols), f32), shape((nb, cols), f32), shape((1, nb), i32)),
        in_specs=[hbm] * 3,
        out_specs=[vmem] * 3,
        scratch_shapes=[
            pltpu.VMEM((rows, nb), bf16),
            pltpu.VMEM((nb, cols), f32),
            pltpu.VMEM((nb, cols), f32),
            pltpu.VMEM((nb, cols), f32),
            pltpu.VMEM((nb // 2, cols), f32),
            pltpu.VMEM((nb, 1), f32),
            pltpu.VMEM((nb, nb), f32),
            pltpu.VMEM((1, nb), i32),
            pltpu.VMEM((nb, cols), bf16),
            pltpu.VMEM((PARTS * nb, cols), bf16),
            pltpu.VMEM((1, nb), i32),
            pltpu.SMEM((1, nb), i32),
            pltpu.SemaphoreType.DMA((TILES + 3,)),
            pltpu.SemaphoreType.DMA((CHUNKS,)),
            pltpu.SemaphoreType.DMA((SLOTS,)),
            pltpu.SemaphoreType.DMA((3,)),
            pltpu.SemaphoreType.DMA((3,)),
        ],
        compiler_params=pltpu.CompilerParams(
            collective_id=0, has_side_effects=True, vmem_limit_bytes=MOVE_VMEM
        ),
        name="move",
    )(stay(pivots.reshape(1, nb)), stay(matrix), stay(l_inverse))
    return pl.pallas_call(
        finish_kernel,
        out_shape=(shape((rows, cols), f32), shape((nb, cols), f32), shape((nb, cols), f32)),
        in_specs=[vmem] * 3,
        out_specs=[hbm] * 3,
        scratch_shapes=[
            pltpu.VMEM((nb, cols), f32),
            pltpu.SMEM((1, nb), i32),
            pltpu.SemaphoreType.DMA((TILES + 6,)),
        ],
        compiler_params=pltpu.CompilerParams(vmem_limit_bytes=FINISH_VMEM),
        name="finish",
    )(work, u_rows, takes)


def solution(mesh):
    return jax.shard_map(
        body,
        mesh=mesh,
        in_specs=(P("row", "col"), P(), P()),
        out_specs=(P("row", "col"), P(None, "col"), P("row", "col")),
        check_vma=False,
    )
```

```python
import jax
import jax.numpy as jnp
from jax import lax
from jax.experimental import pallas as pl
from jax.experimental.pallas import tpu as pltpu
from jax.sharding import PartitionSpec as P

CHUNKS = 32
TILES = 8
SLOTS = 4
PARTS = 2
SIDES = 2
MOVE_VMEM = 24 * 2**20
FINISH_VMEM = 8 * 2**20
NZ = 8
NX = 4


def pick(cond, a, b):
    return jnp.where(cond, a, b)


def column(yh, z, x):
    return (yh * NZ + z) * NX + x


def tree(core, yh, z, x):
    first = core == 0
    second = jnp.logical_not(first)
    root = (yh == 0) & (x == 0)
    off = jnp.logical_not(root)
    flat = z == 0
    up = (z >= 1) & (z <= 3)
    down = (z == 6) | (z == 7)
    odd = (x % 2) == 1
    inplane = pick(first, flat, jnp.logical_not(flat))
    folded = inplane & (first | (z == 1) | (z == 7))
    plain = inplane & jnp.logical_not(folded)
    twin = first & ((x == 2) | ((yh == 1) & (x == 0)))
    only = pick(x == 1, 2, 3)
    along = pick(first, off, root)
    v0 = along & (flat | up | down | (twin & (z == 5)))
    k0 = column(yh, pick(flat, 1, pick(up, z + 1, z - 1)), x)
    c0 = pick(twin & (z == 3), 2, pick(twin & (z == 5), 3, 0))
    drop = second & (z == 1) & off
    over = plain & root
    v2 = (along & flat) | drop | over
    k2 = pick(over, column(1, z, 0), column(yh, pick(drop, 0, 7), x))
    c2 = pick(twin, 1, 0)
    back = first & jnp.logical_not(flat) & (yh == 0) & (x == 1)
    v1 = (folded & jnp.logical_not((yh == 0) & (x == 2))) | back | (plain & (x <= 1))
    x1 = pick(odd, 2, pick(x == 2, 1, pick(yh == 0, 1, 3)))
    k1 = column(yh, z, pick(back, 0, pick(plain, x + 1, x1)))
    c1 = pick(back | root | plain, 0, pick(odd, only, pick(x == 2, 3, 2)))
    v3 = (folded & (root | odd)) | (plain & (x == 0))
    k3 = pick(root | plain, column(yh, z, 3), pick(yh == 0, column(1, z, x), column(1, z, 0)))
    c3 = pick(root | plain, pick(first, 1, 0), only)
    kids = ((v0, c0, k0), (v1, c1, k1), (v2, c2, k2), (v3, c3, k3))
    near = pick(z <= 4, z - 1, (z + 1) % NZ)
    in_a = pick(
        yh == 0,
        pick(odd, column(0, z, 0), column(0, z, 1)),
        pick(x == 1, column(0, z, 1), pick(x == 3, column(1, z, 0), column(1, z, 1))),
    )
    in_b = pick(
        yh == 0,
        pick(odd, column(0, z, 0), column(0, z, 3)),
        pick(x == 1, column(1, z, 2), pick(x == 3, column(0, z, 3), column(1, z, 3))),
    )
    chain_a = pick(root, column(0, z, 1), column(yh, near, x))
    chain_b = pick(twin & (z == 4), column(yh, 5, x), chain_a)
    stem = pick(root, column(0, near, 0), column(yh, 1, x))
    other_plane = pick(first, jnp.logical_not(flat), flat | root)
    in_plain = pick(x == 2, column(yh, z, 1), pick(x == 0, column(0, z, 0), column(yh, z, 0)))
    parent_a = pick(other_plane, pick(first, chain_a, stem), pick(plain, in_plain, in_a))
    parent_b = pick(other_plane, pick(first, chain_b, stem), pick(plain, in_plain, in_b))
    beyond = z >= 5
    turn = pick(flat | (z == 4), pick(flat & (x == 0), 3, 2), pick(beyond, 1, 0))
    side = (yh == 1) & (x == 3) & folded
    order = pick(first, pick(twin, turn, pick(x == 3, 1, 0)), pick(side, 2, 0))
    passes = (flat & root) | (twin & flat)
    return kids, parent_a, parent_b, order, passes


def start_time(core, yh, z, x):
    first = core == 0
    dz = jnp.minimum(z, NZ - z)
    flat = z == 0
    root = (yh == 0) & (x == 0)
    straight = (z != 0) & (z != 1) & (z != 7) & (x == 0)
    none = (root & (jnp.logical_not(first) | flat)) | (jnp.logical_not(first) & straight)
    dx = pick(x % 2 == 1, 1, pick(none, 0, 2))
    dz = dz + pick(flat & jnp.logical_not(first) & jnp.logical_not(root), 2, 0)
    return (pick(first, 7, 5) * dx + pick(first, 6, 4) * dz + pick(first, 8, 6) * yh) * (CHUNKS // 32)


def place():
    r = lax.axis_index("row")
    c = lax.axis_index("col")
    return r, c, r % 2, r // 2, c // (NX * NZ), (c // NX) % NZ, c % NX


def local_row(p, nb, row_count):
    shift = nb.bit_length() - 1
    deal = row_count.bit_length() - 1
    block = jnp.right_shift(p, shift)
    owner = block & (row_count - 1)
    local = jnp.left_shift(jnp.right_shift(block, deal), shift) + (p & (nb - 1))
    return owner, local


def move_kernel(
    row_hbm, mat_hbm, l_hbm, mat, u_ref, takes,
    panel, w_me, w_pair, m_far, comb, code, l_inverse, pivot_row, u_half, parts, from_row, from_at,
    in_sem, recv_sem, send_sem, x_send, x_recv,
):
    r, c, core, yl, yh, z, x = place()
    pair = yl * 2 + 1 - core
    far = (1 - yl) * 2 + core
    source = c == 0
    other = jnp.logical_not(source)
    kids, parent_a, parent_b, order, passes = tree(core, yh, z, x)
    rows, cols = mat_hbm.shape
    tile = rows // TILES
    chunk = rows // CHUNKS
    per = CHUNKS // TILES
    nb, width = l_hbm.shape
    half = nb // 2
    side = cols // SIDES
    row_count = lax.axis_size("row")

    def load(t):
        at = pl.ds(pl.multiple_of(t * tile, tile), tile)
        return pltpu.make_async_copy(mat_hbm.at[at], mat.at[at], in_sem.at[t])

    split_point = CHUNKS // 2

    def turn(mode, j):
        late_first = pick(j < split_point, j + split_point, j - split_point)
        even = j // 2 + (j % 2) * split_point
        lead = CHUNKS // 8
        m = jnp.maximum(j - lead, 0)
        led = pick(m % 2 == 0, m // 2 + split_point, m // 2 + lead)
        led = pick(j < lead, j, pick(j < CHUNKS - lead, led, j))
        return pick(mode == 0, j, pick(mode == 1, late_first, pick(mode == 2, even, led)))

    def forward(i, k):
        at = pl.ds(pl.multiple_of(i * chunk, chunk), chunk)
        return pltpu.make_async_remote_copy(
            src_ref=panel.at[at],
            dst_ref=panel.at[at],
            send_sem=send_sem.at[k],
            recv_sem=recv_sem.at[i],
            device_id={"row": r, "col": kids[k][2]},
            device_id_type=pl.DeviceIdType.MESH,
        )

    def send(i, second=False):
        head = i < split_point
        for k, (valid, kind, _) in enumerate(kids):
            match = jnp.logical_xor((kind % 2) == 1, head)
            both = kind < 2
            if second:
                go = both & jnp.logical_not(match)
            else:
                go = match | (both & jnp.logical_not(passes))

            @pl.when(valid & go)
            def _():
                forward(i, k).start()

    def swap(step, src, dst, to):
        return pltpu.make_async_remote_copy(
            src_ref=src, dst_ref=dst, send_sem=x_send.at[step], recv_sem=x_recv.at[step],
            device_id={"row": to, "col": c}, device_id_type=pl.DeviceIdType.MESH,
        )

    def signal(row, col):
        pl.semaphore_signal(
            barrier, inc=1, device_id={"row": row, "col": col}, device_id_type=pl.DeviceIdType.MESH
        )

    mine = pl.ds(pl.multiple_of(core * half, half), half)
    with_pair = swap(0, w_me, w_pair, pair)
    across = swap(1, comb, m_far.at[mine], far)
    pass_on = swap(2, m_far.at[mine], m_far.at[mine], pair)

    load_p = pltpu.make_async_copy(row_hbm, pivot_row, in_sem.at[TILES])
    give_p = pltpu.make_async_copy(from_row, from_at, in_sem.at[TILES + 1])
    load_l = pltpu.make_async_copy(l_hbm, l_inverse, in_sem.at[TILES + 2])
    load(0).start()
    load(TILES // 2).start()
    load_p.start()

    def load_rest():
        for t in range(1, TILES):
            if t != TILES // 2:
                load(t).start()
        load_l.start()

    pl.when(other)(load_rest)

    barrier = pltpu.get_barrier_semaphore()

    @pl.when(other)
    def _():
        signal(r, parent_a)

        @pl.when(parent_b != parent_a)
        def _():
            signal(r, parent_b)

    signal(pair, c)
    signal(far, c)
    def prepare():
        load_p.wait()
        owner, local = local_row(pivot_row[...], nb, row_count)
        from_row[...] = jnp.where(owner == r, local, lax.broadcasted_iota(jnp.int32, (1, nb), 1))
        takes[...] = jnp.where((owner == r) & (pivot_row[...] >= nb), local, rows)
        mat[pl.ds(rows, 8)] = jnp.zeros((8, cols), mat.dtype)
        kind = jnp.where(owner == r, 0.0, jnp.where(owner == pair, 1.0, 2.0))
        down = lax.broadcasted_iota(jnp.int32, (nb, nb), 0)
        along = lax.broadcasted_iota(jnp.int32, (nb, nb), 1)
        spread = jnp.where(down == along, jnp.broadcast_to(kind, (nb, nb)), 0.0)
        code[...] = jnp.sum(spread, axis=1, keepdims=True)
        give_p.start()

    pl.when(other)(prepare)

    expect = 2
    for k in range(SLOTS):
        expect = expect + kids[k][0].astype(jnp.int32)
    pl.semaphore_wait(barrier, expect)

    @pl.when(source)
    def _():
        @pl.loop(0, TILES // 2)
        def _(t):
            load(t).wait()
            load(t + TILES // 2).wait()
            pl.when(t == 0)(load_rest)

            @pl.loop(t * per, (t + 1) * per)
            def _(i):
                for piece in (i, i + split_point):
                    at = pl.ds(pl.multiple_of(piece * chunk, chunk), chunk)
                    panel[at] = mat[at, :width].astype(panel.dtype)

                @pl.when(i > 0)
                def _():
                    send(jnp.maximum(i - 1, 0))
                    send(jnp.maximum(i - 1, 0) + split_point)

        send(split_point - 1)
        send(CHUNKS - 1)

        @pl.loop(0, CHUNKS)
        def _(j):
            send(turn(2, j), second=True)

        prepare()

    @pl.when(other)
    def _():
        @pl.loop(0, TILES)
        def _(t):
            load(t).wait()

    give_p.wait()

    @pl.loop(0, nb // 8)
    def _(g):
        out = w_me.at[pl.ds(pl.multiple_of(g * 8, 8), 8)]
        got = [mat[pl.ds(from_at[0, g * 8 + s], 1)] for s in range(8)]
        for s in range(8):
            out[pl.ds(s, 1)] = got[s]

    with_pair.start()

    def sent():
        for k, (valid, kind, col) in enumerate(kids):
            for whole in (True, False):
                part = panel if whole else panel.at[pl.ds(0, rows // 2)]

                @pl.when(valid & ((kind < 2) == whole))
                def _():
                    pltpu.make_async_remote_copy(
                        src_ref=part, dst_ref=part, send_sem=send_sem.at[k], recv_sem=recv_sem.at[0],
                        device_id={"row": r, "col": col}, device_id_type=pl.DeviceIdType.MESH,
                    ).wait_send()

    def step_across():
        with_pair.wait_recv()
        kind = code[mine]
        from_pair = (kind > 0.5) & (kind < jnp.where(core == 1, 9.0, 1.5))
        comb[...] = jnp.where(from_pair, w_pair[mine], w_me[mine])
        across.start()

    def step_pass():
        across.wait_recv()
        pass_on.start()

    def step_wait():
        load_l.wait()
        pass_on.wait_recv()

    def step_u(h):
        at = pl.ds(pl.multiple_of(h * side, side), side)
        kind = code[...]
        picked = jnp.where(kind < 0.5, w_me[:, at], jnp.where(kind < 1.5, w_pair[:, at], m_far[:, at]))
        u = jnp.dot(
            l_inverse[...], picked, precision=lax.Precision.HIGHEST, preferred_element_type=jnp.float32
        )
        u_ref[:, at] = u
        u_half[:, at] = u.astype(u_half.dtype)

    def step_split(h):
        at = pl.ds(pl.multiple_of(h * side, side), side)
        whole = jnp.where(
            r == 0, mat[pl.ds(0, nb), at], jnp.where(r == 1, w_pair[:, at], m_far[:, at])
        )
        whole = jnp.where(source & (h * side < width), w_me[:, at], whole)
        edge = float(jnp.finfo(jnp.bfloat16).max)
        for p in range(PARTS):
            part = jnp.clip(whole, -edge, edge).astype(jnp.bfloat16)
            parts[pl.ds(p * nb, nb), at] = part
            whole = whole - part.astype(jnp.float32)

    def step_swap(t):
        at = pl.ds(pl.multiple_of(t * tile, tile), tile)
        index = lax.broadcasted_iota(jnp.int32, (tile, nb), 0) + t * tile
        onehot = jnp.where(index == takes[...], 1.0, 0.0)
        hit = jnp.max(onehot, axis=1, keepdims=True) > 0.5
        onehot = onehot.astype(jnp.bfloat16)
        rows_in = jnp.dot(
            jnp.concatenate([onehot] * PARTS, axis=1), parts[...], preferred_element_type=jnp.float32
        )
        mat[at] = jnp.where(hit, rows_in, mat[at])

    def update(j, size):
        at = pl.ds(pl.multiple_of(j * size, size), size)
        is_top = (r == 0) & (j < nb // size)

        @pl.when(is_top & other)
        def _():
            mat[at] = u_ref[pl.ds(pl.multiple_of((j % (nb // size)) * size, size), size)]

        @pl.when(is_top & source)
        def _():
            mat[at, width:] = u_ref[pl.ds(pl.multiple_of((j % (nb // size)) * size, size), size), width:]

        @pl.when(jnp.logical_not(is_top) & other)
        def _():
            mat[at] = mat[at] - jnp.dot(panel[at], u_half[...], preferred_element_type=jnp.float32)

        @pl.when(jnp.logical_not(is_top) & source)
        def _():
            mat[at, width:] = mat[at, width:] - jnp.dot(
                panel[at], u_half[:, width:], preferred_element_type=jnp.float32
            )

    came = start_time(core, yh, z, x)
    edge = (z == 1) | (z == 7)
    late = (yh == 0) & (((z == 0) & (x % 2 == 1)) | (edge & (x == 1)))
    compact = (expect == 2) & jnp.logical_not(late)
    spread_out = jnp.logical_not(compact)
    unit = CHUNKS // 32
    free_link = unit * 25
    swap_time = pick(late, free_link, unit * 11)
    at_across = jnp.maximum(0, swap_time - came)
    at_pass = jnp.maximum(0, pick(late, free_link + unit * 23, unit * 33) - came)
    slow = (core == 1) & (yh == 1) & (z != 0) & jnp.logical_not(edge)
    at_pass = pick(slow, at_pass // 2, at_pass)
    lags = (core == 1) & (yh == 1) & edge & (x % 2 == 1)
    fast = (lags & (z == 7)) | ((core == 1) & (yh == 1) & (z == 1) & (x == 0))
    at_pass = pick(lags, pick(x == 1, CHUNKS // 2 - 1, CHUNKS // 8), at_pass)
    after_pass = jnp.maximum(unit * 3, unit * 41 - came)
    after_pass = pick(slow, after_pass * 2 // 3, after_pass)
    after_pass = pick(lags & (x == 1), CHUNKS // 2, jnp.maximum(after_pass, at_pass + 1))
    last = pick(passes, 2 * CHUNKS, CHUNKS)
    settle = passes & other
    at_across = pick(source, 0, pick(settle, jnp.minimum(2 * at_across, last), at_across))
    at_pass = pick(source, 1, pick(settle, last, at_pass))
    at_u = pick(source, 2, pick(settle, last + 1, pick(late, at_pass + unit * 8, after_pass)))
    split_at = 4 * SIDES
    swap_at = split_at + 2 * SIDES
    steps = swap_at + 2 * TILES

    def tile_turn(p):
        upper = TILES // 2
        return pick(order == 0, p, pick(order == 1, (p + upper) % TILES, p // 2 + (p % 2) * upper))

    def early(p):
        done = pick(order == 2, (p // 2 + 1) * 2 * per - 1, (p + 1) * per - 1)
        step = swap_at + 2 * p
        return at_u + pick(fast, step // 2, step) >= jnp.minimum(done, CHUNKS - 1)

    @pl.when(compact)
    def _():
        step_across()
        step_pass()
        step_wait()

        @pl.loop(0, SIDES)
        def _(h):
            step_u(h)
            step_split(h)

        @pl.loop(0, TILES)
        def _(t):
            step_swap(t)

        group = CHUNKS // 4

        @pl.loop(0, 4)
        def _(g):
            @pl.loop(g * group, (g + 1) * group)
            def _(j):
                forward(turn(order, j), 0).wait_recv()

            one = pick(order == 0, 2 * g, pick(order == 1, (2 * g + TILES // 2) % TILES, g))
            update(one, tile)
            update(one + pick(order == 2, TILES // 2, 1), tile)

    @pl.when(spread_out)
    def _():
        @pl.loop(0, jnp.maximum(last, at_u + pick(fast, steps // 2, steps)))
        def _(j):
            pl.when(j == at_across)(step_across)
            pl.when(j == at_pass)(step_pass)

            @pl.when((j < CHUNKS) & other)
            def _():
                i = turn(order, j)
                forward(i, 0).wait_recv()
                send(i)

            @pl.when(settle & (j >= CHUNKS) & (j < last))
            def _():
                send(turn(2, jnp.minimum(j - CHUNKS, CHUNKS - 1)), second=True)

            q = (j - at_u) * pick(fast, 2, 1)
            pl.when(q == 0)(step_wait)

            @pl.when((q >= 0) & (q < split_at) & (q % 4 == 0))
            def _():
                step_u(q // 4)

            @pl.when((q >= split_at) & (q < swap_at) & (q % 2 == 0))
            def _():
                step_split((q - split_at) // 2)

            @pl.when((q >= swap_at) & (q < steps) & (q % 2 == 0))
            def _():
                p = (q - swap_at) // 2
                step_swap(tile_turn(p))

                @pl.when(early(p))
                def _():
                    update(tile_turn(p), tile)

        @pl.loop(0, TILES)
        def _(p):
            @pl.when(jnp.logical_not(early(p)))
            def _():
                update(tile_turn(p), tile)

    with_pair.wait_send()
    across.wait_send()
    pass_on.wait_send()
    sent()


def finish_kernel(mat, u_ref, takes, out, u_out, moved_out, moved, takes_at, sem):
    rows = out.shape[0]
    tile = rows // TILES
    nb = u_ref.shape[0]
    give_t = pltpu.make_async_copy(takes, takes_at, sem.at[TILES])
    give_t.start()
    copies = [
        pltpu.make_async_copy(mat.at[pl.ds(t * tile, tile)], out.at[pl.ds(t * tile, tile)], sem.at[t])
        for t in range(TILES)
    ]
    copies.append(pltpu.make_async_copy(u_ref, u_out, sem.at[TILES + 1]))
    for copy in copies:
        copy.start()
    give_t.wait()

    def gather(g):
        eight = moved.at[pl.ds(pl.multiple_of(g * 8, 8), 8)]
        got = [mat[pl.ds(takes_at[0, g * 8 + s], 1)] for s in range(8)]
        for s in range(8):
            eight[pl.ds(s, 1)] = got[s]

    part = nb // 4
    for p in range(4):
        pl.loop(p * part // 8, (p + 1) * part // 8)(gather)
        at = pl.ds(p * part, part)
        last = pltpu.make_async_copy(moved.at[at], moved_out.at[at], sem.at[TILES + 2 + p])
        last.start()
        copies.append(last)
    for copy in copies:
        copy.wait()


def body(matrix, pivots, l_inverse):
    rows, cols = matrix.shape
    nb = l_inverse.shape[0]
    f32, bf16, i32 = jnp.float32, jnp.bfloat16, jnp.int32
    vmem = pl.BlockSpec(memory_space=pltpu.VMEM)
    hbm = pl.BlockSpec(memory_space=pltpu.HBM)
    shape = jax.ShapeDtypeStruct
    stay = lambda array: pltpu.with_memory_space_constraint(array, pltpu.HBM)
    work, u_rows, takes = pl.pallas_call(
        move_kernel,
        out_shape=(shape((rows + 8, cols), f32), shape((nb, cols), f32), shape((1, nb), i32)),
        in_specs=[hbm] * 3,
        out_specs=[vmem] * 3,
        scratch_shapes=[
            pltpu.VMEM((rows, nb), bf16),
            pltpu.VMEM((nb, cols), f32),
            pltpu.VMEM((nb, cols), f32),
            pltpu.VMEM((nb, cols), f32),
            pltpu.VMEM((nb // 2, cols), f32),
            pltpu.VMEM((nb, 1), f32),
            pltpu.VMEM((nb, nb), f32),
            pltpu.VMEM((1, nb), i32),
            pltpu.VMEM((nb, cols), bf16),
            pltpu.VMEM((PARTS * nb, cols), bf16),
            pltpu.VMEM((1, nb), i32),
            pltpu.SMEM((1, nb), i32),
            pltpu.SemaphoreType.DMA((TILES + 3,)),
            pltpu.SemaphoreType.DMA((CHUNKS,)),
            pltpu.SemaphoreType.DMA((SLOTS,)),
            pltpu.SemaphoreType.DMA((3,)),
            pltpu.SemaphoreType.DMA((3,)),
        ],
        compiler_params=pltpu.CompilerParams(
            collective_id=0, has_side_effects=True, vmem_limit_bytes=MOVE_VMEM
        ),
        name="move",
    )(stay(pivots.reshape(1, nb)), stay(matrix), stay(l_inverse))
    return pl.pallas_call(
        finish_kernel,
        out_shape=(shape((rows, cols), f32), shape((nb, cols), f32), shape((nb, cols), f32)),
        in_specs=[vmem] * 3,
        out_specs=[hbm] * 3,
        scratch_shapes=[
            pltpu.VMEM((nb, cols), f32),
            pltpu.SMEM((1, nb), i32),
            pltpu.SemaphoreType.DMA((TILES + 6,)),
        ],
        compiler_params=pltpu.CompilerParams(vmem_limit_bytes=FINISH_VMEM),
        name="finish",
    )(work, u_rows, takes)


def solution(mesh):
    return jax.shard_map(
        body,
        mesh=mesh,
        in_specs=(P("row", "col"), P(), P()),
        out_specs=(P("row", "col"), P(None, "col"), P("row", "col")),
        check_vma=False,
    )
```
